512 devices in a mesh: gz: 64 (over z, x), gy: 8 (over y, core).
Axes of the slice: x: 4, y: 4, z: 16, core: 2. Of those that a mesh axis runs over, the one named last changes fastest.
Arguments:
- fields: float32 [4, 256, 128, 512], P(None, 'gz', 'gy'), may hold values from -4 to 4
- velocity: float32 [2, 256, 128, 512], P(None, 'gz', 'gy'), may hold values from -3 to 3
- face_rate: float32 [256, 128, 512], P('gz', 'gy'), may hold values from 1 to 4
- xy_rate: float32 [4], replicated, may hold values from 0.05 to 0.2
- z_scale: float32 [4], replicated, may hold values from 128 to 512
Outputs:
- advanced: float32 [4, 256, 128, 512], P(None, 'gz', 'gy')
The draws below stay inside these ranges and needn't reach their ends.
All inputs are finite; a program needn't handle non-finite values.
Results may differ from the reference program's by a relative error of at most 0.0003.
Values sent between devices are 32-bit elements; how exact they have to be, the bound alone decides.
No kernel may reach another device: no remote copies, remote signals or barrier semaphores. Data moves between devices by JAX's collectives and lax.ppermute only.
A program may use at most 64 MiB of HBM per device.

```python
import math
import jax
import jax.numpy as jnp
from jax import lax

FIELDS = 4
STEPS = 2
NX = 512
NY = 128
NZ = 256


def draw_fields(key, part):
    shape = (FIELDS, NZ, NY, NX)
    column_shape = (FIELDS, 1, NY, NX)
    height = (jnp.arange(NZ, dtype=jnp.float32) + 0.5) / NZ
    rough = 0.8 * jax.random.normal(jax.random.fold_in(key, 5), shape, jnp.float32)
    contrast = 1.3 * jax.random.normal(jax.random.fold_in(key, 7), column_shape, jnp.float32)
    smooth = 0.5 + 1.5 * height
    values = rough + contrast + smooth[None, :, None, None]
    return jnp.clip(values, -4.0, 4.0)


def level_of(key, shape, shards, smallest, top_value):
    def one(dim, shards_of):
        steps = jax.random.uniform(jax.random.fold_in(jax.random.fold_in(key, 6), dim), (shards_of,), jnp.float32, smallest / len(shards), top_value / len(shards))
        return jnp.repeat(jnp.exp(steps), shape[dim] // shards_of).reshape((-1,) + (1,) * (len(shape) - dim - 1))

    gain = one(*shards[0])
    for cut in shards[1:]:
        gain = gain * one(*cut)
    return gain


def normal_values(stream_key, extent, deviation, most, shards=(), kind=jnp.bfloat16):
    factor_of = level_of(stream_key, extent, shards, -0.22, 0.18) if shards else 1.0
    values = jax.random.normal(stream_key, extent, jnp.float32) * deviation * factor_of
    return jnp.minimum(jnp.maximum(values, -most), most).astype(kind)


def setup_inputs(seed: int = 0) -> dict:
    seeds = jax.random.split(jax.random.key(seed), 6)
    fields = draw_fields(jax.random.fold_in(seeds[5], 71), 0)
    velocity = normal_values(seeds[1], (2, NZ, NY, NX), 0.5, 3.0, ((1, 64), (2, 8)), jnp.float32)
    face_rate = jnp.clip(jnp.exp(math.log(4.0) - 1.3862944 * jax.random.uniform(seeds[2], (NZ, NY, NX), jnp.float32) ** level_of(seeds[2], (NZ, NY, NX), ((0, 64), (1, 8)), -0.2, 0.2)), 1.0, 4.0)
    xy_rate = jnp.clip(jax.random.uniform(seeds[3], (FIELDS,), jnp.float32, 0.05, 0.2), 0.05, 0.2)
    z_scale = jnp.clip(jnp.exp(jax.random.uniform(seeds[4], (FIELDS,), jnp.float32, math.log(128.0), math.log(512.0))), 128.0, 512.0)
    return dict(fields=fields, velocity=velocity, face_rate=face_rate, xy_rate=xy_rate, z_scale=z_scale)


def tendency(present, along_x, along_y, spread):
    eastern = jnp.roll(present, -1, 2)
    western = jnp.roll(present, 1, 2)
    north = jnp.roll(present, -1, 1)
    south = jnp.roll(present, 1, 1)
    return spread * (eastern + western + north + south - 4.0 * present) - 0.5 * (along_x * (eastern - western) + along_y * (north - south))


def forward_sweep(carried, inputs):
    factor_prev, value_prev = carried
    source, face_below, face_above = inputs
    pivot = 1.0 + face_below + face_above + face_below * factor_prev
    factor_new = -face_above / pivot
    value_new = (source + face_below * value_prev) / pivot
    return (factor_new, value_new), (factor_new, value_new)


def backward_sweep(solved_above, inputs):
    factor_now, value_now = inputs
    solved = value_now - factor_now * solved_above
    return solved, solved


def advance_field(field_items, velocity, face_rate):
    present, spread, vertical_scale = field_items
    along_x = velocity[0]
    along_y = velocity[1]
    sectioned = present + tendency(present, along_x, along_y, spread)
    explicit = 0.5 * present + 0.5 * (sectioned + tendency(sectioned, along_x, along_y, spread))
    face_below = vertical_scale * face_rate
    face_above = jnp.concatenate([face_below[1:], jnp.zeros_like(face_below[:1])], 0)
    start = (jnp.zeros_like(present[0]), jnp.zeros_like(present[0]))
    ignored, sweeps = lax.scan(forward_sweep, start, (explicit, face_below, face_above))
    ignored, vertical = lax.scan(backward_sweep, jnp.zeros_like(present[0]), sweeps, reverse=True)
    return vertical


def reference(fields, velocity, face_rate, xy_rate, z_scale):
    def advance(field_items):
        return advance_field(field_items, velocity, face_rate)

    present = fields
    for step_index in range(STEPS):
        present = lax.map(advance, (present, xy_rate, z_scale))
    return present
```

```python
import functools

import jax
import jax.numpy as jnp
from jax import lax
from jax.experimental import pallas as pl
from jax.experimental.pallas import tpu as pltpu
from jax.sharding import PartitionSpec as P

FIELDS = 4
LEVELS = 4
ROWS = 16
WIDTH = 512
LANES = 128
BLOCKS = 64
HALF = BLOCKS // 2
COLUMNS = WIDTH // LANES


def tendency(middle, half_x, half_y, spread):
    rows = middle.shape[0]
    eastern = pltpu.roll(middle, WIDTH - 1, 1)
    western = pltpu.roll(middle, 1, 1)
    north = pltpu.roll(middle, rows - 1, 0)
    south = pltpu.roll(middle, 1, 0)
    return spread * (eastern + western + north + south - 4.0 * middle) - (
        half_x * (eastern - western) + half_y * (north - south)
    )


def inner_pivots(rates):
    hold = 1.0 + rates[0]
    inverse = []
    for level in range(LEVELS - 1):
        once = 1.0 / (hold + rates[level + 1])
        inverse.append(once)
        hold = 1.0 + rates[level + 1] * hold * once
    return inverse


def solve_inner(source, rates, inverse):
    first = source[0]
    second = source[1] + rates[1] * inverse[0] * first
    third = (source[2] + rates[2] * inverse[1] * second) * inverse[2]
    second = (second + rates[2] * third) * inverse[1]
    first = (first + rates[1] * second) * inverse[0]
    return first, second, third


def explicit_kernel(chunk, xy_ref, zs_ref, present_ref, south_ref, north_ref, vel_ref, vel_south_ref,
                    vel_north_ref, face_ref, explicit_ref, send_ref, tail_ref, vel_tail_ref):
    tail_ref[:, 0:2, :] = north_ref[...]
    tail_ref[:, 6:8, :] = south_ref[...]
    vel_tail_ref[:, 0:1, :] = vel_north_ref[...]
    vel_tail_ref[:, 7:8, :] = vel_south_ref[...]
    for level in range(LEVELS):
        half_x = 0.5 * jnp.concatenate([vel_ref[level], vel_tail_ref[level]], 0)
        half_y = 0.5 * jnp.concatenate([vel_ref[LEVELS + level], vel_tail_ref[LEVELS + level]], 0)
        for field in range(FIELDS):
            item = field * LEVELS + level
            spread = xy_ref[field]
            middle = jnp.concatenate([present_ref[item], tail_ref[item]], 0)
            sectioned = middle + tendency(middle, half_x, half_y, spread)
            again = sectioned + tendency(sectioned, half_x, half_y, spread)
            explicit_ref[item] = (0.5 * middle + 0.5 * again)[:ROWS]
    for tile in range(ROWS // 8):
        rows = slice(tile * 8, tile * 8 + 8)
        for field in range(FIELDS):
            scale = zs_ref[field]
            rates = [scale * face_ref[level, rows, :] for level in range(LEVELS)]
            source = [explicit_ref[field * LEVELS + level, rows, :] for level in range(LEVELS)]
            first, _, third = solve_inner(source, rates, inner_pivots(rates))
            own = source[3] + rates[3] * third
            under = rates[0] * first
            for column in range(COLUMNS):
                lanes = slice(column * LANES, column * LANES + LANES)
                start = (tile * 8 * COLUMNS + column) * chunk
                send_ref[pl.ds(start + field, 8, stride=COLUMNS * chunk), :] = own[:, lanes]
                send_ref[pl.ds(start + FIELDS + field, 8, stride=COLUMNS * chunk), :] = under[:, lanes]
        if chunk > 8:
            for level in range(LEVELS):
                for column in range(COLUMNS):
                    lanes = slice(column * LANES, column * LANES + LANES)
                    start = (tile * 8 * COLUMNS + column) * chunk
                    send_ref[pl.ds(start + 8 + level, 8, stride=COLUMNS * chunk), :] = face_ref[level, rows, lanes]


def swap(value):
    return pltpu.roll(value, 4, 0)


def lower_half():
    return lax.broadcasted_iota(jnp.int32, (8, LANES), 0) < 4


def factor_kernel(got_ref, zs_ref, weight_ref, gain_ref):
    low = lower_half()
    scale = zs_ref[...]
    couple, own, under = [], [], []
    for step in range(HALF):
        rates = [
            scale
            * jnp.where(
                low,
                jnp.broadcast_to(got_ref[step, 8 + level : 9 + level, :], (8, LANES)),
                jnp.broadcast_to(got_ref[BLOCKS - 1 - step, 8 + level : 9 + level, :], (8, LANES)),
            )
            for level in range(LEVELS)
        ]
        inverse = inner_pivots(rates)
        one = jnp.ones((8, LANES), jnp.float32)
        first, _, third = solve_inner([one, one, one], rates, inverse)
        own.append(1.0 + rates[3] * third)
        under.append(rates[0] * first)
        couple.append(rates[0] * inverse[0] * rates[1] * inverse[1] * rates[2] * inverse[2] * rates[3])
    zero = jnp.zeros((8, LANES), jnp.float32)
    hold = None
    for step in range(HALF):
        last = step == HALF - 1
        below = swap(under[step]) if last else under[step + 1]
        above = zero if step == 0 else under[step - 1]
        mass = own[step] + jnp.where(low, below, above)
        hold = mass + (jnp.where(low, couple[0], zero) if step == 0 else hold * gain)
        inward = jnp.where(low, swap(couple[step]) if last else couple[step + 1], couple[step])
        if last:
            other = swap(hold)
            inverse = 1.0 / (hold * other + inward * (hold + other))
            weight_ref[step] = (other + inward) * inverse
            gain_ref[step] = inward * inverse
        else:
            weight = 1.0 / (hold + inward)
            gain = inward * weight
            weight_ref[step] = weight
            gain_ref[step] = gain


def separator_kernel(got_ref, weight_ref, gain_ref, back_ref):
    low = lower_half()

    def side(block):
        value = got_ref[block, 0:8, :]
        if block + 1 < BLOCKS:
            return value + swap(got_ref[block + 1, 0:8, :])
        return jnp.where(low, value, 0.0)

    value = None
    kept = []
    for step in range(HALF):
        source = jnp.where(low, side(step), swap(side(BLOCKS - 1 - step)))
        value = source if step == 0 else source + gain_ref[step - 1] * value
        kept.append(value)
    value = weight_ref[HALF - 1] * value + gain_ref[HALF - 1] * swap(value)
    back_ref[HALF] = value
    for step in reversed(range(HALF)):
        inner = value
        turned = swap(inner)
        if step > 0:
            value = weight_ref[step - 1] * kept[step - 1] + gain_ref[step - 1] * inner
            back_ref[step] = jnp.where(low, value, turned)
            back_ref[BLOCKS - step] = jnp.where(low, turned, value)
        else:
            back_ref[0] = jnp.where(low, 0.0, turned)


def finish_kernel(edges, zs_ref, explicit_ref, face_ref, back_ref, present_ref, *edge_refs):
    for tile in range(ROWS // 8):
        rows = slice(tile * 8, tile * 8 + 8)
        for field in range(FIELDS):
            scale = zs_ref[field]
            rates = [scale * face_ref[level, rows, :] for level in range(LEVELS)]
            source = [explicit_ref[field * LEVELS + level, rows, :] for level in range(LEVELS - 1)]
            below, top = [], []
            for column in range(COLUMNS):
                start = (tile * 8 * COLUMNS + column) * 8
                below.append(back_ref[pl.ds(start + field, 8, stride=COLUMNS * 8), :])
                top.append(back_ref[pl.ds(start + FIELDS + field, 8, stride=COLUMNS * 8), :])
            below = jnp.concatenate(below, 1)
            top = jnp.concatenate(top, 1)
            source[0] = source[0] + rates[0] * below
            source[2] = source[2] + rates[3] * top
            solved = solve_inner(source, rates, inner_pivots(rates)) + (top,)
            for level in range(LEVELS):
                item = field * LEVELS + level
                present_ref[item, rows, :] = solved[level]
                if edges and tile == 0:
                    edge_refs[0][item] = solved[level][0:2]
                if edges and tile == 1:
                    edge_refs[1][item] = solved[level][6:8]


VMEM = pl.BlockSpec(memory_space=pltpu.VMEM)
SMEM = pl.BlockSpec(memory_space=pltpu.SMEM)


def struct(*shape):
    return jax.ShapeDtypeStruct(shape, jnp.float32)


def explicit_part(chunk, *operands):
    return pl.pallas_call(
        functools.partial(explicit_kernel, chunk),
        out_shape=(struct(FIELDS * LEVELS, ROWS, WIDTH), struct(BLOCKS * chunk, LANES)),
        in_specs=[SMEM, SMEM] + [VMEM] * 7,
        out_specs=(VMEM, VMEM),
        scratch_shapes=[
            pltpu.VMEM((FIELDS * LEVELS, 8, WIDTH), jnp.float32),
            pltpu.VMEM((2 * LEVELS, 8, WIDTH), jnp.float32),
        ],
        name="explicit_part",
    )(*operands)


def factor_part(got, scale):
    return pl.pallas_call(
        factor_kernel,
        out_shape=(struct(HALF, 8, LANES), struct(HALF, 8, LANES)),
        in_specs=[VMEM, VMEM],
        out_specs=(VMEM, VMEM),
        name="factor_part",
    )(got, scale)


def separator_part(got, weight, gain):
    return pl.pallas_call(
        separator_kernel,
        out_shape=struct(BLOCKS, 8, LANES),
        in_specs=[VMEM] * 3,
        out_specs=VMEM,
        name="separator_part",
    )(got, weight, gain)


def finish_part(edges, *operands):
    shapes = [struct(FIELDS * LEVELS, ROWS, WIDTH)]
    if edges:
        shapes += [struct(FIELDS * LEVELS, 2, WIDTH)] * 2
    return pl.pallas_call(
        functools.partial(finish_kernel, edges),
        out_shape=tuple(shapes),
        in_specs=[SMEM] + [VMEM] * 3,
        out_specs=(VMEM,) * len(shapes),
        name="finish_part",
    )(*operands)


def on_device(fields, velocity, face_rate, xy_rate, z_scale):
    count = lax.axis_size("gy")
    up = [(i, (i + 1) % count) for i in range(count)]
    down = [(target, source) for source, target in up]
    present = fields.reshape(FIELDS * LEVELS, ROWS, WIDTH)
    vel = velocity.reshape(2 * LEVELS, ROWS, WIDTH)
    scale = jnp.broadcast_to(jnp.tile(z_scale, 2)[:, None], (8, LANES))

    lowest = jnp.concatenate([present[:, 0:2].reshape(-1, WIDTH), vel[:, 0]], 0)
    highest = jnp.concatenate([present[:, ROWS - 2 :].reshape(-1, WIDTH), vel[:, ROWS - 1]], 0)
    south = lax.ppermute(highest, "gy", up)
    north = lax.ppermute(lowest, "gy", down)
    cut = 2 * FIELDS * LEVELS
    vel_south, vel_north = south[cut:, None], north[cut:, None]
    south = south[:cut].reshape(-1, 2, WIDTH)
    north = north[:cut].reshape(-1, 2, WIDTH)

    def swap_over(chunks):
        return lax.all_to_all(chunks, "gz", 0, 0, tiled=True)

    explicit, send = explicit_part(
        16, xy_rate, z_scale, present, south, north, vel, vel_south, vel_north, face_rate
    )
    got = swap_over(send.reshape(BLOCKS, 16, LANES))
    weight, gain = factor_part(got, scale)
    back = swap_over(separator_part(got, weight, gain))
    present, lowest, highest = finish_part(
        True, z_scale, explicit, face_rate, back.reshape(BLOCKS * 8, LANES)
    )
    south = lax.ppermute(highest, "gy", up)
    north = lax.ppermute(lowest, "gy", down)
    explicit, send = explicit_part(
        8, xy_rate, z_scale, present, south, north, vel, vel_south, vel_north, face_rate
    )
    got = swap_over(send.reshape(BLOCKS, 8, LANES))
    back = swap_over(separator_part(got, weight, gain))
    (present,) = finish_part(False, z_scale, explicit, face_rate, back.reshape(BLOCKS * 8, LANES))
    return present.reshape(fields.shape)


def solution(mesh):
    in_specs = (P(None, "gz", "gy", None), P(None, "gz", "gy", None), P("gz", "gy", None), P(), P())
    out_specs = P(None, "gz", "gy", None)
    return jax.shard_map(
        on_device, mesh=mesh, in_specs=in_specs, out_specs=out_specs, check_vma=False
    )
```

```python
import functools

import jax
import jax.numpy as jnp
from jax import lax
from jax.experimental import pallas as pl
from jax.experimental.pallas import tpu as pltpu
from jax.sharding import PartitionSpec as P

FIELDS = 4
LEVELS = 4
ITEMS = FIELDS * LEVELS
ROWS = 16
WIDTH = 512
LANES = 128
BLOCKS = 64
HALF = BLOCKS // 2
COLUMNS = WIDTH // LANES


def tendency(middle, half_x, half_y, spread):
    rows = middle.shape[0]
    eastern = pltpu.roll(middle, WIDTH - 1, 1)
    western = pltpu.roll(middle, 1, 1)
    north = pltpu.roll(middle, rows - 1, 0)
    south = pltpu.roll(middle, 1, 0)
    return spread * (eastern + western + north + south - 4.0 * middle) - (
        half_x * (eastern - western) + half_y * (north - south)
    )


def inner_pivots(rates):
    hold = 1.0 + rates[0]
    inverse = []
    for level in range(LEVELS - 1):
        once = 1.0 / (hold + rates[level + 1])
        inverse.append(once)
        hold = 1.0 + rates[level + 1] * hold * once
    return inverse


def solve_inner(source, rates, inverse):
    first = source[0]
    second = source[1] + rates[1] * inverse[0] * first
    third = (source[2] + rates[2] * inverse[1] * second) * inverse[2]
    second = (second + rates[2] * third) * inverse[1]
    first = (first + rates[1] * second) * inverse[0]
    return first, second, third


def pack_kernel(present_ref, vel_ref, low_ref, high_ref):
    low_ref[0:ITEMS] = present_ref[:, 0:2, :]
    high_ref[0:ITEMS] = present_ref[:, ROWS - 2 : ROWS, :]
    for item in range(2 * LEVELS):
        low_ref[ITEMS + item // 2, item % 2 : item % 2 + 1, :] = vel_ref[item, 0:1, :]
        high_ref[ITEMS + item // 2, item % 2 : item % 2 + 1, :] = vel_ref[item, ROWS - 1 : ROWS, :]


def explicit_kernel(chunk, xy_ref, zs_ref, present_ref, south_ref, north_ref, vel_ref, vel_south_ref,
                    vel_north_ref, face_ref, explicit_ref, send_ref, tail_ref, vel_tail_ref):
    tail_ref[:, 0:2, :] = north_ref[0:ITEMS]
    tail_ref[:, 6:8, :] = south_ref[0:ITEMS]
    for item in range(2 * LEVELS):
        row = slice(item % 2, item % 2 + 1)
        vel_tail_ref[item, 0:1, :] = vel_north_ref[ITEMS + item // 2, row, :]
        vel_tail_ref[item, 7:8, :] = vel_south_ref[ITEMS + item // 2, row, :]
    for level in range(LEVELS):
        half_x = 0.5 * jnp.concatenate([vel_ref[level], vel_tail_ref[level]], 0)
        half_y = 0.5 * jnp.concatenate([vel_ref[LEVELS + level], vel_tail_ref[LEVELS + level]], 0)
        for field in range(FIELDS):
            item = field * LEVELS + level
            spread = xy_ref[field]
            middle = jnp.concatenate([present_ref[item], tail_ref[item]], 0)
            sectioned = middle + tendency(middle, half_x, half_y, spread)
            again = sectioned + tendency(sectioned, half_x, half_y, spread)
            explicit_ref[item] = (0.5 * middle + 0.5 * again)[:ROWS]
    for tile in range(ROWS // 8):
        rows = slice(tile * 8, tile * 8 + 8)
        for field in range(FIELDS):
            scale = zs_ref[field]
            rates = [scale * face_ref[level, rows, :] for level in range(LEVELS)]
            source = [explicit_ref[field * LEVELS + level, rows, :] for level in range(LEVELS)]
            first, _, third = solve_inner(source, rates, inner_pivots(rates))
            own = source[3] + rates[3] * third
            under = rates[0] * first
            for column in range(COLUMNS):
                lanes = slice(column * LANES, column * LANES + LANES)
                start = (tile * 8 * COLUMNS + column) * chunk
                send_ref[pl.ds(start + field, 8, stride=COLUMNS * chunk), :] = own[:, lanes]
                send_ref[pl.ds(start + FIELDS + field, 8, stride=COLUMNS * chunk), :] = under[:, lanes]
        if chunk > 8:
            for level in range(LEVELS):
                for column in range(COLUMNS):
                    lanes = slice(column * LANES, column * LANES + LANES)
                    start = (tile * 8 * COLUMNS + column) * chunk
                    send_ref[pl.ds(start + 8 + level, 8, stride=COLUMNS * chunk), :] = face_ref[level, rows, lanes]


def swap(value):
    return pltpu.roll(value, 4, 0)


def lower_half():
    return lax.broadcasted_iota(jnp.int32, (8, LANES), 0) < 4


def factor_kernel(zs_ref, got_ref, weight_ref, gain_ref, back_ref):
    low = lower_half()
    field = lax.rem(lax.broadcasted_iota(jnp.int32, (8, LANES), 0), FIELDS)
    scale = jnp.full((8, LANES), zs_ref[0], jnp.float32)
    for other in range(1, FIELDS):
        scale = jnp.where(field == other, zs_ref[other], scale)
    couple, own, under = [], [], []
    for step in range(HALF):
        rates = [
            scale
            * jnp.where(
                low,
                jnp.broadcast_to(got_ref[step, 8 + level : 9 + level, :], (8, LANES)),
                jnp.broadcast_to(got_ref[BLOCKS - 1 - step, 8 + level : 9 + level, :], (8, LANES)),
            )
            for level in range(LEVELS)
        ]
        inverse = inner_pivots(rates)
        one = jnp.ones((8, LANES), jnp.float32)
        first, _, third = solve_inner([one, one, one], rates, inverse)
        own.append(1.0 + rates[3] * third)
        under.append(rates[0] * first)
        couple.append(rates[0] * inverse[0] * rates[1] * inverse[1] * rates[2] * inverse[2] * rates[3])
    zero = jnp.zeros((8, LANES), jnp.float32)
    hold = None
    for step in range(HALF):
        last = step == HALF - 1
        below = swap(under[step]) if last else under[step + 1]
        above = zero if step == 0 else under[step - 1]
        mass = own[step] + jnp.where(low, below, above)
        hold = mass + (jnp.where(low, couple[0], zero) if step == 0 else hold * gain)
        inward = jnp.where(low, swap(couple[step]) if last else couple[step + 1], couple[step])
        if last:
            other = swap(hold)
            inverse = 1.0 / (hold * other + inward * (hold + other))
            weight_ref[step] = (other + inward) * inverse
            gain_ref[step] = inward * inverse
        else:
            weight = 1.0 / (hold + inward)
            gain = inward * weight
            weight_ref[step] = weight
            gain_ref[step] = gain
    separator_kernel(got_ref, weight_ref, gain_ref, back_ref)


def separator_kernel(got_ref, weight_ref, gain_ref, back_ref):
    low = lower_half()

    def side(block):
        value = got_ref[block, 0:8, :]
        if block + 1 < BLOCKS:
            return value + swap(got_ref[block + 1, 0:8, :])
        return jnp.where(low, value, 0.0)

    value = None
    kept = []
    for step in range(HALF):
        source = jnp.where(low, side(step), swap(side(BLOCKS - 1 - step)))
        value = source if step == 0 else source + gain_ref[step - 1] * value
        kept.append(value)
    value = weight_ref[HALF - 1] * value + gain_ref[HALF - 1] * swap(value)
    back_ref[HALF] = value
    for step in reversed(range(HALF)):
        inner = value
        turned = swap(inner)
        if step > 0:
            value = weight_ref[step - 1] * kept[step - 1] + gain_ref[step - 1] * inner
            back_ref[step] = jnp.where(low, value, turned)
            back_ref[BLOCKS - step] = jnp.where(low, turned, value)
        else:
            back_ref[0] = jnp.where(low, 0.0, turned)


def finish_kernel(edges, zs_ref, explicit_ref, face_ref, back_ref, present_ref, *edge_refs):
    for tile in range(ROWS // 8):
        rows = slice(tile * 8, tile * 8 + 8)
        for field in range(FIELDS):
            scale = zs_ref[field]
            rates = [scale * face_ref[level, rows, :] for level in range(LEVELS)]
            source = [explicit_ref[field * LEVELS + level, rows, :] for level in range(LEVELS - 1)]
            below, top = [], []
            for column in range(COLUMNS):
                start = (tile * 8 * COLUMNS + column) * 8
                below.append(back_ref[pl.ds(start + field, 8, stride=COLUMNS * 8), :])
                top.append(back_ref[pl.ds(start + FIELDS + field, 8, stride=COLUMNS * 8), :])
            below = jnp.concatenate(below, 1)
            top = jnp.concatenate(top, 1)
            source[0] = source[0] + rates[0] * below
            source[2] = source[2] + rates[3] * top
            solved = solve_inner(source, rates, inner_pivots(rates)) + (top,)
            for level in range(LEVELS):
                item = field * LEVELS + level
                present_ref[item, rows, :] = solved[level]
                if edges and tile == 0:
                    edge_refs[0][item] = solved[level][0:2]
                if edges and tile == 1:
                    edge_refs[1][item] = solved[level][6:8]


VMEM = pl.BlockSpec(memory_space=pltpu.VMEM)
SMEM = pl.BlockSpec(memory_space=pltpu.SMEM)
PARAMS = pltpu.CompilerParams(vmem_limit_bytes=6 << 20)


def struct(*shape):
    return jax.ShapeDtypeStruct(shape, jnp.float32)


def pack_part(present, vel):
    shape = struct(ITEMS + LEVELS, 2, WIDTH)
    return pl.pallas_call(
        pack_kernel,
        out_shape=(shape, shape),
        in_specs=[VMEM, VMEM],
        out_specs=(VMEM, VMEM),
        compiler_params=PARAMS,
        name="pack_part",
    )(present, vel)


def explicit_part(chunk, *operands):
    return pl.pallas_call(
        functools.partial(explicit_kernel, chunk),
        out_shape=(struct(ITEMS, ROWS, WIDTH), struct(BLOCKS * chunk, LANES)),
        in_specs=[SMEM, SMEM] + [VMEM] * 7,
        out_specs=(VMEM, VMEM),
        scratch_shapes=[
            pltpu.VMEM((ITEMS, 8, WIDTH), jnp.float32),
            pltpu.VMEM((2 * LEVELS, 8, WIDTH), jnp.float32),
        ],
        compiler_params=PARAMS,
        name="explicit_part",
    )(*operands)


def factor_part(scale, got):
    return pl.pallas_call(
        factor_kernel,
        out_shape=(struct(HALF, 8, LANES), struct(HALF, 8, LANES), struct(BLOCKS, 8, LANES)),
        in_specs=[SMEM, VMEM],
        out_specs=(VMEM, VMEM, VMEM),
        compiler_params=PARAMS,
        name="factor_part",
    )(scale, got)


def separator_part(got, weight, gain):
    return pl.pallas_call(
        separator_kernel,
        out_shape=struct(BLOCKS, 8, LANES),
        in_specs=[VMEM] * 3,
        out_specs=VMEM,
        compiler_params=PARAMS,
        name="separator_part",
    )(got, weight, gain)


def finish_part(edges, *operands):
    shapes = [struct(ITEMS, ROWS, WIDTH)]
    if edges:
        shapes += [struct(ITEMS, 2, WIDTH)] * 2
    return pl.pallas_call(
        functools.partial(finish_kernel, edges),
        out_shape=tuple(shapes),
        in_specs=[SMEM] + [VMEM] * 3,
        out_specs=(VMEM,) * len(shapes),
        compiler_params=PARAMS,
        name="finish_part",
    )(*operands)


def on_device(fields, velocity, face_rate, xy_rate, z_scale):
    count = lax.axis_size("gy")
    up = [(i, (i + 1) % count) for i in range(count)]
    down = [(target, source) for source, target in up]
    present = fields.reshape(ITEMS, ROWS, WIDTH)
    vel = velocity.reshape(2 * LEVELS, ROWS, WIDTH)
    lowest, highest = pack_part(present, vel)
    south = lax.ppermute(highest, "gy", up)
    north = lax.ppermute(lowest, "gy", down)
    vel_south, vel_north = south, north

    def swap_over(chunks):
        return lax.all_to_all(chunks, "gz", 0, 0, tiled=True)

    explicit, send = explicit_part(
        16, xy_rate, z_scale, present, south, north, vel, vel_south, vel_north, face_rate
    )
    got = swap_over(send.reshape(BLOCKS, 16, LANES))
    weight, gain, back = factor_part(z_scale, got)
    back = swap_over(back)
    present, lowest, highest = finish_part(
        True, z_scale, explicit, face_rate, back.reshape(BLOCKS * 8, LANES)
    )
    south = lax.ppermute(highest, "gy", up)
    north = lax.ppermute(lowest, "gy", down)
    explicit, send = explicit_part(
        8, xy_rate, z_scale, present, south, north, vel, vel_south, vel_north, face_rate
    )
    got = swap_over(send.reshape(BLOCKS, 8, LANES))
    back = swap_over(separator_part(got, weight, gain))
    (present,) = finish_part(False, z_scale, explicit, face_rate, back.reshape(BLOCKS * 8, LANES))
    return present.reshape(fields.shape)


def solution(mesh):
    in_specs = (P(None, "gz", "gy", None), P(None, "gz", "gy", None), P("gz", "gy", None), P(), P())
    out_specs = P(None, "gz", "gy", None)
    return jax.shard_map(
        on_device, mesh=mesh, in_specs=in_specs, out_specs=out_specs, check_vma=False
    )
```

```python
import functools

import jax
import jax.numpy as jnp
from jax import lax
from jax.experimental import pallas as pl
from jax.experimental.pallas import tpu as pltpu
from jax.sharding import Mesh, PartitionSpec as P

STEPS = 2
FIELDS = 4
LEVELS = 4
ITEMS = FIELDS * LEVELS
ROWS = 16
WIDTH = 512
GROUPS = 4
MEMBERS = 16
PAIRS = MEMBERS // 2
LANES = 128
COLUMNS = WIDTH // LANES
TILE = (COLUMNS, 8, LANES)


def tendency(middle, half_x, half_y, spread):
    rows = middle.shape[0]
    eastern = pltpu.roll(middle, WIDTH - 1, 1)
    western = pltpu.roll(middle, 1, 1)
    north = pltpu.roll(middle, rows - 1, 0)
    south = pltpu.roll(middle, 1, 0)
    return spread * (eastern + western + north + south - 4.0 * middle) - (
        half_x * (eastern - western) + half_y * (north - south)
    )


def inner_pivots(rates):
    hold = 1.0 + rates[0]
    inverse = []
    for level in range(LEVELS - 1):
        once = 1.0 / (hold + rates[level + 1])
        inverse.append(once)
        hold = 1.0 + rates[level + 1] * hold * once
    return inverse


def solve_inner(source, rates, inverse):
    first = source[0]
    second = source[1] + rates[1] * inverse[0] * first
    third = (source[2] + rates[2] * inverse[1] * second) * inverse[2]
    second = (second + rates[2] * third) * inverse[1]
    first = (first + rates[1] * second) * inverse[0]
    return first, second, third


def pack_kernel(present_ref, vel_ref, low_ref, high_ref):
    low_ref[0:ITEMS] = present_ref[:, 0:2, :]
    high_ref[0:ITEMS] = present_ref[:, ROWS - 2 : ROWS, :]
    for item in range(2 * LEVELS):
        low_ref[ITEMS + item // 2, item % 2 : item % 2 + 1, :] = vel_ref[item, 0:1, :]
        high_ref[ITEMS + item // 2, item % 2 : item % 2 + 1, :] = vel_ref[item, ROWS - 1 : ROWS, :]


def places(tile, chunk, line):
    for column in range(COLUMNS):
        start = (tile * 8 * (chunk // 8) + line // 8) * COLUMNS * 8 + column * 8 + line % 8
        yield slice(column * LANES, column * LANES + LANES), pl.ds(start, 8, stride=COLUMNS * chunk)


def spread_rows(send_ref, tile, chunk, line, value):
    for lanes, lines in places(tile, chunk, line):
        send_ref[lines, :] = value[:, lanes]


def explicit_kernel(chunk, xy_ref, zs_ref, present_ref, south_ref, north_ref, vel_ref, vel_south_ref,
                    vel_north_ref, face_ref, explicit_ref, send_ref, tail_ref, vel_tail_ref):
    tail_ref[:, 0:2, :] = north_ref[0:ITEMS]
    tail_ref[:, 6:8, :] = south_ref[0:ITEMS]
    for item in range(2 * LEVELS):
        row = slice(item % 2, item % 2 + 1)
        vel_tail_ref[item, 0:1, :] = vel_north_ref[ITEMS + item // 2, row, :]
        vel_tail_ref[item, 7:8, :] = vel_south_ref[ITEMS + item // 2, row, :]
    for level in range(LEVELS):
        half_x = 0.5 * jnp.concatenate([vel_ref[level], vel_tail_ref[level]], 0)
        half_y = 0.5 * jnp.concatenate([vel_ref[LEVELS + level], vel_tail_ref[LEVELS + level]], 0)
        for field in range(FIELDS):
            item = field * LEVELS + level
            spread = xy_ref[field]
            middle = jnp.concatenate([present_ref[item], tail_ref[item]], 0)
            sectioned = middle + tendency(middle, half_x, half_y, spread)
            again = sectioned + tendency(sectioned, half_x, half_y, spread)
            explicit_ref[item] = (0.5 * middle + 0.5 * again)[:ROWS]
    for tile in range(ROWS // 8):
        rows = slice(tile * 8, tile * 8 + 8)
        for field in range(FIELDS):
            scale = zs_ref[field]
            rates = [scale * face_ref[level, rows, :] for level in range(LEVELS)]
            source = [explicit_ref[field * LEVELS + level, rows, :] for level in range(LEVELS)]
            first, _, third = solve_inner(source, rates, inner_pivots(rates))
            spread_rows(send_ref, tile, chunk, field, source[3] + rates[3] * third)
            spread_rows(send_ref, tile, chunk, FIELDS + field, rates[0] * first)
        if chunk > 8:
            for level in range(LEVELS):
                spread_rows(send_ref, tile, chunk, 8 + level, face_ref[level, rows, :])


def swap(value):
    return pltpu.roll(value, 4, 1)


def lower_half():
    return lax.broadcasted_iota(jnp.int32, TILE, 1) < 4


def pair_sources(got_ref, low):
    def side(block):
        return got_ref[block, 0] + swap(got_ref[block + 1, 0])

    return [jnp.where(low, side(step), swap(side(MEMBERS - 2 - step))) for step in range(PAIRS)]


def outer_source(got_ref, low):
    return jnp.where(low, swap(got_ref[0, 0]), swap(got_ref[MEMBERS - 1, 0]))


def eliminate(sources, gain_ref, center):
    value = sources[0]
    kept = [value]
    for step in range(1, PAIRS - 1):
        value = sources[step] + gain_ref[step - 1] * value
        kept.append(value)
    value = gain_ref[PAIRS - 2] * value
    return kept, (sources[PAIRS - 1] + value + swap(value)) * center


def reduce_kernel(first, zs_ref, got_ref, *refs):
    low = lower_half()
    if first:
        weight_ref, gain_ref, edge_ref, source_ref, send_ref = refs
        field = lax.rem(lax.broadcasted_iota(jnp.int32, TILE, 1), FIELDS)
        scale = jnp.full(TILE, zs_ref[0], jnp.float32)
        for other in range(1, FIELDS):
            scale = jnp.where(field == other, zs_ref[other], scale)
        couple, own, under = [], [], []
        for step in range(PAIRS):
            rates = [
                scale
                * jnp.where(
                    low,
                    jnp.broadcast_to(got_ref[step, 1, :, level : level + 1, :], TILE),
                    jnp.broadcast_to(got_ref[MEMBERS - 1 - step, 1, :, level : level + 1, :], TILE),
                )
                for level in range(LEVELS)
            ]
            inverse = inner_pivots(rates)
            one = jnp.ones(TILE, jnp.float32)
            bottom, _, third = solve_inner([one, one, one], rates, inverse)
            own.append(1.0 + rates[3] * third)
            under.append(rates[0] * bottom)
            couple.append(rates[0] * inverse[0] * rates[1] * inverse[1] * rates[2] * inverse[2] * rates[3])
        masses = [
            jnp.where(low, own[step] + under[step + 1], own[step + 1] + under[step]) for step in range(PAIRS - 1)
        ]
        last_own, last_under = own[PAIRS - 1], under[PAIRS - 1]
        masses.append(jnp.where(low, last_own + swap(last_under), swap(last_own) + last_under))
        hold = masses[0] + couple[0]
        through = couple[0]
        for step in range(PAIRS - 1):
            inward = couple[step + 1]
            weight = 1.0 / (hold + inward)
            gain = inward * weight
            weight_ref[step] = weight
            gain_ref[step] = gain
            through = through * gain
            hold = hold * gain + (masses[step + 1] if step + 2 < PAIRS else 0.0)
        center = 1.0 / (masses[PAIRS - 1] + hold + swap(hold))
        weight_ref[PAIRS - 1] = center
        edge_ref[...] = couple[0]
        kept, value = eliminate(masses, gain_ref, center)
        for step in reversed(range(PAIRS - 1)):
            value = weight_ref[step] * kept[step] + gain_ref[step] * value
        outer = jnp.where(low, under[0], own[0]) + couple[0] * value
        through = through * swap(through) * center
        for group in range(GROUPS):
            send_ref[group, 1] = outer
            send_ref[group, 2] = through
    else:
        weight_ref, gain_ref, edge_ref, source_ref, send_ref = refs
    sources = pair_sources(got_ref, low)
    for step in range(PAIRS):
        source_ref[step] = sources[step]
    kept, value = eliminate(sources, gain_ref, weight_ref[PAIRS - 1])
    for step in reversed(range(PAIRS - 1)):
        value = weight_ref[step] * kept[step] + gain_ref[step] * value
    outer = outer_source(got_ref, low) + edge_ref[...] * value
    for group in range(GROUPS):
        send_ref[group, 0] = outer


def across(parts, low):
    ends = jnp.where(low, swap(parts[0]) + parts[1], parts[3])
    middle = jnp.where(low, swap(parts[1]) + parts[2], parts[2] + swap(parts[3]))
    return ends, middle


def return_kernel(first, place_ref, got_ref, source_ref, weight_ref, gain_ref, edge_ref, *refs):
    low = lower_half()
    if first:
        top_ref, back_ref = refs
        ends, middle = across([got_ref[group, 1] for group in range(GROUPS)], low)
        through = [got_ref[group, 2] for group in range(GROUPS)]
        hold = ends + jnp.where(low, through[0], 0.0)
        inward = jnp.where(low, through[1], through[3])
        weight = 1.0 / (hold + inward)
        gain = inward * weight
        hold = middle + hold * gain
        other = swap(hold)
        inverse = 1.0 / (hold * other + through[2] * (hold + other))
        mine, cross = (other + through[2]) * inverse, through[2] * inverse
        for item, value in enumerate((weight, gain, mine, cross)):
            top_ref[item] = value
    else:
        top_ref, back_ref = refs
        weight, gain, mine, cross = (top_ref[item] for item in range(4))
    ends, middle = across([got_ref[group, 0] for group in range(GROUPS)], low)
    inner = middle + gain * ends
    inner = mine * inner + cross * swap(inner)
    ends = weight * ends + gain * inner
    turned = swap(ends)
    place = place_ref[0]
    value = jnp.where(
        place == 0,
        jnp.where(low, 0.0, turned),
        jnp.where(
            place == 1,
            jnp.where(low, ends, swap(inner)),
            jnp.where(place == 2, inner, jnp.where(low, swap(inner), ends)),
        ),
    )
    sources = [source_ref[step] for step in range(PAIRS)]
    sources[0] = sources[0] + edge_ref[...] * value
    kept, center = eliminate(sources, gain_ref, weight_ref[PAIRS - 1])
    solved = [center]
    for step in reversed(range(PAIRS - 1)):
        solved.insert(0, weight_ref[step] * kept[step] + gain_ref[step] * solved[0])
    outer = value
    for step in range(PAIRS):
        turned = swap(solved[step])
        back_ref[step] = jnp.where(low, outer, turned)
        back_ref[MEMBERS - 1 - step] = jnp.where(low, turned, outer)
        outer = solved[step]


def finish_kernel(edges, zs_ref, explicit_ref, face_ref, back_ref, present_ref, *edge_refs):
    for tile in range(ROWS // 8):
        rows = slice(tile * 8, tile * 8 + 8)
        for field in range(FIELDS):
            scale = zs_ref[field]
            rates = [scale * face_ref[level, rows, :] for level in range(LEVELS)]
            source = [explicit_ref[field * LEVELS + level, rows, :] for level in range(LEVELS - 1)]
            below = jnp.concatenate([back_ref[lines, :] for _, lines in places(tile, 8, field)], 1)
            top = jnp.concatenate([back_ref[lines, :] for _, lines in places(tile, 8, FIELDS + field)], 1)
            source[0] = source[0] + rates[0] * below
            source[2] = source[2] + rates[3] * top
            solved = solve_inner(source, rates, inner_pivots(rates)) + (top,)
            for level in range(LEVELS):
                item = field * LEVELS + level
                present_ref[item, rows, :] = solved[level]
                if edges and tile == 0:
                    edge_refs[0][item] = solved[level][0:2]
                if edges and tile == 1:
                    edge_refs[1][item] = solved[level][6:8]


VMEM = pl.BlockSpec(memory_space=pltpu.VMEM)
SMEM = pl.BlockSpec(memory_space=pltpu.SMEM)
PARAMS = pltpu.CompilerParams(vmem_limit_bytes=6 << 20)


def struct(*shape):
    return jax.ShapeDtypeStruct(shape, jnp.float32)


def pack_part(present, vel):
    shape = struct(ITEMS + LEVELS, 2, WIDTH)
    return pl.pallas_call(
        pack_kernel,
        out_shape=(shape, shape),
        in_specs=[VMEM, VMEM],
        out_specs=(VMEM, VMEM),
        compiler_params=PARAMS,
        name="pack_part",
    )(present, vel)


def explicit_part(chunk, *operands):
    return pl.pallas_call(
        functools.partial(explicit_kernel, chunk),
        out_shape=(struct(ITEMS, ROWS, WIDTH), struct(MEMBERS * COLUMNS * chunk, LANES)),
        in_specs=[SMEM, SMEM] + [VMEM] * 7,
        out_specs=(VMEM, VMEM),
        scratch_shapes=[
            pltpu.VMEM((ITEMS, 8, WIDTH), jnp.float32),
            pltpu.VMEM((2 * LEVELS, 8, WIDTH), jnp.float32),
        ],
        compiler_params=PARAMS,
        name="explicit_part",
    )(*operands)


def reduce_part(scale, got, factors=None):
    shapes = (struct(PAIRS, *TILE), struct(PAIRS - 1, *TILE), struct(*TILE))
    outs = (struct(PAIRS, *TILE), struct(GROUPS, 1 if factors else 3, *TILE))
    if not factors:
        outs = shapes + outs
    return pl.pallas_call(
        functools.partial(reduce_kernel, not factors),
        out_shape=outs,
        in_specs=[SMEM, VMEM] + [VMEM] * (3 if factors else 0),
        out_specs=(VMEM,) * len(outs),
        compiler_params=PARAMS,
        name="reduce_part",
    )(scale, got, *(factors or ()))


def return_part(place, got, sources, factors, top=None):
    outs = (struct(MEMBERS, *TILE),)
    if top is None:
        outs = (struct(4, *TILE),) + outs
    operands = (got, sources) + tuple(factors) + (() if top is None else (top,))
    return pl.pallas_call(
        functools.partial(return_kernel, top is None),
        out_shape=outs,
        in_specs=[SMEM] + [VMEM] * len(operands),
        out_specs=(VMEM,) * len(outs),
        compiler_params=PARAMS,
        name="return_part",
    )(place, *operands)


def finish_part(edges, *operands):
    shapes = [struct(ITEMS, ROWS, WIDTH)]
    if edges:
        shapes += [struct(ITEMS, 2, WIDTH)] * 2
    return pl.pallas_call(
        functools.partial(finish_kernel, edges),
        out_shape=tuple(shapes),
        in_specs=[SMEM] + [VMEM] * 3,
        out_specs=(VMEM,) * len(shapes),
        compiler_params=PARAMS,
        name="finish_part",
    )(*operands)


def on_device(fields, velocity, face_rate, xy_rate, z_scale):
    count = lax.axis_size("gy")
    up = [(i, (i + 1) % count) for i in range(count)]
    down = [(target, source) for source, target in up]
    present = fields.reshape(ITEMS, ROWS, WIDTH)
    vel = velocity.reshape(2 * LEVELS, ROWS, WIDTH)
    lowest, highest = pack_part(present, vel)
    south = lax.ppermute(highest, "gy", up)
    north = lax.ppermute(lowest, "gy", down)
    vel_south, vel_north = south, north

    place = lax.axis_index("zh").astype(jnp.int32).reshape(1)

    def near(chunks):
        return lax.all_to_all(chunks, "zi", 0, 0, tiled=True)

    def far(chunks):
        return lax.all_to_all(chunks, "zh", 0, 0, tiled=True)

    factors = top = None
    for step in range(STEPS):
        if step > 0:
            south = lax.ppermute(highest, "gy", up)
            north = lax.ppermute(lowest, "gy", down)
        chunk = 8 if factors else 16
        explicit, send = explicit_part(
            chunk, xy_rate, z_scale, present, south, north, vel, vel_south, vel_north, face_rate
        )
        got = near(send.reshape(MEMBERS, chunk // 8, *TILE))
        *made, sources, ports = reduce_part(z_scale, got, factors)
        factors = factors or tuple(made)
        *made, back = return_part(place, far(ports), sources, factors, top)
        top = made[0] if made else top
        present, *edges = finish_part(
            step + 1 < STEPS, z_scale, explicit, face_rate, near(back).reshape(MEMBERS * COLUMNS * 8, LANES)
        )
        if edges:
            lowest, highest = edges
    return present.reshape(fields.shape)


def solution(mesh):
    split = Mesh(mesh.devices.reshape(GROUPS, MEMBERS, -1), ("zh", "zi", "gy"))
    depth = ("zh", "zi")
    in_specs = (P(None, depth, "gy", None), P(None, depth, "gy", None), P(depth, "gy", None), P(), P())
    out_specs = P(None, depth, "gy", None)
    return jax.shard_map(
        on_device, mesh=split, in_specs=in_specs, out_specs=out_specs, check_vma=False
    )
```

```python
import functools

import jax
import jax.numpy as jnp
from jax import lax
from jax.experimental import pallas as pl
from jax.experimental.pallas import tpu as pltpu
from jax.sharding import Mesh, PartitionSpec as P

STEPS = 2
FIELDS = 4
LEVELS = 4
ITEMS = FIELDS * LEVELS
ROWS = 16
WIDTH = 512
GROUPS = 4
MEMBERS = 16
PAIRS = MEMBERS // 2
FACTORS = 7
LANES = 128
COLUMNS = WIDTH // LANES
TILE = (COLUMNS, 8, LANES)


def columns():
    return [slice(column * LANES, column * LANES + LANES) for column in range(COLUMNS)]


def inner_pivots(rates):
    hold = 1.0 + rates[0]
    inverse = []
    for level in range(LEVELS - 1):
        once = 1.0 / (hold + rates[level + 1])
        inverse.append(once)
        hold = 1.0 + rates[level + 1] * hold * once
    return inverse


def inner_factors(rates):
    inverse = inner_pivots(rates)
    return [*inverse, rates[1] * inverse[0], rates[2] * inverse[1], rates[0], rates[3]]


def solve_inner(source, factors):
    second = source[1] + factors[3] * source[0]
    third = (source[2] + factors[4] * second) * factors[2]
    second = second * factors[1] + factors[4] * third
    return source[0] * factors[0] + factors[3] * second, second, third


def pack_kernel(present_ref, vel_ref, low_ref, high_ref):
    low_ref[0:ITEMS] = present_ref[:, 0:2, :]
    high_ref[0:ITEMS] = present_ref[:, ROWS - 2 : ROWS, :]
    for item in range(2 * LEVELS):
        low_ref[ITEMS + item // 2, item % 2 : item % 2 + 1, :] = vel_ref[item, 0:1, :]
        high_ref[ITEMS + item // 2, item % 2 : item % 2 + 1, :] = vel_ref[item, ROWS - 1 : ROWS, :]


def factor_kernel(scale_ref, face_ref, factor_ref):
    for tile in range(ROWS // 8):
        rows = slice(tile * 8, tile * 8 + 8)
        for lanes in columns():
            faces = [face_ref[level, rows, lanes] for level in range(LEVELS)]
            for field in range(FIELDS):
                scale = jnp.broadcast_to(scale_ref[field : field + 1, :], (8, LANES))
                for item, value in enumerate(inner_factors([scale * face for face in faces])):
                    factor_ref[item, field, rows, lanes] = value


def places(tile, chunk, line):
    for column in range(COLUMNS):
        start = (tile * 8 * (chunk // 8) + line // 8) * COLUMNS * 8 + column * 8 + line % 8
        yield pl.ds(start, 8, stride=COLUMNS * chunk)


def along_x(middle, last, begin):
    ahead = [pltpu.roll(value, LANES - 1, 1) for value in middle]
    behind = [pltpu.roll(value, 1, 1) for value in middle]
    for column in range(COLUMNS):
        eastern = jnp.where(last, ahead[(column + 1) % COLUMNS], ahead[column])
        western = jnp.where(begin, behind[column - 1], behind[column])
        yield eastern, western


def tendency(middle, eastern, western, north, south, half_x, half_y, spread):
    return spread * (eastern + western + north + south - 4.0 * middle) - (
        half_x * (eastern - western) + half_y * (north - south)
    )


def explicit_kernel(chunk, scale_ref, factor_ref, present_ref, south_ref, north_ref, vel_ref, vel_south_ref,
                    vel_north_ref, face_ref, explicit_ref, send_ref, wide_ref, vel_wide_ref, sectioned_ref):
    for column, lanes in enumerate(columns()):
        for item in range(2 * LEVELS):
            row = slice(item % 2, item % 2 + 1)
            vel_wide_ref[item, column, 8:24, :] = 0.5 * vel_ref[item, :, lanes]
            vel_wide_ref[item, column, 7:8, :] = 0.5 * vel_south_ref[ITEMS + item // 2, row, lanes]
            vel_wide_ref[item, column, 24:25, :] = 0.5 * vel_north_ref[ITEMS + item // 2, row, lanes]
        for item in range(ITEMS):
            wide_ref[item, column, 8:24, :] = present_ref[item, :, lanes]
            wide_ref[item, column, 6:8, :] = south_ref[item, :, lanes]
            wide_ref[item, column, 24:26, :] = north_ref[item, :, lanes]
    lane = lax.broadcasted_iota(jnp.int32, (8, LANES), 1)
    last, begin = lane == LANES - 1, lane == 0
    for level in range(LEVELS):
        for field in range(FIELDS):
            item = field * LEVELS + level
            spread = jnp.broadcast_to(scale_ref[FIELDS + field : FIELDS + field + 1, :], (8, LANES))
            for tile in range(3):
                at = 7 + tile * 8
                middle = [wide_ref[item, column, at : at + 8, :] for column in range(COLUMNS)]
                for column, (eastern, western) in enumerate(along_x(middle, last, begin)):
                    sectioned_ref[item, column, tile * 8 : tile * 8 + 8, :] = middle[column] + tendency(
                        middle[column],
                        eastern,
                        western,
                        wide_ref[item, column, at + 1 : at + 9, :],
                        wide_ref[item, column, at - 1 : at + 7, :],
                        vel_wide_ref[level, column, at : at + 8, :],
                        vel_wide_ref[LEVELS + level, column, at : at + 8, :],
                        spread,
                    )
            for tile in range(ROWS // 8):
                at, row = tile * 8 + 1, tile * 8 + 8
                middle = [sectioned_ref[item, column, at : at + 8, :] for column in range(COLUMNS)]
                for column, (eastern, western) in enumerate(along_x(middle, last, begin)):
                    change = tendency(
                        middle[column],
                        eastern,
                        western,
                        sectioned_ref[item, column, at + 1 : at + 9, :],
                        sectioned_ref[item, column, at - 1 : at + 7, :],
                        vel_wide_ref[level, column, row : row + 8, :],
                        vel_wide_ref[LEVELS + level, column, row : row + 8, :],
                        spread,
                    )
                    explicit_ref[item, tile * 8 : tile * 8 + 8, column * LANES : column * LANES + LANES] = 0.5 * (
                        wide_ref[item, column, row : row + 8, :] + (middle[column] + change)
                    )
    for tile in range(ROWS // 8):
        rows = slice(tile * 8, tile * 8 + 8)
        for field in range(FIELDS):
            lines = zip(columns(), places(tile, chunk, field), places(tile, chunk, FIELDS + field), strict=True)
            for lanes, own, under in lines:
                factors = [factor_ref[item, field, rows, lanes] for item in range(FACTORS)]
                source = [explicit_ref[field * LEVELS + level, rows, lanes] for level in range(LEVELS)]
                first, _, third = solve_inner(source, factors)
                send_ref[own, :] = source[3] + factors[6] * third
                send_ref[under, :] = factors[5] * first
        if chunk > 8:
            for level in range(LEVELS):
                for lanes, line in zip(columns(), places(tile, chunk, 8 + level), strict=True):
                    send_ref[line, :] = face_ref[level, rows, lanes]


def swap(value):
    return pltpu.roll(value, 4, 1)


def lower_half():
    return lax.broadcasted_iota(jnp.int32, TILE, 1) < 4


def pair_sources(got_ref, low):
    def side(block):
        return got_ref[block, 0] + swap(got_ref[block + 1, 0])

    return [jnp.where(low, side(step), swap(side(MEMBERS - 2 - step))) for step in range(PAIRS)]


def outer_source(got_ref, low):
    return jnp.where(low, swap(got_ref[0, 0]), swap(got_ref[MEMBERS - 1, 0]))


def eliminate(sources, gain_ref, center):
    value = sources[0]
    kept = [value]
    for step in range(1, PAIRS - 1):
        value = sources[step] + gain_ref[step - 1] * value
        kept.append(value)
    value = gain_ref[PAIRS - 2] * value
    return kept, (sources[PAIRS - 1] + value + swap(value)) * center


def reduce_kernel(first, got_ref, *refs):
    low = lower_half()
    if first:
        scale_ref, weight_ref, gain_ref, edge_ref, source_ref, send_ref = refs
        scale = jnp.concatenate([scale_ref[0:FIELDS, :]] * 2, 0)[None]
        couple, own, under = [], [], []
        for step in range(PAIRS):
            rates = [
                scale
                * jnp.where(
                    low,
                    jnp.broadcast_to(got_ref[step, 1, :, level : level + 1, :], TILE),
                    jnp.broadcast_to(got_ref[MEMBERS - 1 - step, 1, :, level : level + 1, :], TILE),
                )
                for level in range(LEVELS)
            ]
            part = inner_factors(rates)
            one = jnp.ones(TILE, jnp.float32)
            bottom, _, third = solve_inner([one, one, one], part)
            own.append(1.0 + rates[3] * third)
            under.append(rates[0] * bottom)
            couple.append(rates[0] * part[3] * part[4] * part[2] * rates[3])
        masses = [
            jnp.where(low, own[step] + under[step + 1], own[step + 1] + under[step]) for step in range(PAIRS - 1)
        ]
        last_own, last_under = own[PAIRS - 1], under[PAIRS - 1]
        masses.append(jnp.where(low, last_own + swap(last_under), swap(last_own) + last_under))
        hold = masses[0] + couple[0]
        through = couple[0]
        for step in range(PAIRS - 1):
            inward = couple[step + 1]
            weight = 1.0 / (hold + inward)
            gain = inward * weight
            weight_ref[step] = weight
            gain_ref[step] = gain
            through = through * gain
            hold = hold * gain + (masses[step + 1] if step + 2 < PAIRS else 0.0)
        center = 1.0 / (masses[PAIRS - 1] + hold + swap(hold))
        weight_ref[PAIRS - 1] = center
        edge_ref[...] = couple[0]
        kept, value = eliminate(masses, gain_ref, center)
        for step in reversed(range(PAIRS - 1)):
            value = weight_ref[step] * kept[step] + gain_ref[step] * value
        outer = jnp.where(low, under[0], own[0]) + couple[0] * value
        through = through * swap(through) * center
        for group in range(GROUPS):
            send_ref[group, 1] = outer
            send_ref[group, 2] = through
    else:
        weight_ref, gain_ref, edge_ref, source_ref, send_ref = refs
    sources = pair_sources(got_ref, low)
    for step in range(PAIRS):
        source_ref[step] = sources[step]
    kept, value = eliminate(sources, gain_ref, weight_ref[PAIRS - 1])
    for step in reversed(range(PAIRS - 1)):
        value = weight_ref[step] * kept[step] + gain_ref[step] * value
    outer = outer_source(got_ref, low) + edge_ref[...] * value
    for group in range(GROUPS):
        send_ref[group, 0] = outer


def across(parts, low):
    ends = jnp.where(low, swap(parts[0]) + parts[1], parts[3])
    middle = jnp.where(low, swap(parts[1]) + parts[2], parts[2] + swap(parts[3]))
    return ends, middle


def return_kernel(first, place_ref, got_ref, source_ref, weight_ref, gain_ref, edge_ref, *refs):
    low = lower_half()
    if first:
        top_ref, back_ref = refs
        ends, middle = across([got_ref[group, 1] for group in range(GROUPS)], low)
        through = [got_ref[group, 2] for group in range(GROUPS)]
        hold = ends + jnp.where(low, through[0], 0.0)
        inward = jnp.where(low, through[1], through[3])
        weight = 1.0 / (hold + inward)
        gain = inward * weight
        hold = middle + hold * gain
        other = swap(hold)
        inverse = 1.0 / (hold * other + through[2] * (hold + other))
        mine, cross = (other + through[2]) * inverse, through[2] * inverse
        for item, value in enumerate((weight, gain, mine, cross)):
            top_ref[item] = value
    else:
        top_ref, back_ref = refs
        weight, gain, mine, cross = (top_ref[item] for item in range(4))
    ends, middle = across([got_ref[group, 0] for group in range(GROUPS)], low)
    inner = middle + gain * ends
    inner = mine * inner + cross * swap(inner)
    ends = weight * ends + gain * inner
    turned = swap(ends)
    place = place_ref[0]
    value = jnp.where(
        place == 0,
        jnp.where(low, 0.0, turned),
        jnp.where(
            place == 1,
            jnp.where(low, ends, swap(inner)),
            jnp.where(place == 2, inner, jnp.where(low, swap(inner), ends)),
        ),
    )
    sources = [source_ref[step] for step in range(PAIRS)]
    sources[0] = sources[0] + edge_ref[...] * value
    kept, center = eliminate(sources, gain_ref, weight_ref[PAIRS - 1])
    solved = [center]
    for step in reversed(range(PAIRS - 1)):
        solved.insert(0, weight_ref[step] * kept[step] + gain_ref[step] * solved[0])
    outer = value
    for step in range(PAIRS):
        turned = swap(solved[step])
        back_ref[step] = jnp.where(low, outer, turned)
        back_ref[MEMBERS - 1 - step] = jnp.where(low, turned, outer)
        outer = solved[step]


def finish_kernel(edges, factor_ref, explicit_ref, back_ref, present_ref, *edge_refs):
    for tile in range(ROWS // 8):
        rows = slice(tile * 8, tile * 8 + 8)
        for field in range(FIELDS):
            lines = zip(columns(), places(tile, 8, field), places(tile, 8, FIELDS + field), strict=True)
            for lanes, below, top in lines:
                factors = [factor_ref[item, field, rows, lanes] for item in range(FACTORS)]
                source = [explicit_ref[field * LEVELS + level, rows, lanes] for level in range(LEVELS - 1)]
                top = back_ref[top, :]
                source[0] = source[0] + factors[5] * back_ref[below, :]
                source[2] = source[2] + factors[6] * top
                solved = solve_inner(source, factors) + (top,)
                for level in range(LEVELS):
                    item = field * LEVELS + level
                    present_ref[item, rows, lanes] = solved[level]
                    if edges and tile == 0:
                        edge_refs[0][item, :, lanes] = solved[level][0:2]
                    if edges and tile == 1:
                        edge_refs[1][item, :, lanes] = solved[level][6:8]


VMEM = pl.BlockSpec(memory_space=pltpu.VMEM)
SMEM = pl.BlockSpec(memory_space=pltpu.SMEM)
PARAMS = pltpu.CompilerParams(vmem_limit_bytes=8 << 20)


def struct(*shape):
    return jax.ShapeDtypeStruct(shape, jnp.float32)


def pack_part(present, vel):
    edge = struct(ITEMS + LEVELS, 2, WIDTH)
    return pl.pallas_call(
        pack_kernel,
        out_shape=(edge, edge),
        in_specs=[VMEM, VMEM],
        out_specs=(VMEM, VMEM),
        compiler_params=PARAMS,
        name="pack_part",
    )(present, vel)


def factor_part(scale, faces):
    return pl.pallas_call(
        factor_kernel,
        out_shape=struct(FACTORS, FIELDS, ROWS, WIDTH),
        in_specs=[VMEM, VMEM],
        out_specs=VMEM,
        compiler_params=PARAMS,
        name="factor_part",
    )(scale, faces)


def explicit_part(chunk, *operands):
    return pl.pallas_call(
        functools.partial(explicit_kernel, chunk),
        out_shape=(struct(ITEMS, ROWS, WIDTH), struct(MEMBERS * COLUMNS * chunk, LANES)),
        in_specs=[VMEM] * 9,
        out_specs=(VMEM, VMEM),
        scratch_shapes=[
            pltpu.VMEM((ITEMS, COLUMNS, 32, LANES), jnp.float32),
            pltpu.VMEM((2 * LEVELS, COLUMNS, 32, LANES), jnp.float32),
            pltpu.VMEM((ITEMS, COLUMNS, 24, LANES), jnp.float32),
        ],
        compiler_params=PARAMS,
        name="explicit_part",
    )(*operands)


def reduce_part(got, factors=None, scale=None):
    shapes = (struct(PAIRS, *TILE), struct(PAIRS - 1, *TILE), struct(*TILE))
    outs = (struct(PAIRS, *TILE), struct(GROUPS, 1 if factors else 3, *TILE))
    if not factors:
        outs = shapes + outs
    return pl.pallas_call(
        functools.partial(reduce_kernel, not factors),
        out_shape=outs,
        in_specs=[VMEM] * (4 if factors else 2),
        out_specs=(VMEM,) * len(outs),
        compiler_params=PARAMS,
        name="reduce_part",
    )(got, *(factors or (scale,)))


def return_part(place, got, sources, factors, top=None):
    outs = (struct(MEMBERS, *TILE),)
    if top is None:
        outs = (struct(4, *TILE),) + outs
    operands = (got, sources) + tuple(factors) + (() if top is None else (top,))
    return pl.pallas_call(
        functools.partial(return_kernel, top is None),
        out_shape=outs,
        in_specs=[SMEM] + [VMEM] * len(operands),
        out_specs=(VMEM,) * len(outs),
        compiler_params=PARAMS,
        name="return_part",
    )(place, *operands)


def finish_part(edges, *operands):
    shapes = [struct(ITEMS, ROWS, WIDTH)]
    if edges:
        shapes += [struct(ITEMS, 2, WIDTH)] * 2
    return pl.pallas_call(
        functools.partial(finish_kernel, edges),
        out_shape=tuple(shapes),
        in_specs=[VMEM] * 3,
        out_specs=(VMEM,) * len(shapes),
        compiler_params=PARAMS,
        name="finish_part",
    )(*operands)


def on_device(fields, velocity, face_rate, xy_rate, z_scale):
    count = lax.axis_size("gy")
    up = [(i, (i + 1) % count) for i in range(count)]
    down = [(target, source) for source, target in up]
    scale = jnp.broadcast_to(jnp.concatenate([z_scale, xy_rate])[:, None], (2 * FIELDS, LANES))
    place = lax.axis_index("zh").astype(jnp.int32).reshape(1)
    scale, place = lax.optimization_barrier((scale, place))

    present = fields.reshape(ITEMS, ROWS, WIDTH)
    vel = velocity.reshape(2 * LEVELS, ROWS, WIDTH)
    faces = face_rate
    lowest, highest = pack_part(present, vel)
    south = vel_south = lax.ppermute(highest, "gy", up)
    north = vel_north = lax.ppermute(lowest, "gy", down)
    inner = factor_part(scale, faces)

    def near(chunks):
        return lax.all_to_all(chunks, "zi", 0, 0, tiled=True)

    def far(chunks):
        return lax.all_to_all(chunks, "zh", 0, 0, tiled=True)

    factors = top = None
    for step in range(STEPS):
        if step > 0:
            south = lax.ppermute(highest, "gy", up)
            north = lax.ppermute(lowest, "gy", down)
        chunk = 8 if factors else 16
        explicit, send = explicit_part(
            chunk, scale, inner, present, south, north, vel, vel_south, vel_north, faces
        )
        got = near(send.reshape(MEMBERS, chunk // 8, *TILE))
        *made, sources, ports = reduce_part(got, factors, scale)
        factors = factors or tuple(made)
        *made, back = return_part(place, far(ports), sources, factors, top)
        top = made[0] if made else top
        present, *edges = finish_part(
            step + 1 < STEPS, inner, explicit, near(back).reshape(MEMBERS * COLUMNS * 8, LANES)
        )
        if edges:
            lowest, highest = edges
    return present.reshape(fields.shape)


def solution(mesh):
    split = Mesh(mesh.devices.reshape(GROUPS, MEMBERS, -1), ("zh", "zi", "gy"))
    depth = ("zh", "zi")
    in_specs = (P(None, depth, "gy", None), P(None, depth, "gy", None), P(depth, "gy", None), P(), P())
    out_specs = P(None, depth, "gy", None)
    return jax.shard_map(
        on_device, mesh=split, in_specs=in_specs, out_specs=out_specs, check_vma=False
    )
```

```python
import functools

import jax
import jax.numpy as jnp
from jax import lax
from jax.experimental import pallas as pl
from jax.experimental.pallas import tpu as pltpu
from jax.sharding import PartitionSpec as P

STEPS = 2
FIELDS = 4
LEVELS = 4
ITEMS = FIELDS * LEVELS
ROWS = 16
WIDTH = 512
GROUPS = 4
MEMBERS = 16
PAIRS = MEMBERS // 2
FACTORS = 7
LANES = 128
COLUMNS = WIDTH // LANES
TILE = (COLUMNS, 8, LANES)


def columns():
    return [slice(column * LANES, column * LANES + LANES) for column in range(COLUMNS)]


def inner_pivots(rates):
    hold = 1.0 + rates[0]
    inverse = []
    for level in range(LEVELS - 1):
        once = 1.0 / (hold + rates[level + 1])
        inverse.append(once)
        hold = 1.0 + rates[level + 1] * hold * once
    return inverse


def inner_factors(rates):
    inverse = inner_pivots(rates)
    return [*inverse, rates[1] * inverse[0], rates[2] * inverse[1], rates[0], rates[3]]


def solve_inner(source, factors):
    second = source[1] + factors[3] * source[0]
    third = (source[2] + factors[4] * second) * factors[2]
    second = second * factors[1] + factors[4] * third
    return source[0] * factors[0] + factors[3] * second, second, third


def pack_kernel(present_ref, vel_ref, low_ref, high_ref):
    low_ref[0:ITEMS] = present_ref[:, 0:2, :]
    high_ref[0:ITEMS] = present_ref[:, ROWS - 2 : ROWS, :]
    for item in range(2 * LEVELS):
        low_ref[ITEMS + item // 2, item % 2 : item % 2 + 1, :] = vel_ref[item, 0:1, :]
        high_ref[ITEMS + item // 2, item % 2 : item % 2 + 1, :] = vel_ref[item, ROWS - 1 : ROWS, :]


def factor_kernel(scale_ref, face_ref, factor_ref):
    for tile in range(ROWS // 8):
        rows = slice(tile * 8, tile * 8 + 8)
        for lanes in columns():
            faces = [face_ref[level, rows, lanes] for level in range(LEVELS)]
            for field in range(FIELDS):
                scale = jnp.broadcast_to(scale_ref[field : field + 1, :], (8, LANES))
                for item, value in enumerate(inner_factors([scale * face for face in faces])):
                    factor_ref[item, field, rows, lanes] = value


def turned_tile(place_ref, tile):
    return jnp.where(place_ref[0] >= GROUPS // 2, 1 - tile, tile)


def places(tile, parts, line):
    for column in range(COLUMNS):
        start = column * 8 + line if line < 8 else face_line(column, line - 8)
        yield pl.ds(tile * (64 * parts) + start, 8, stride=8 * parts)


def face_line(column, level):
    return (COLUMNS + column // 2) * 8 + column % 2 * LEVELS + level


def along_x(middle, last, begin):
    ahead = [pltpu.roll(value, LANES - 1, 1) for value in middle]
    behind = [pltpu.roll(value, 1, 1) for value in middle]
    for column in range(COLUMNS):
        eastern = jnp.where(last, ahead[(column + 1) % COLUMNS], ahead[column])
        western = jnp.where(begin, behind[column - 1], behind[column])
        yield eastern, western


def tendency(middle, eastern, western, north, south, half_x, half_y, spread):
    return spread * (eastern + western + north + south - 4.0 * middle) - (
        half_x * (eastern - western) + half_y * (north - south)
    )


def explicit_kernel(parts, place_ref, scale_ref, factor_ref, present_ref, south_ref, north_ref, vel_ref, vel_south_ref,
                    vel_north_ref, face_ref, explicit_ref, send_ref, wide_ref, vel_wide_ref, sectioned_ref):
    for column, lanes in enumerate(columns()):
        for item in range(2 * LEVELS):
            row = slice(item % 2, item % 2 + 1)
            vel_wide_ref[item, column, 8:24, :] = 0.5 * vel_ref[item, :, lanes]
            vel_wide_ref[item, column, 7:8, :] = 0.5 * vel_south_ref[ITEMS + item // 2, row, lanes]
            vel_wide_ref[item, column, 24:25, :] = 0.5 * vel_north_ref[ITEMS + item // 2, row, lanes]
        for item in range(ITEMS):
            wide_ref[item, column, 8:24, :] = present_ref[item, :, lanes]
            wide_ref[item, column, 6:8, :] = south_ref[item, :, lanes]
            wide_ref[item, column, 24:26, :] = north_ref[item, :, lanes]
    lane = lax.broadcasted_iota(jnp.int32, (8, LANES), 1)
    last, begin = lane == LANES - 1, lane == 0

    def section(item, tile):
        field, level = divmod(item, LEVELS)
        spread = jnp.broadcast_to(scale_ref[FIELDS + field : FIELDS + field + 1, :], (8, LANES))
        at = 7 + tile * 8
        middle = [wide_ref[item, column, at : at + 8, :] for column in range(COLUMNS)]
        for column, (eastern, western) in enumerate(along_x(middle, last, begin)):
            sectioned_ref[item, column, tile * 8 : tile * 8 + 8, :] = middle[column] + tendency(
                middle[column],
                eastern,
                western,
                wide_ref[item, column, at + 1 : at + 9, :],
                wide_ref[item, column, at - 1 : at + 7, :],
                vel_wide_ref[level, column, at : at + 8, :],
                vel_wide_ref[LEVELS + level, column, at : at + 8, :],
                spread,
            )

    def average(item, tile):
        field, level = divmod(item, LEVELS)
        spread = jnp.broadcast_to(scale_ref[FIELDS + field : FIELDS + field + 1, :], (8, LANES))
        at, row = tile * 8 + 1, tile * 8 + 8
        middle = [sectioned_ref[item, column, at : at + 8, :] for column in range(COLUMNS)]
        for column, (eastern, western) in enumerate(along_x(middle, last, begin)):
            change = tendency(
                middle[column],
                eastern,
                western,
                sectioned_ref[item, column, at + 1 : at + 9, :],
                sectioned_ref[item, column, at - 1 : at + 7, :],
                vel_wide_ref[level, column, row : row + 8, :],
                vel_wide_ref[LEVELS + level, column, row : row + 8, :],
                spread,
            )
            explicit_ref[item, tile * 8 : tile * 8 + 8, column * LANES : column * LANES + LANES] = 0.5 * (
                wide_ref[item, column, row : row + 8, :] + (middle[column] + change)
            )

    order = [field * LEVELS + level for level in range(LEVELS) for field in range(FIELDS)]
    for turn in range(ITEMS + 1):
        for tile in range(3):
            if turn < ITEMS:
                section(order[turn], tile)
            if turn > 0 and tile < ROWS // 8:
                average(order[turn - 1], tile)
    for tile in range(ROWS // 8):
        rows = slice(tile * 8, tile * 8 + 8)
        target = turned_tile(place_ref, tile)
        for field in range(FIELDS):
            lines = zip(columns(), places(target, parts, field), places(target, parts, FIELDS + field), strict=True)
            for lanes, own, under in lines:
                factors = [factor_ref[item, field, rows, lanes] for item in range(FACTORS)]
                source = [explicit_ref[field * LEVELS + level, rows, lanes] for level in range(LEVELS)]
                first, _, third = solve_inner(source, factors)
                send_ref[own, :] = source[3] + factors[6] * third
                send_ref[under, :] = factors[5] * first
        if parts > COLUMNS:
            for level in range(LEVELS):
                for lanes, line in zip(columns(), places(target, parts, 8 + level), strict=True):
                    send_ref[line, :] = face_ref[level, rows, lanes]


def swap(value):
    return pltpu.roll(value, 4, 1)


def lower_half():
    return lax.broadcasted_iota(jnp.int32, TILE, 1) < 4


def pair_sources(got_ref, low):
    def side(block):
        return got_ref[block, 0:COLUMNS] + swap(got_ref[block + 1, 0:COLUMNS])

    return [jnp.where(low, side(step), swap(side(MEMBERS - 2 - step))) for step in range(PAIRS)]


def outer_source(got_ref, low):
    return jnp.where(low, swap(got_ref[0, 0:COLUMNS]), swap(got_ref[MEMBERS - 1, 0:COLUMNS]))


def eliminate(sources, gain_ref, center):
    value = sources[0]
    kept = [value]
    for step in range(1, PAIRS - 1):
        value = sources[step] + gain_ref[step - 1] * value
        kept.append(value)
    value = gain_ref[PAIRS - 2] * value
    return kept, (sources[PAIRS - 1] + value + swap(value)) * center


def face_rows(got_ref, block, level):
    rows = []
    for column in range(COLUMNS):
        tile, line = divmod(face_line(column, level), 8)
        rows.append(jnp.broadcast_to(got_ref[block, tile, line : line + 1, :], (8, LANES)))
    return jnp.stack(rows)


def reduce_kernel(first, got_ref, *refs):
    low = lower_half()
    if first:
        scale_ref, weight_ref, gain_ref, edge_ref, source_ref, send_ref = refs
        scale = jnp.concatenate([scale_ref[0:FIELDS, :]] * 2, 0)[None]
        couple, own, under = [], [], []
        for step in range(PAIRS):
            rates = [
                scale
                * jnp.where(
                    low,
                    face_rows(got_ref, step, level),
                    face_rows(got_ref, MEMBERS - 1 - step, level),
                )
                for level in range(LEVELS)
            ]
            part = inner_factors(rates)
            one = jnp.ones(TILE, jnp.float32)
            bottom, _, third = solve_inner([one, one, one], part)
            own.append(1.0 + rates[3] * third)
            under.append(rates[0] * bottom)
            couple.append(rates[0] * part[3] * part[4] * part[2] * rates[3])
        masses = [
            jnp.where(low, own[step] + under[step + 1], own[step + 1] + under[step]) for step in range(PAIRS - 1)
        ]
        last_own, last_under = own[PAIRS - 1], under[PAIRS - 1]
        masses.append(jnp.where(low, last_own + swap(last_under), swap(last_own) + last_under))
        hold = masses[0] + couple[0]
        through = couple[0]
        for step in range(PAIRS - 1):
            inward = couple[step + 1]
            weight = 1.0 / (hold + inward)
            gain = inward * weight
            weight_ref[step] = weight
            gain_ref[step] = gain
            through = through * gain
            hold = hold * gain + (masses[step + 1] if step + 2 < PAIRS else 0.0)
        center = 1.0 / (masses[PAIRS - 1] + hold + swap(hold))
        weight_ref[PAIRS - 1] = center
        edge_ref[...] = couple[0]
        kept, value = eliminate(masses, gain_ref, center)
        for step in reversed(range(PAIRS - 1)):
            value = weight_ref[step] * kept[step] + gain_ref[step] * value
        outer = jnp.where(low, under[0], own[0]) + couple[0] * value
        through = through * swap(through) * center
        for group in range(GROUPS):
            send_ref[group, 1] = outer
            send_ref[group, 2] = through
    else:
        weight_ref, gain_ref, edge_ref, source_ref, send_ref = refs
    sources = pair_sources(got_ref, low)
    for step in range(PAIRS):
        source_ref[step] = sources[step]
    kept, value = eliminate(sources, gain_ref, weight_ref[PAIRS - 1])
    for step in reversed(range(PAIRS - 1)):
        value = weight_ref[step] * kept[step] + gain_ref[step] * value
    outer = outer_source(got_ref, low) + edge_ref[...] * value
    for group in range(GROUPS):
        send_ref[group, 0] = outer


def across(parts, low):
    ends = jnp.where(low, swap(parts[0]) + parts[1], parts[3])
    middle = jnp.where(low, swap(parts[1]) + parts[2], parts[2] + swap(parts[3]))
    return ends, middle


def return_kernel(first, place_ref, got_ref, source_ref, weight_ref, gain_ref, edge_ref, *refs):
    low = lower_half()
    if first:
        top_ref, back_ref = refs
        ends, middle = across([got_ref[group, 1] for group in range(GROUPS)], low)
        through = [got_ref[group, 2] for group in range(GROUPS)]
        hold = ends + jnp.where(low, through[0], 0.0)
        inward = jnp.where(low, through[1], through[3])
        weight = 1.0 / (hold + inward)
        gain = inward * weight
        hold = middle + hold * gain
        other = swap(hold)
        inverse = 1.0 / (hold * other + through[2] * (hold + other))
        mine, cross = (other + through[2]) * inverse, through[2] * inverse
        for item, value in enumerate((weight, gain, mine, cross)):
            top_ref[item] = value
    else:
        top_ref, back_ref = refs
        weight, gain, mine, cross = (top_ref[item] for item in range(4))
    ends, middle = across([got_ref[group, 0] for group in range(GROUPS)], low)
    inner = middle + gain * ends
    inner = mine * inner + cross * swap(inner)
    ends = weight * ends + gain * inner
    turned = swap(ends)
    place = place_ref[0]
    value = jnp.where(
        place == 0,
        jnp.where(low, 0.0, turned),
        jnp.where(
            place == 1,
            jnp.where(low, ends, swap(inner)),
            jnp.where(place == 2, inner, jnp.where(low, swap(inner), ends)),
        ),
    )
    sources = [source_ref[step] for step in range(PAIRS)]
    sources[0] = sources[0] + edge_ref[...] * value
    kept, center = eliminate(sources, gain_ref, weight_ref[PAIRS - 1])
    solved = [center]
    for step in reversed(range(PAIRS - 1)):
        solved.insert(0, weight_ref[step] * kept[step] + gain_ref[step] * solved[0])
    outer = value
    for step in range(PAIRS):
        turned = swap(solved[step])
        back_ref[step] = jnp.where(low, outer, turned)
        back_ref[MEMBERS - 1 - step] = jnp.where(low, turned, outer)
        outer = solved[step]


def finish_kernel(edges, place_ref, factor_ref, explicit_ref, back_ref, present_ref, *edge_refs):
    for tile in range(ROWS // 8):
        rows = slice(tile * 8, tile * 8 + 8)
        target = turned_tile(place_ref, tile)
        for field in range(FIELDS):
            lines = zip(columns(), places(target, COLUMNS, field), places(target, COLUMNS, FIELDS + field), strict=True)
            for lanes, below, top in lines:
                factors = [factor_ref[item, field, rows, lanes] for item in range(FACTORS)]
                source = [explicit_ref[field * LEVELS + level, rows, lanes] for level in range(LEVELS - 1)]
                top = back_ref[top, :]
                source[0] = source[0] + factors[5] * back_ref[below, :]
                source[2] = source[2] + factors[6] * top
                solved = solve_inner(source, factors) + (top,)
                for level in range(LEVELS):
                    item = field * LEVELS + level
                    present_ref[item, rows, lanes] = solved[level]
                    if edges and tile == 0:
                        edge_refs[0][item, :, lanes] = solved[level][0:2]
                    if edges and tile == 1:
                        edge_refs[1][item, :, lanes] = solved[level][6:8]


VMEM = pl.BlockSpec(memory_space=pltpu.VMEM)
SMEM = pl.BlockSpec(memory_space=pltpu.SMEM)
PARAMS = pltpu.CompilerParams(vmem_limit_bytes=8 << 20)


def struct(*shape):
    return jax.ShapeDtypeStruct(shape, jnp.float32)


def pack_part(present, vel):
    edge = struct(ITEMS + LEVELS, 2, WIDTH)
    return pl.pallas_call(
        pack_kernel,
        out_shape=(edge, edge),
        in_specs=[VMEM, VMEM],
        out_specs=(VMEM, VMEM),
        compiler_params=PARAMS,
        name="pack_part",
    )(present, vel)


def factor_part(scale, faces):
    return pl.pallas_call(
        factor_kernel,
        out_shape=struct(FACTORS, FIELDS, ROWS, WIDTH),
        in_specs=[VMEM, VMEM],
        out_specs=VMEM,
        compiler_params=PARAMS,
        name="factor_part",
    )(scale, faces)


def explicit_part(parts, *operands):
    return pl.pallas_call(
        functools.partial(explicit_kernel, parts),
        out_shape=(struct(ITEMS, ROWS, WIDTH), struct(MEMBERS * parts * 8, LANES)),
        in_specs=[SMEM] + [VMEM] * 9,
        out_specs=(VMEM, VMEM),
        scratch_shapes=[
            pltpu.VMEM((ITEMS, COLUMNS, 32, LANES), jnp.float32),
            pltpu.VMEM((2 * LEVELS, COLUMNS, 32, LANES), jnp.float32),
            pltpu.VMEM((ITEMS, COLUMNS, 24, LANES), jnp.float32),
        ],
        compiler_params=PARAMS,
        name="explicit_part",
    )(*operands)


def reduce_part(got, factors=None, scale=None):
    shapes = (struct(PAIRS, *TILE), struct(PAIRS - 1, *TILE), struct(*TILE))
    outs = (struct(PAIRS, *TILE), struct(GROUPS, 1 if factors else 3, *TILE))
    if not factors:
        outs = shapes + outs
    return pl.pallas_call(
        functools.partial(reduce_kernel, not factors),
        out_shape=outs,
        in_specs=[VMEM] * (4 if factors else 2),
        out_specs=(VMEM,) * len(outs),
        compiler_params=PARAMS,
        name="reduce_part",
    )(got, *(factors or (scale,)))


def return_part(place, got, sources, factors, top=None):
    outs = (struct(MEMBERS, *TILE),)
    if top is None:
        outs = (struct(4, *TILE),) + outs
    operands = (got, sources) + tuple(factors) + (() if top is None else (top,))
    return pl.pallas_call(
        functools.partial(return_kernel, top is None),
        out_shape=outs,
        in_specs=[SMEM] + [VMEM] * len(operands),
        out_specs=(VMEM,) * len(outs),
        compiler_params=PARAMS,
        name="return_part",
    )(place, *operands)


def finish_part(edges, *operands):
    shapes = [struct(ITEMS, ROWS, WIDTH)]
    if edges:
        shapes += [struct(ITEMS, 2, WIDTH)] * 2
    return pl.pallas_call(
        functools.partial(finish_kernel, edges),
        out_shape=tuple(shapes),
        in_specs=[SMEM] + [VMEM] * 3,
        out_specs=(VMEM,) * len(shapes),
        compiler_params=PARAMS,
        name="finish_part",
    )(*operands)


def on_device(fields, velocity, face_rate, xy_rate, z_scale):
    count = lax.axis_size("gy")
    up = [(i, (i + 1) % count) for i in range(count)]
    down = [(target, source) for source, target in up]
    scale = jnp.broadcast_to(jnp.concatenate([z_scale, xy_rate])[:, None], (2 * FIELDS, LANES))
    place = (lax.axis_index("gz") // MEMBERS).astype(jnp.int32).reshape(1)
    scale, place = lax.optimization_barrier((scale, place))

    present = fields.reshape(ITEMS, ROWS, WIDTH)
    vel = velocity.reshape(2 * LEVELS, ROWS, WIDTH)
    faces = face_rate
    lowest, highest = pack_part(present, vel)
    south = vel_south = lax.ppermute(highest, "gy", up)
    north = vel_north = lax.ppermute(lowest, "gy", down)
    inner = factor_part(scale, faces)

    near_groups = [[group * MEMBERS + member for member in range(MEMBERS)] for group in range(GROUPS)]
    far_groups = [
        [group * MEMBERS + (row + group // 2 * 8) % MEMBERS for group in range(GROUPS)] for row in range(MEMBERS)
    ]

    def near(chunks):
        return lax.all_to_all(chunks, "gz", 0, 0, tiled=True, axis_index_groups=near_groups)

    def far(chunks):
        return lax.all_to_all(chunks, "gz", 0, 0, tiled=True, axis_index_groups=far_groups)

    factors = top = None
    for step in range(STEPS):
        if step > 0:
            south = lax.ppermute(highest, "gy", up)
            north = lax.ppermute(lowest, "gy", down)
        parts = COLUMNS if factors else COLUMNS + 2
        explicit, send = explicit_part(
            parts, place, scale, inner, present, south, north, vel, vel_south, vel_north, faces
        )
        got = near(send.reshape(MEMBERS, parts, 8, LANES))
        *made, sources, ports = reduce_part(got, factors, scale)
        factors = factors or tuple(made)
        *made, back = return_part(place, far(ports), sources, factors, top)
        top = made[0] if made else top
        present, *edges = finish_part(
            step + 1 < STEPS, place, inner, explicit, near(back).reshape(MEMBERS * COLUMNS * 8, LANES)
        )
        if edges:
            lowest, highest = edges
    return present.reshape(fields.shape)


def solution(mesh):
    in_specs = (P(None, "gz", "gy", None), P(None, "gz", "gy", None), P("gz", "gy", None), P(), P())
    out_specs = P(None, "gz", "gy", None)
    return jax.shard_map(
        on_device, mesh=mesh, in_specs=in_specs, out_specs=out_specs, check_vma=False
    )
```

```python
import functools

import jax
import jax.numpy as jnp
from jax import lax
from jax.experimental import pallas as pl
from jax.experimental.pallas import tpu as pltpu
from jax.sharding import PartitionSpec as P

STEPS = 2
FIELDS = 4
LEVELS = 4
ITEMS = FIELDS * LEVELS
ROWS = 16
WIDTH = 512
GROUPS = 4
MEMBERS = 16
PAIRS = MEMBERS // 2
FACTORS = 7
LANES = 128
COLUMNS = WIDTH // LANES
TILE = (COLUMNS, 8, LANES)


def columns():
    return [slice(column * LANES, column * LANES + LANES) for column in range(COLUMNS)]


def inner_pivots(rates):
    hold = 1.0 + rates[0]
    inverse = []
    for level in range(LEVELS - 1):
        once = 1.0 / (hold + rates[level + 1])
        inverse.append(once)
        hold = 1.0 + rates[level + 1] * hold * once
    return inverse


def inner_factors(rates):
    inverse = inner_pivots(rates)
    return [*inverse, rates[1] * inverse[0], rates[2] * inverse[1], rates[0], rates[3]]


def solve_inner(source, factors):
    second = source[1] + factors[3] * source[0]
    third = (source[2] + factors[4] * second) * factors[2]
    second = second * factors[1] + factors[4] * third
    return source[0] * factors[0] + factors[3] * second, second, third


def pack_kernel(present_ref, vel_ref, low_ref, high_ref):
    low_ref[0:ITEMS] = present_ref[:, 0:2, :]
    high_ref[0:ITEMS] = present_ref[:, ROWS - 2 : ROWS, :]
    for item in range(2 * LEVELS):
        low_ref[ITEMS + item // 2, item % 2 : item % 2 + 1, :] = vel_ref[item, 0:1, :]
        high_ref[ITEMS + item // 2, item % 2 : item % 2 + 1, :] = vel_ref[item, ROWS - 1 : ROWS, :]


def factor_kernel(scale_ref, face_ref, factor_ref):
    for tile in range(ROWS // 8):
        rows = slice(tile * 8, tile * 8 + 8)
        for lanes in columns():
            faces = [face_ref[level, rows, lanes] for level in range(LEVELS)]
            for field in range(FIELDS):
                scale = jnp.broadcast_to(scale_ref[field : field + 1, :], (8, LANES))
                for item, value in enumerate(inner_factors([scale * face for face in faces])):
                    factor_ref[item, field, rows, lanes] = value


def turned_tile(place_ref, tile):
    return jnp.where(place_ref[0] >= GROUPS // 2, 1 - tile, tile)


def places(tile, parts, line):
    for column in range(COLUMNS):
        start = column * 8 + line if line < 8 else face_line(column, line - 8)
        yield pl.ds(tile * (64 * parts) + start, 8, stride=8 * parts)


def face_line(column, level):
    return (COLUMNS + column // 2) * 8 + column % 2 * LEVELS + level


def along_x(middle, last, begin):
    ahead = [pltpu.roll(value, LANES - 1, 1) for value in middle]
    behind = [pltpu.roll(value, 1, 1) for value in middle]
    for column in range(COLUMNS):
        eastern = jnp.where(last, ahead[(column + 1) % COLUMNS], ahead[column])
        western = jnp.where(begin, behind[column - 1], behind[column])
        yield eastern, western


def tendency(middle, eastern, western, north, south, half_x, half_y, spread):
    return spread * (eastern + western + north + south - 4.0 * middle) - (
        half_x * (eastern - western) + half_y * (north - south)
    )


def edge_lanes():
    lane = lax.broadcasted_iota(jnp.int32, (8, LANES), 1)
    return lane == LANES - 1, lane == 0


def spread_of(scale_ref, field):
    return jnp.broadcast_to(scale_ref[FIELDS + field : FIELDS + field + 1, :], (8, LANES))


ORDER = [field * LEVELS + level for level in range(LEVELS) for field in range(FIELDS)]


def interior_kernel(scale_ref, present_ref, vel_ref, explicit_ref, wide_ref, sectioned_ref):
    last, begin = edge_lanes()

    def section(item, tile):
        field, level = divmod(item, LEVELS)
        rows, at = slice(tile * 8, tile * 8 + 8), tile * 8 + 8
        middle = [present_ref[item, rows, lanes] for lanes in columns()]
        for column, (eastern, western) in enumerate(along_x(middle, last, begin)):
            lanes = slice(column * LANES, column * LANES + LANES)
            sectioned_ref[item, column, at : at + 8, :] = middle[column] + tendency(
                middle[column],
                eastern,
                western,
                wide_ref[item, column, at + 1 : at + 9, :],
                wide_ref[item, column, at - 1 : at + 7, :],
                0.5 * vel_ref[level, rows, lanes],
                0.5 * vel_ref[LEVELS + level, rows, lanes],
                spread_of(scale_ref, field),
            )

    def average(item, tile):
        field, level = divmod(item, LEVELS)
        rows, at = slice(tile * 8, tile * 8 + 8), tile * 8 + 8
        middle = [sectioned_ref[item, column, at : at + 8, :] for column in range(COLUMNS)]
        for column, (eastern, western) in enumerate(along_x(middle, last, begin)):
            lanes = slice(column * LANES, column * LANES + LANES)
            change = tendency(
                middle[column],
                eastern,
                western,
                sectioned_ref[item, column, at + 1 : at + 9, :],
                sectioned_ref[item, column, at - 1 : at + 7, :],
                0.5 * vel_ref[level, rows, lanes],
                0.5 * vel_ref[LEVELS + level, rows, lanes],
                spread_of(scale_ref, field),
            )
            explicit_ref[item, rows, lanes] = 0.5 * (present_ref[item, rows, lanes] + (middle[column] + change))

    for item in range(ITEMS):
        for column, lanes in enumerate(columns()):
            wide_ref[item, column, 8:24, :] = present_ref[item, :, lanes]
    for turn in range(ITEMS + 1):
        for tile in range(ROWS // 8):
            if turn < ITEMS:
                section(ORDER[turn], tile)
            if turn > 0:
                average(ORDER[turn - 1], tile)


def strip_tiles(strip_ref, item, column, low):
    lines = [strip_ref[item, column, at : at + 8, :] for at in range(5)]
    return [jnp.where(low, lines[at], lines[at + 2]) for at in range(3)]


def explicit_kernel(parts, place_ref, scale_ref, factor_ref, inner_ref, present_ref, south_ref, north_ref, vel_ref,
                    vel_south_ref, vel_north_ref, face_ref, explicit_ref, send_ref, strip_ref, vel_strip_ref,
                    vel_tile_ref, sectioned_ref):
    last, begin = edge_lanes()
    low = lax.broadcasted_iota(jnp.int32, (8, LANES), 0) < 4
    for column, lanes in enumerate(columns()):
        for item in range(2 * LEVELS):
            row = slice(item % 2, item % 2 + 1)
            vel_strip_ref[item, column, 1:2, :] = 0.5 * vel_south_ref[ITEMS + item // 2, row, lanes]
            vel_strip_ref[item, column, 2:6, :] = 0.5 * vel_ref[item, 0:4, lanes]
            vel_strip_ref[item, column, 6:10, :] = 0.5 * vel_ref[item, ROWS - 4 : ROWS, lanes]
            vel_strip_ref[item, column, 10:11, :] = 0.5 * vel_north_ref[ITEMS + item // 2, row, lanes]
            _, near, far = strip_tiles(vel_strip_ref, item, column, low)
            vel_tile_ref[0, item, column] = near
            vel_tile_ref[1, item, column] = far
        for item in range(ITEMS):
            strip_ref[item, column, 0:2, :] = south_ref[item, :, lanes]
            strip_ref[item, column, 2:6, :] = present_ref[item, 0:4, lanes]
            strip_ref[item, column, 6:10, :] = present_ref[item, ROWS - 4 : ROWS, lanes]
            strip_ref[item, column, 10:12, :] = north_ref[item, :, lanes]

    def section(item):
        field, level = divmod(item, LEVELS)
        tiles = [strip_tiles(strip_ref, item, column, low) for column in range(COLUMNS)]
        middle = [tile[1] for tile in tiles]
        for column, (eastern, western) in enumerate(along_x(middle, last, begin)):
            sectioned_ref[item, column, 0:8, :] = middle[column] + tendency(
                middle[column],
                eastern,
                western,
                tiles[column][2],
                tiles[column][0],
                vel_tile_ref[0, level, column],
                vel_tile_ref[0, LEVELS + level, column],
                spread_of(scale_ref, field),
            )

    def average(item):
        field, level = divmod(item, LEVELS)
        middle = [sectioned_ref[item, column, 1:9, :] for column in range(COLUMNS)]
        for column, (eastern, western) in enumerate(along_x(middle, last, begin)):
            lanes = slice(column * LANES, column * LANES + LANES)
            change = tendency(
                middle[column],
                eastern,
                western,
                sectioned_ref[item, column, 2:10, :],
                sectioned_ref[item, column, 0:8, :],
                vel_tile_ref[1, level, column],
                vel_tile_ref[1, LEVELS + level, column],
                spread_of(scale_ref, field),
            )
            here = jnp.where(low, strip_ref[item, column, 2:10, :], strip_ref[item, column, 4:12, :])
            value = 0.5 * (here + (middle[column] + change))
            explicit_ref[item, 0:2, lanes] = value[0:2]
            explicit_ref[item, ROWS - 2 : ROWS, lanes] = value[4:6]

    for item in range(ITEMS):
        explicit_ref[item, 2 : ROWS - 2, :] = inner_ref[item, 2 : ROWS - 2, :]
    for turn in range(ITEMS + 1):
        if turn < ITEMS:
            section(ORDER[turn])
        if turn > 0:
            average(ORDER[turn - 1])
    for tile in range(ROWS // 8):
        rows = slice(tile * 8, tile * 8 + 8)
        target = turned_tile(place_ref, tile)
        for field in range(FIELDS):
            lines = zip(columns(), places(target, parts, field), places(target, parts, FIELDS + field), strict=True)
            for lanes, own, under in lines:
                factors = [factor_ref[item, field, rows, lanes] for item in range(FACTORS)]
                source = [explicit_ref[field * LEVELS + level, rows, lanes] for level in range(LEVELS)]
                first, _, third = solve_inner(source, factors)
                send_ref[own, :] = source[3] + factors[6] * third
                send_ref[under, :] = factors[5] * first
        if parts > COLUMNS:
            for level in range(LEVELS):
                for lanes, line in zip(columns(), places(target, parts, 8 + level), strict=True):
                    send_ref[line, :] = face_ref[level, rows, lanes]


def swap(value):
    return pltpu.roll(value, 4, 1)


def lower_half():
    return lax.broadcasted_iota(jnp.int32, TILE, 1) < 4


def pair_sources(got_ref, low):
    def side(block):
        return got_ref[block, 0:COLUMNS] + swap(got_ref[block + 1, 0:COLUMNS])

    return [jnp.where(low, side(step), swap(side(MEMBERS - 2 - step))) for step in range(PAIRS)]


def outer_source(got_ref, low):
    return jnp.where(low, swap(got_ref[0, 0:COLUMNS]), swap(got_ref[MEMBERS - 1, 0:COLUMNS]))


def eliminate(sources, gain_ref, center):
    value = sources[0]
    kept = [value]
    for step in range(1, PAIRS - 1):
        value = sources[step] + gain_ref[step - 1] * value
        kept.append(value)
    value = gain_ref[PAIRS - 2] * value
    return kept, (sources[PAIRS - 1] + value + swap(value)) * center


def face_rows(got_ref, block, level):
    rows = []
    for column in range(COLUMNS):
        tile, line = divmod(face_line(column, level), 8)
        rows.append(jnp.broadcast_to(got_ref[block, tile, line : line + 1, :], (8, LANES)))
    return jnp.stack(rows)


def reduce_kernel(first, got_ref, *refs):
    low = lower_half()
    if first:
        scale_ref, weight_ref, gain_ref, edge_ref, source_ref, send_ref = refs
        scale = jnp.concatenate([scale_ref[0:FIELDS, :]] * 2, 0)[None]
        couple, own, under = [], [], []
        for step in range(PAIRS):
            rates = [
                scale
                * jnp.where(
                    low,
                    face_rows(got_ref, step, level),
                    face_rows(got_ref, MEMBERS - 1 - step, level),
                )
                for level in range(LEVELS)
            ]
            part = inner_factors(rates)
            one = jnp.ones(TILE, jnp.float32)
            bottom, _, third = solve_inner([one, one, one], part)
            own.append(1.0 + rates[3] * third)
            under.append(rates[0] * bottom)
            couple.append(rates[0] * part[3] * part[4] * part[2] * rates[3])
        masses = [
            jnp.where(low, own[step] + under[step + 1], own[step + 1] + under[step]) for step in range(PAIRS - 1)
        ]
        last_own, last_under = own[PAIRS - 1], under[PAIRS - 1]
        masses.append(jnp.where(low, last_own + swap(last_under), swap(last_own) + last_under))
        hold = masses[0] + couple[0]
        through = couple[0]
        for step in range(PAIRS - 1):
            inward = couple[step + 1]
            weight = 1.0 / (hold + inward)
            gain = inward * weight
            weight_ref[step] = weight
            gain_ref[step] = gain
            through = through * gain
            hold = hold * gain + (masses[step + 1] if step + 2 < PAIRS else 0.0)
        center = 1.0 / (masses[PAIRS - 1] + hold + swap(hold))
        weight_ref[PAIRS - 1] = center
        edge_ref[...] = couple[0]
        kept, value = eliminate(masses, gain_ref, center)
        for step in reversed(range(PAIRS - 1)):
            value = weight_ref[step] * kept[step] + gain_ref[step] * value
        outer = jnp.where(low, under[0], own[0]) + couple[0] * value
        through = through * swap(through) * center
        for group in range(GROUPS):
            send_ref[group, 1] = outer
            send_ref[group, 2] = through
    else:
        weight_ref, gain_ref, edge_ref, source_ref, send_ref = refs
    sources = pair_sources(got_ref, low)
    for step in range(PAIRS):
        source_ref[step] = sources[step]
    kept, value = eliminate(sources, gain_ref, weight_ref[PAIRS - 1])
    for step in reversed(range(PAIRS - 1)):
        value = weight_ref[step] * kept[step] + gain_ref[step] * value
    outer = outer_source(got_ref, low) + edge_ref[...] * value
    for group in range(GROUPS):
        send_ref[group, 0] = outer


def across(parts, low):
    ends = jnp.where(low, swap(parts[0]) + parts[1], parts[3])
    middle = jnp.where(low, swap(parts[1]) + parts[2], parts[2] + swap(parts[3]))
    return ends, middle


def return_kernel(first, place_ref, got_ref, source_ref, weight_ref, gain_ref, edge_ref, *refs):
    low = lower_half()
    if first:
        top_ref, back_ref = refs
        ends, middle = across([got_ref[group, 1] for group in range(GROUPS)], low)
        through = [got_ref[group, 2] for group in range(GROUPS)]
        hold = ends + jnp.where(low, through[0], 0.0)
        inward = jnp.where(low, through[1], through[3])
        weight = 1.0 / (hold + inward)
        gain = inward * weight
        hold = middle + hold * gain
        other = swap(hold)
        inverse = 1.0 / (hold * other + through[2] * (hold + other))
        mine, cross = (other + through[2]) * inverse, through[2] * inverse
        for item, value in enumerate((weight, gain, mine, cross)):
            top_ref[item] = value
    else:
        top_ref, back_ref = refs
        weight, gain, mine, cross = (top_ref[item] for item in range(4))
    ends, middle = across([got_ref[group, 0] for group in range(GROUPS)], low)
    inner = middle + gain * ends
    inner = mine * inner + cross * swap(inner)
    ends = weight * ends + gain * inner
    turned = swap(ends)
    place = place_ref[0]
    value = jnp.where(
        place == 0,
        jnp.where(low, 0.0, turned),
        jnp.where(
            place == 1,
            jnp.where(low, ends, swap(inner)),
            jnp.where(place == 2, inner, jnp.where(low, swap(inner), ends)),
        ),
    )
    sources = [source_ref[step] for step in range(PAIRS)]
    sources[0] = sources[0] + edge_ref[...] * value
    kept, center = eliminate(sources, gain_ref, weight_ref[PAIRS - 1])
    solved = [center]
    for step in reversed(range(PAIRS - 1)):
        solved.insert(0, weight_ref[step] * kept[step] + gain_ref[step] * solved[0])
    outer = value
    for step in range(PAIRS):
        turned = swap(solved[step])
        back_ref[step] = jnp.where(low, outer, turned)
        back_ref[MEMBERS - 1 - step] = jnp.where(low, turned, outer)
        outer = solved[step]


def finish_kernel(edges, place_ref, factor_ref, explicit_ref, back_ref, present_ref, *edge_refs):
    for tile in range(ROWS // 8):
        rows = slice(tile * 8, tile * 8 + 8)
        target = turned_tile(place_ref, tile)
        for field in range(FIELDS):
            lines = zip(columns(), places(target, COLUMNS, field), places(target, COLUMNS, FIELDS + field), strict=True)
            for lanes, below, top in lines:
                factors = [factor_ref[item, field, rows, lanes] for item in range(FACTORS)]
                source = [explicit_ref[field * LEVELS + level, rows, lanes] for level in range(LEVELS - 1)]
                top = back_ref[top, :]
                source[0] = source[0] + factors[5] * back_ref[below, :]
                source[2] = source[2] + factors[6] * top
                solved = solve_inner(source, factors) + (top,)
                for level in range(LEVELS):
                    item = field * LEVELS + level
                    present_ref[item, rows, lanes] = solved[level]
                    if edges and tile == 0:
                        edge_refs[0][item, :, lanes] = solved[level][0:2]
                    if edges and tile == 1:
                        edge_refs[1][item, :, lanes] = solved[level][6:8]


VMEM = pl.BlockSpec(memory_space=pltpu.VMEM)
SMEM = pl.BlockSpec(memory_space=pltpu.SMEM)
PARAMS = pltpu.CompilerParams(vmem_limit_bytes=8 << 20)


def struct(*shape):
    return jax.ShapeDtypeStruct(shape, jnp.float32)


def pack_part(present, vel):
    edge = struct(ITEMS + LEVELS, 2, WIDTH)
    return pl.pallas_call(
        pack_kernel,
        out_shape=(edge, edge),
        in_specs=[VMEM, VMEM],
        out_specs=(VMEM,) * 2,
        compiler_params=PARAMS,
        name="pack_part",
    )(present, vel)


def factor_part(scale, faces):
    return pl.pallas_call(
        factor_kernel,
        out_shape=struct(FACTORS, FIELDS, ROWS, WIDTH),
        in_specs=[VMEM, VMEM],
        out_specs=VMEM,
        compiler_params=PARAMS,
        name="factor_part",
    )(scale, faces)


def interior_part(scale, present, vel):
    return pl.pallas_call(
        interior_kernel,
        out_shape=struct(ITEMS, ROWS, WIDTH),
        in_specs=[VMEM] * 3,
        out_specs=VMEM,
        scratch_shapes=[pltpu.VMEM((ITEMS, COLUMNS, 32, LANES), jnp.float32)] * 2,
        compiler_params=PARAMS,
        cost_estimate=pl.CostEstimate(flops=8 << 20, bytes_accessed=3 << 20, transcendentals=0),
        name="interior_part",
    )(scale, present, vel)


def explicit_part(parts, *operands):
    return pl.pallas_call(
        functools.partial(explicit_kernel, parts),
        out_shape=(struct(ITEMS, ROWS, WIDTH), struct(MEMBERS * parts * 8, LANES)),
        in_specs=[SMEM] + [VMEM] * 10,
        out_specs=(VMEM, VMEM),
        scratch_shapes=[
            pltpu.VMEM((ITEMS, COLUMNS, 16, LANES), jnp.float32),
            pltpu.VMEM((2 * LEVELS, COLUMNS, 16, LANES), jnp.float32),
            pltpu.VMEM((2, 2 * LEVELS, COLUMNS, 8, LANES), jnp.float32),
            pltpu.VMEM((ITEMS, COLUMNS, 16, LANES), jnp.float32),
        ],
        compiler_params=PARAMS,
        name="explicit_part",
    )(*operands)


def reduce_part(got, factors=None, scale=None):
    shapes = (struct(PAIRS, *TILE), struct(PAIRS - 1, *TILE), struct(*TILE))
    outs = (struct(PAIRS, *TILE), struct(GROUPS, 1 if factors else 3, *TILE))
    if not factors:
        outs = shapes + outs
    return pl.pallas_call(
        functools.partial(reduce_kernel, not factors),
        out_shape=outs,
        in_specs=[VMEM] * (4 if factors else 2),
        out_specs=(VMEM,) * len(outs),
        compiler_params=PARAMS,
        name="reduce_part",
    )(got, *(factors or (scale,)))


def return_part(place, got, sources, factors, top=None):
    outs = (struct(MEMBERS, *TILE),)
    if top is None:
        outs = (struct(4, *TILE),) + outs
    operands = (got, sources) + tuple(factors) + (() if top is None else (top,))
    return pl.pallas_call(
        functools.partial(return_kernel, top is None),
        out_shape=outs,
        in_specs=[SMEM] + [VMEM] * len(operands),
        out_specs=(VMEM,) * len(outs),
        compiler_params=PARAMS,
        name="return_part",
    )(place, *operands)


def finish_part(edges, *operands):
    shapes = [struct(ITEMS, ROWS, WIDTH)]
    if edges:
        shapes += [struct(ITEMS, 2, WIDTH)] * 2
    return pl.pallas_call(
        functools.partial(finish_kernel, edges),
        out_shape=tuple(shapes),
        in_specs=[SMEM] + [VMEM] * 3,
        out_specs=(VMEM,) * len(shapes),
        compiler_params=PARAMS,
        name="finish_part",
    )(*operands)


def on_device(fields, velocity, face_rate, xy_rate, z_scale):
    count = lax.axis_size("gy")
    up = [(i, (i + 1) % count) for i in range(count)]
    down = [(target, source) for source, target in up]
    scale = jnp.broadcast_to(jnp.concatenate([z_scale, xy_rate])[:, None], (2 * FIELDS, LANES))
    place = (lax.axis_index("gz") // MEMBERS).astype(jnp.int32).reshape(1)
    scale, place = lax.optimization_barrier((scale, place))

    present = fields.reshape(ITEMS, ROWS, WIDTH)
    vel = velocity.reshape(2 * LEVELS, ROWS, WIDTH)
    faces = face_rate
    lowest, highest = pack_part(present, vel)
    half_vel = vel
    south = vel_south = lax.ppermute(highest, "gy", up)
    north = vel_north = lax.ppermute(lowest, "gy", down)
    inner = factor_part(scale, faces)

    near_groups = [[group * MEMBERS + member for member in range(MEMBERS)] for group in range(GROUPS)]
    far_groups = [
        [group * MEMBERS + (row + group // 2 * 8) % MEMBERS for group in range(GROUPS)] for row in range(MEMBERS)
    ]

    def near(chunks):
        return lax.all_to_all(chunks, "gz", 0, 0, tiled=True, axis_index_groups=near_groups)

    def far(chunks):
        return lax.all_to_all(chunks, "gz", 0, 0, tiled=True, axis_index_groups=far_groups)

    factors = top = None
    for step in range(STEPS):
        if step > 0:
            south = lax.ppermute(highest, "gy", up)
            north = lax.ppermute(lowest, "gy", down)
        parts = COLUMNS if factors else COLUMNS + 2
        interior = interior_part(scale, present, half_vel)
        explicit, send = explicit_part(
            parts, place, scale, inner, interior, present, south, north, half_vel, vel_south, vel_north, faces
        )
        got = near(send.reshape(MEMBERS, parts, 8, LANES))
        *made, sources, ports = reduce_part(got, factors, scale)
        factors = factors or tuple(made)
        *made, back = return_part(place, far(ports), sources, factors, top)
        top = made[0] if made else top
        present, *edges = finish_part(
            step + 1 < STEPS, place, inner, explicit, near(back).reshape(MEMBERS * COLUMNS * 8, LANES)
        )
        if edges:
            lowest, highest = edges
    return present.reshape(fields.shape)


def solution(mesh):
    in_specs = (P(None, "gz", "gy", None), P(None, "gz", "gy", None), P("gz", "gy", None), P(), P())
    out_specs = P(None, "gz", "gy", None)
    return jax.shard_map(
        on_device, mesh=mesh, in_specs=in_specs, out_specs=out_specs, check_vma=False
    )
```

```python
import functools

import jax
import jax.numpy as jnp
from jax import lax
from jax.experimental import pallas as pl
from jax.experimental.pallas import tpu as pltpu
from jax.sharding import PartitionSpec as P

STEPS = 2
FIELDS = 4
LEVELS = 4
ITEMS = FIELDS * LEVELS
ROWS = 16
WIDTH = 512
GROUPS = 4
MEMBERS = 16
PAIRS = MEMBERS // 2
FACTORS = 7
LANES = 128
COLUMNS = WIDTH // LANES
TILE = (COLUMNS, 8, LANES)


def columns():
    return [slice(column * LANES, column * LANES + LANES) for column in range(COLUMNS)]


def inner_pivots(rates):
    hold = 1.0 + rates[0]
    inverse = []
    for level in range(LEVELS - 1):
        once = 1.0 / (hold + rates[level + 1])
        inverse.append(once)
        hold = 1.0 + rates[level + 1] * hold * once
    return inverse


def inner_factors(rates):
    inverse = inner_pivots(rates)
    return [*inverse, rates[1] * inverse[0], rates[2] * inverse[1], rates[0], rates[3]]


def solve_inner(source, factors):
    second = source[1] + factors[3] * source[0]
    third = (source[2] + factors[4] * second) * factors[2]
    second = second * factors[1] + factors[4] * third
    return source[0] * factors[0] + factors[3] * second, second, third


def pack_kernel(present_ref, vel_ref, low_ref, high_ref):
    low_ref[0:ITEMS] = present_ref[:, 0:2, :]
    high_ref[0:ITEMS] = present_ref[:, ROWS - 2 : ROWS, :]
    for item in range(2 * LEVELS):
        low_ref[ITEMS + item // 2, item % 2 : item % 2 + 1, :] = vel_ref[item, 0:1, :]
        high_ref[ITEMS + item // 2, item % 2 : item % 2 + 1, :] = vel_ref[item, ROWS - 1 : ROWS, :]


def factor_kernel(scale_ref, face_ref, factor_ref):
    for tile in range(ROWS // 8):
        rows = slice(tile * 8, tile * 8 + 8)
        for lanes in columns():
            faces = [face_ref[level, rows, lanes] for level in range(LEVELS)]
            for field in range(FIELDS):
                scale = jnp.broadcast_to(scale_ref[field : field + 1, :], (8, LANES))
                for item, value in enumerate(inner_factors([scale * face for face in faces])):
                    factor_ref[item, field, rows, lanes] = value


def turned_tile(place_ref, tile):
    return jnp.where(place_ref[0] >= GROUPS // 2, 1 - tile, tile)


def places(tile, parts, line):
    for column in range(COLUMNS):
        start = column * 8 + line if line < 8 else face_line(column, line - 8)
        yield pl.ds(tile * (64 * parts) + start, 8, stride=8 * parts)


def face_line(column, level):
    return (COLUMNS + column // 2) * 8 + column % 2 * LEVELS + level


def along_x(middle, last, begin):
    ahead = [pltpu.roll(value, LANES - 1, 1) for value in middle]
    behind = [pltpu.roll(value, 1, 1) for value in middle]
    for column in range(COLUMNS):
        eastern = jnp.where(last, ahead[(column + 1) % COLUMNS], ahead[column])
        western = jnp.where(begin, behind[column - 1], behind[column])
        yield eastern, western


def tendency(middle, eastern, western, north, south, half_x, half_y, spread):
    return spread * (eastern + western + north + south - 4.0 * middle) - (
        half_x * (eastern - western) + half_y * (north - south)
    )


def edge_lanes():
    lane = lax.broadcasted_iota(jnp.int32, (8, LANES), 1)
    return lane == LANES - 1, lane == 0


def spread_of(scale_ref, field):
    return jnp.broadcast_to(scale_ref[FIELDS + field : FIELDS + field + 1, :], (8, LANES))


ORDER = [field * LEVELS + level for level in range(LEVELS) for field in range(FIELDS)]


def interior_kernel(scale_ref, present_ref, vel_ref, explicit_ref, wide_ref, sectioned_ref):
    last, begin = edge_lanes()

    def section(item, tile):
        field, level = divmod(item, LEVELS)
        rows, at = slice(tile * 8, tile * 8 + 8), tile * 8 + 8
        middle = [present_ref[item, rows, lanes] for lanes in columns()]
        for column, (eastern, western) in enumerate(along_x(middle, last, begin)):
            lanes = slice(column * LANES, column * LANES + LANES)
            sectioned_ref[item, column, at : at + 8, :] = middle[column] + tendency(
                middle[column],
                eastern,
                western,
                wide_ref[item, column, at + 1 : at + 9, :],
                wide_ref[item, column, at - 1 : at + 7, :],
                0.5 * vel_ref[level, rows, lanes],
                0.5 * vel_ref[LEVELS + level, rows, lanes],
                spread_of(scale_ref, field),
            )

    def average(item, tile):
        field, level = divmod(item, LEVELS)
        rows, at = slice(tile * 8, tile * 8 + 8), tile * 8 + 8
        middle = [sectioned_ref[item, column, at : at + 8, :] for column in range(COLUMNS)]
        for column, (eastern, western) in enumerate(along_x(middle, last, begin)):
            lanes = slice(column * LANES, column * LANES + LANES)
            change = tendency(
                middle[column],
                eastern,
                western,
                sectioned_ref[item, column, at + 1 : at + 9, :],
                sectioned_ref[item, column, at - 1 : at + 7, :],
                0.5 * vel_ref[level, rows, lanes],
                0.5 * vel_ref[LEVELS + level, rows, lanes],
                spread_of(scale_ref, field),
            )
            explicit_ref[item, rows, lanes] = 0.5 * (present_ref[item, rows, lanes] + (middle[column] + change))

    for item in range(ITEMS):
        for column, lanes in enumerate(columns()):
            wide_ref[item, column, 8:24, :] = present_ref[item, :, lanes]
    for turn in range(ITEMS + 1):
        for tile in range(ROWS // 8):
            if turn < ITEMS:
                section(ORDER[turn], tile)
            if turn > 0:
                average(ORDER[turn - 1], tile)


def strip_tiles(strip_ref, item, column, low):
    lines = [strip_ref[item, column, at : at + 8, :] for at in range(5)]
    return [jnp.where(low, lines[at], lines[at + 2]) for at in range(3)]


def explicit_kernel(parts, place_ref, scale_ref, factor_ref, inner_ref, present_ref, south_ref, north_ref, vel_ref,
                    vel_south_ref, vel_north_ref, face_ref, explicit_ref, send_ref, strip_ref, vel_strip_ref,
                    vel_tile_ref, sectioned_ref):
    last, begin = edge_lanes()
    low = lax.broadcasted_iota(jnp.int32, (8, LANES), 0) < 4
    for column, lanes in enumerate(columns()):
        for item in range(2 * LEVELS):
            row = slice(item % 2, item % 2 + 1)
            vel_strip_ref[item, column, 1:2, :] = 0.5 * vel_south_ref[ITEMS + item // 2, row, lanes]
            vel_strip_ref[item, column, 2:6, :] = 0.5 * vel_ref[item, 0:4, lanes]
            vel_strip_ref[item, column, 6:10, :] = 0.5 * vel_ref[item, ROWS - 4 : ROWS, lanes]
            vel_strip_ref[item, column, 10:11, :] = 0.5 * vel_north_ref[ITEMS + item // 2, row, lanes]
            _, near, far = strip_tiles(vel_strip_ref, item, column, low)
            vel_tile_ref[0, item, column] = near
            vel_tile_ref[1, item, column] = far
        for item in range(ITEMS):
            strip_ref[item, column, 0:2, :] = south_ref[item, :, lanes]
            strip_ref[item, column, 2:6, :] = present_ref[item, 0:4, lanes]
            strip_ref[item, column, 6:10, :] = present_ref[item, ROWS - 4 : ROWS, lanes]
            strip_ref[item, column, 10:12, :] = north_ref[item, :, lanes]

    def section(item):
        field, level = divmod(item, LEVELS)
        tiles = [strip_tiles(strip_ref, item, column, low) for column in range(COLUMNS)]
        middle = [tile[1] for tile in tiles]
        for column, (eastern, western) in enumerate(along_x(middle, last, begin)):
            sectioned_ref[item, column, 0:8, :] = middle[column] + tendency(
                middle[column],
                eastern,
                western,
                tiles[column][2],
                tiles[column][0],
                vel_tile_ref[0, level, column],
                vel_tile_ref[0, LEVELS + level, column],
                spread_of(scale_ref, field),
            )

    def average(item):
        field, level = divmod(item, LEVELS)
        middle = [sectioned_ref[item, column, 1:9, :] for column in range(COLUMNS)]
        for column, (eastern, western) in enumerate(along_x(middle, last, begin)):
            lanes = slice(column * LANES, column * LANES + LANES)
            change = tendency(
                middle[column],
                eastern,
                western,
                sectioned_ref[item, column, 2:10, :],
                sectioned_ref[item, column, 0:8, :],
                vel_tile_ref[1, level, column],
                vel_tile_ref[1, LEVELS + level, column],
                spread_of(scale_ref, field),
            )
            here = jnp.where(low, strip_ref[item, column, 2:10, :], strip_ref[item, column, 4:12, :])
            value = 0.5 * (here + (middle[column] + change))
            explicit_ref[item, 0:2, lanes] = value[0:2]
            explicit_ref[item, ROWS - 2 : ROWS, lanes] = value[4:6]

    for item in range(ITEMS):
        explicit_ref[item, 2 : ROWS - 2, :] = inner_ref[item, 2 : ROWS - 2, :]
    for turn in range(ITEMS + 1):
        if turn < ITEMS:
            section(ORDER[turn])
        if turn > 0:
            average(ORDER[turn - 1])
    for tile in range(ROWS // 8):
        rows = slice(tile * 8, tile * 8 + 8)
        target = turned_tile(place_ref, tile)
        for field in range(FIELDS):
            lines = zip(columns(), places(target, parts, field), places(target, parts, FIELDS + field), strict=True)
            for lanes, own, under in lines:
                factors = [factor_ref[item, field, rows, lanes] for item in range(FACTORS)]
                source = [explicit_ref[field * LEVELS + level, rows, lanes] for level in range(LEVELS)]
                first, _, third = solve_inner(source, factors)
                send_ref[own, :] = source[3] + factors[6] * third
                send_ref[under, :] = factors[5] * first
        if parts > COLUMNS:
            for level in range(LEVELS):
                for lanes, line in zip(columns(), places(target, parts, 8 + level), strict=True):
                    send_ref[line, :] = face_ref[level, rows, lanes]


def swap(value):
    return pltpu.roll(value, 4, 1)


def lower_half():
    return lax.broadcasted_iota(jnp.int32, TILE, 1) < 4


def pair_sources(got_ref, low):
    def side(block):
        return got_ref[block, 0:COLUMNS] + swap(got_ref[block + 1, 0:COLUMNS])

    return [jnp.where(low, side(step), swap(side(MEMBERS - 2 - step))) for step in range(PAIRS)]


def outer_source(got_ref, low):
    return jnp.where(low, swap(got_ref[0, 0:COLUMNS]), swap(got_ref[MEMBERS - 1, 0:COLUMNS]))


def eliminate(sources, gain_ref, center):
    value = sources[0]
    kept = [value]
    for step in range(1, PAIRS - 1):
        value = sources[step] + gain_ref[step - 1] * value
        kept.append(value)
    value = gain_ref[PAIRS - 2] * value
    return kept, (sources[PAIRS - 1] + value + swap(value)) * center


def face_rows(got_ref, block, level):
    rows = []
    for column in range(COLUMNS):
        tile, line = divmod(face_line(column, level), 8)
        rows.append(jnp.broadcast_to(got_ref[block, tile, line : line + 1, :], (8, LANES)))
    return jnp.stack(rows)


def reduce_kernel(first, got_ref, *refs):
    low = lower_half()
    if first:
        scale_ref, weight_ref, gain_ref, edge_ref, source_ref, send_ref = refs
        scale = jnp.concatenate([scale_ref[0:FIELDS, :]] * 2, 0)[None]
        couple, own, under = [], [], []
        for step in range(PAIRS):
            rates = [
                scale
                * jnp.where(
                    low,
                    face_rows(got_ref, step, level),
                    face_rows(got_ref, MEMBERS - 1 - step, level),
                )
                for level in range(LEVELS)
            ]
            part = inner_factors(rates)
            one = jnp.ones(TILE, jnp.float32)
            bottom, _, third = solve_inner([one, one, one], part)
            own.append(1.0 + rates[3] * third)
            under.append(rates[0] * bottom)
            couple.append(rates[0] * part[3] * part[4] * part[2] * rates[3])
        masses = [
            jnp.where(low, own[step] + under[step + 1], own[step + 1] + under[step]) for step in range(PAIRS - 1)
        ]
        last_own, last_under = own[PAIRS - 1], under[PAIRS - 1]
        masses.append(jnp.where(low, last_own + swap(last_under), swap(last_own) + last_under))
        hold = masses[0] + couple[0]
        through = couple[0]
        for step in range(PAIRS - 1):
            inward = couple[step + 1]
            weight = 1.0 / (hold + inward)
            gain = inward * weight
            weight_ref[step] = weight
            gain_ref[step] = gain
            through = through * gain
            hold = hold * gain + (masses[step + 1] if step + 2 < PAIRS else 0.0)
        center = 1.0 / (masses[PAIRS - 1] + hold + swap(hold))
        weight_ref[PAIRS - 1] = center
        edge_ref[...] = couple[0]
        kept, value = eliminate(masses, gain_ref, center)
        for step in reversed(range(PAIRS - 1)):
            value = weight_ref[step] * kept[step] + gain_ref[step] * value
        outer = jnp.where(low, under[0], own[0]) + couple[0] * value
        through = through * swap(through) * center
        for group in range(GROUPS):
            send_ref[group, COLUMNS : 2 * COLUMNS] = outer
            for column in range(0, COLUMNS, 2):
                pair = jnp.where(low[0], through[column], through[column + 1])
                send_ref[group, 2 * COLUMNS + column // 2] = pair
    else:
        weight_ref, gain_ref, edge_ref, source_ref, send_ref = refs
    sources = pair_sources(got_ref, low)
    for step in range(PAIRS):
        source_ref[step] = sources[step]
    kept, value = eliminate(sources, gain_ref, weight_ref[PAIRS - 1])
    for step in reversed(range(PAIRS - 1)):
        value = weight_ref[step] * kept[step] + gain_ref[step] * value
    outer = outer_source(got_ref, low) + edge_ref[...] * value
    for group in range(GROUPS):
        send_ref[group, 0:COLUMNS] = outer


def across(parts, low):
    ends = jnp.where(low, swap(parts[0]) + parts[1], parts[3])
    middle = jnp.where(low, swap(parts[1]) + parts[2], parts[2] + swap(parts[3]))
    return ends, middle


def return_kernel(first, place_ref, got_ref, source_ref, weight_ref, gain_ref, edge_ref, *refs):
    low = lower_half()
    if first:
        top_ref, back_ref = refs
        ends, middle = across([got_ref[group, COLUMNS : 2 * COLUMNS] for group in range(GROUPS)], low)
        through = []
        for group in range(GROUPS):
            pairs = got_ref[group, 2 * COLUMNS : 2 * COLUMNS + COLUMNS // 2]
            turned = swap(pairs)
            tiles = [jnp.where(low[0], one, other) for pair in zip(pairs, turned) for one, other in (pair, pair[::-1])]
            through.append(jnp.stack(tiles))
        hold = ends + jnp.where(low, through[0], 0.0)
        inward = jnp.where(low, through[1], through[3])
        weight = 1.0 / (hold + inward)
        gain = inward * weight
        hold = middle + hold * gain
        other = swap(hold)
        inverse = 1.0 / (hold * other + through[2] * (hold + other))
        mine, cross = (other + through[2]) * inverse, through[2] * inverse
        for item, value in enumerate((weight, gain, mine, cross)):
            top_ref[item] = value
    else:
        top_ref, back_ref = refs
        weight, gain, mine, cross = (top_ref[item] for item in range(4))
    ends, middle = across([got_ref[group, 0:COLUMNS] for group in range(GROUPS)], low)
    inner = middle + gain * ends
    inner = mine * inner + cross * swap(inner)
    ends = weight * ends + gain * inner
    turned = swap(ends)
    place = place_ref[0]
    value = jnp.where(
        place == 0,
        jnp.where(low, 0.0, turned),
        jnp.where(
            place == 1,
            jnp.where(low, ends, swap(inner)),
            jnp.where(place == 2, inner, jnp.where(low, swap(inner), ends)),
        ),
    )
    sources = [source_ref[step] for step in range(PAIRS)]
    sources[0] = sources[0] + edge_ref[...] * value
    kept, center = eliminate(sources, gain_ref, weight_ref[PAIRS - 1])
    solved = [center]
    for step in reversed(range(PAIRS - 1)):
        solved.insert(0, weight_ref[step] * kept[step] + gain_ref[step] * solved[0])
    outer = value
    for step in range(PAIRS):
        turned = swap(solved[step])
        back_ref[step] = jnp.where(low, outer, turned)
        back_ref[MEMBERS - 1 - step] = jnp.where(low, turned, outer)
        outer = solved[step]


def finish_kernel(edges, place_ref, factor_ref, explicit_ref, back_ref, present_ref, *edge_refs):
    for tile in range(ROWS // 8):
        rows = slice(tile * 8, tile * 8 + 8)
        target = turned_tile(place_ref, tile)
        for field in range(FIELDS):
            lines = zip(columns(), places(target, COLUMNS, field), places(target, COLUMNS, FIELDS + field), strict=True)
            for lanes, below, top in lines:
                factors = [factor_ref[item, field, rows, lanes] for item in range(FACTORS)]
                source = [explicit_ref[field * LEVELS + level, rows, lanes] for level in range(LEVELS - 1)]
                top = back_ref[top, :]
                source[0] = source[0] + factors[5] * back_ref[below, :]
                source[2] = source[2] + factors[6] * top
                solved = solve_inner(source, factors) + (top,)
                for level in range(LEVELS):
                    item = field * LEVELS + level
                    present_ref[item, rows, lanes] = solved[level]
                    if edges and tile == 0:
                        edge_refs[0][item, :, lanes] = solved[level][0:2]
                    if edges and tile == 1:
                        edge_refs[1][item, :, lanes] = solved[level][6:8]


VMEM = pl.BlockSpec(memory_space=pltpu.VMEM)
SMEM = pl.BlockSpec(memory_space=pltpu.SMEM)
PARAMS = pltpu.CompilerParams(vmem_limit_bytes=8 << 20)


def struct(*shape):
    return jax.ShapeDtypeStruct(shape, jnp.float32)


def pack_part(present, vel):
    edge = struct(ITEMS + LEVELS, 2, WIDTH)
    return pl.pallas_call(
        pack_kernel,
        out_shape=(edge, edge),
        in_specs=[VMEM, VMEM],
        out_specs=(VMEM,) * 2,
        compiler_params=PARAMS,
        name="pack_part",
    )(present, vel)


def factor_part(scale, faces):
    return pl.pallas_call(
        factor_kernel,
        out_shape=struct(FACTORS, FIELDS, ROWS, WIDTH),
        in_specs=[VMEM, VMEM],
        out_specs=VMEM,
        compiler_params=PARAMS,
        name="factor_part",
    )(scale, faces)


def interior_part(scale, present, vel):
    return pl.pallas_call(
        interior_kernel,
        out_shape=struct(ITEMS, ROWS, WIDTH),
        in_specs=[VMEM] * 3,
        out_specs=VMEM,
        scratch_shapes=[pltpu.VMEM((ITEMS, COLUMNS, 32, LANES), jnp.float32)] * 2,
        compiler_params=PARAMS,
        cost_estimate=pl.CostEstimate(flops=8 << 20, bytes_accessed=3 << 20, transcendentals=0),
        name="interior_part",
    )(scale, present, vel)


def explicit_part(parts, *operands):
    return pl.pallas_call(
        functools.partial(explicit_kernel, parts),
        out_shape=(struct(ITEMS, ROWS, WIDTH), struct(MEMBERS * parts * 8, LANES)),
        in_specs=[SMEM] + [VMEM] * 10,
        out_specs=(VMEM, VMEM),
        scratch_shapes=[
            pltpu.VMEM((ITEMS, COLUMNS, 16, LANES), jnp.float32),
            pltpu.VMEM((2 * LEVELS, COLUMNS, 16, LANES), jnp.float32),
            pltpu.VMEM((2, 2 * LEVELS, COLUMNS, 8, LANES), jnp.float32),
            pltpu.VMEM((ITEMS, COLUMNS, 16, LANES), jnp.float32),
        ],
        compiler_params=PARAMS,
        name="explicit_part",
    )(*operands)


def reduce_part(got, factors=None, scale=None):
    shapes = (struct(PAIRS, *TILE), struct(PAIRS - 1, *TILE), struct(*TILE))
    outs = (struct(PAIRS, *TILE), struct(GROUPS, COLUMNS if factors else 2 * COLUMNS + COLUMNS // 2, 8, LANES))
    if not factors:
        outs = shapes + outs
    return pl.pallas_call(
        functools.partial(reduce_kernel, not factors),
        out_shape=outs,
        in_specs=[VMEM] * (4 if factors else 2),
        out_specs=(VMEM,) * len(outs),
        compiler_params=PARAMS,
        name="reduce_part",
    )(got, *(factors or (scale,)))


def return_part(place, got, sources, factors, top=None):
    outs = (struct(MEMBERS, *TILE),)
    if top is None:
        outs = (struct(4, *TILE),) + outs
    operands = (got, sources) + tuple(factors) + (() if top is None else (top,))
    return pl.pallas_call(
        functools.partial(return_kernel, top is None),
        out_shape=outs,
        in_specs=[SMEM] + [VMEM] * len(operands),
        out_specs=(VMEM,) * len(outs),
        compiler_params=PARAMS,
        name="return_part",
    )(place, *operands)


def finish_part(edges, *operands):
    shapes = [struct(ITEMS, ROWS, WIDTH)]
    if edges:
        shapes += [struct(ITEMS, 2, WIDTH)] * 2
    return pl.pallas_call(
        functools.partial(finish_kernel, edges),
        out_shape=tuple(shapes),
        in_specs=[SMEM] + [VMEM] * 3,
        out_specs=(VMEM,) * len(shapes),
        compiler_params=PARAMS,
        name="finish_part",
    )(*operands)


def on_device(fields, velocity, face_rate, xy_rate, z_scale):
    count = lax.axis_size("gy")
    up = [(i, (i + 1) % count) for i in range(count)]
    down = [(target, source) for source, target in up]
    scale = jnp.broadcast_to(jnp.concatenate([z_scale, xy_rate])[:, None], (2 * FIELDS, LANES))
    place = (lax.axis_index("gz") // MEMBERS).astype(jnp.int32).reshape(1)
    scale, place = lax.optimization_barrier((scale, place))

    present = fields.reshape(ITEMS, ROWS, WIDTH)
    vel = velocity.reshape(2 * LEVELS, ROWS, WIDTH)
    faces = face_rate
    lowest, highest = pack_part(present, vel)
    half_vel = vel
    south = vel_south = lax.ppermute(highest, "gy", up)
    north = vel_north = lax.ppermute(lowest, "gy", down)
    inner = factor_part(scale, faces)

    near_groups = [[group * MEMBERS + member for member in range(MEMBERS)] for group in range(GROUPS)]
    far_groups = [
        [group * MEMBERS + (row + group // 2 * 8) % MEMBERS for group in range(GROUPS)] for row in range(MEMBERS)
    ]

    def near(chunks):
        return lax.all_to_all(chunks, "gz", 0, 0, tiled=True, axis_index_groups=near_groups)

    def far(chunks):
        return lax.all_to_all(chunks, "gz", 0, 0, tiled=True, axis_index_groups=far_groups)

    factors = top = None
    for step in range(STEPS):
        if step > 0:
            south = lax.ppermute(highest, "gy", up)
            north = lax.ppermute(lowest, "gy", down)
        parts = COLUMNS if factors else COLUMNS + 2
        interior = interior_part(scale, present, half_vel)
        explicit, send = explicit_part(
            parts, place, scale, inner, interior, present, south, north, half_vel, vel_south, vel_north, faces
        )
        got = near(send.reshape(MEMBERS, parts, 8, LANES))
        *made, sources, ports = reduce_part(got, factors, scale)
        factors = factors or tuple(made)
        *made, back = return_part(place, far(ports), sources, factors, top)
        top = made[0] if made else top
        present, *edges = finish_part(
            step + 1 < STEPS, place, inner, explicit, near(back).reshape(MEMBERS * COLUMNS * 8, LANES)
        )
        if edges:
            lowest, highest = edges
    return present.reshape(fields.shape)


def solution(mesh):
    in_specs = (P(None, "gz", "gy", None), P(None, "gz", "gy", None), P("gz", "gy", None), P(), P())
    out_specs = P(None, "gz", "gy", None)
    return jax.shard_map(
        on_device, mesh=mesh, in_specs=in_specs, out_specs=out_specs, check_vma=False
    )
```

```python
import functools

import jax
import jax.numpy as jnp
from jax import lax
from jax.experimental import pallas as pl
from jax.experimental.pallas import tpu as pltpu
from jax.sharding import PartitionSpec as P

STEPS = 2
FIELDS = 4
LEVELS = 4
ITEMS = FIELDS * LEVELS
ROWS = 16
WIDTH = 512
GROUPS = 4
MEMBERS = 16
PAIRS = MEMBERS // 2
FACTORS = 7
LANES = 128
COLUMNS = WIDTH // LANES
TILE = (COLUMNS, 8, LANES)


def columns():
    return [slice(column * LANES, column * LANES + LANES) for column in range(COLUMNS)]


def inner_pivots(rates):
    hold = 1.0 + rates[0]
    inverse = []
    for level in range(LEVELS - 1):
        once = 1.0 / (hold + rates[level + 1])
        inverse.append(once)
        hold = 1.0 + rates[level + 1] * hold * once
    return inverse


def inner_factors(rates):
    inverse = inner_pivots(rates)
    return [*inverse, rates[1] * inverse[0], rates[2] * inverse[1], rates[0], rates[3]]


def solve_inner(source, factors):
    second = source[1] + factors[3] * source[0]
    third = (source[2] + factors[4] * second) * factors[2]
    second = second * factors[1] + factors[4] * third
    return source[0] * factors[0] + factors[3] * second, second, third


def pack_kernel(present_ref, vel_ref, low_ref, high_ref):
    low_ref[0:ITEMS] = present_ref[:, 0:2, :]
    high_ref[0:ITEMS] = present_ref[:, ROWS - 2 : ROWS, :]
    for item in range(2 * LEVELS):
        low_ref[ITEMS + item // 2, item % 2 : item % 2 + 1, :] = vel_ref[item, 0:1, :]
        high_ref[ITEMS + item // 2, item % 2 : item % 2 + 1, :] = vel_ref[item, ROWS - 1 : ROWS, :]


def factor_kernel(scale_ref, face_ref, factor_ref):
    for tile in range(ROWS // 8):
        rows = slice(tile * 8, tile * 8 + 8)
        for lanes in columns():
            faces = [face_ref[level, rows, lanes] for level in range(LEVELS)]
            for field in range(FIELDS):
                scale = jnp.broadcast_to(scale_ref[field : field + 1, :], (8, LANES))
                for item, value in enumerate(inner_factors([scale * face for face in faces])):
                    factor_ref[item, field, rows, lanes] = value


def turned_tile(place_ref, tile):
    return jnp.where(place_ref[0] >= GROUPS // 2, 1 - tile, tile)


def places(tile, parts, line):
    for column in range(COLUMNS):
        start = column * 8 + line if line < 8 else face_line(column, line - 8)
        yield pl.ds(tile * (64 * parts) + start, 8, stride=8 * parts)


def face_line(column, level):
    return (COLUMNS + column // 2) * 8 + column % 2 * LEVELS + level


def along_x(middle, last, begin):
    ahead = [pltpu.roll(value, LANES - 1, 1) for value in middle]
    behind = [pltpu.roll(value, 1, 1) for value in middle]
    for column in range(COLUMNS):
        eastern = jnp.where(last, ahead[(column + 1) % COLUMNS], ahead[column])
        western = jnp.where(begin, behind[column - 1], behind[column])
        yield eastern, western


def tendency(middle, eastern, western, north, south, half_x, half_y, spread):
    return spread * (eastern + western + north + south - 4.0 * middle) - (
        half_x * (eastern - western) + half_y * (north - south)
    )


def edge_lanes():
    lane = lax.broadcasted_iota(jnp.int32, (8, LANES), 1)
    return lane == LANES - 1, lane == 0


def spread_of(scale_ref, field):
    return jnp.broadcast_to(scale_ref[FIELDS + field : FIELDS + field + 1, :], (8, LANES))


ORDER = [field * LEVELS + level for level in range(LEVELS) for field in range(FIELDS)]


def interior_kernel(scale_ref, present_ref, vel_ref, explicit_ref, wide_ref, sectioned_ref):
    last, begin = edge_lanes()

    def section(item, tile):
        field, level = divmod(item, LEVELS)
        rows, at = slice(tile * 8, tile * 8 + 8), tile * 8 + 8
        middle = [present_ref[item, rows, lanes] for lanes in columns()]
        for column, (eastern, western) in enumerate(along_x(middle, last, begin)):
            lanes = slice(column * LANES, column * LANES + LANES)
            sectioned_ref[item, column, at : at + 8, :] = middle[column] + tendency(
                middle[column],
                eastern,
                western,
                wide_ref[item, column, at + 1 : at + 9, :],
                wide_ref[item, column, at - 1 : at + 7, :],
                0.5 * vel_ref[level, rows, lanes],
                0.5 * vel_ref[LEVELS + level, rows, lanes],
                spread_of(scale_ref, field),
            )

    def average(item, tile):
        field, level = divmod(item, LEVELS)
        rows, at = slice(tile * 8, tile * 8 + 8), tile * 8 + 8
        middle = [sectioned_ref[item, column, at : at + 8, :] for column in range(COLUMNS)]
        for column, (eastern, western) in enumerate(along_x(middle, last, begin)):
            lanes = slice(column * LANES, column * LANES + LANES)
            change = tendency(
                middle[column],
                eastern,
                western,
                sectioned_ref[item, column, at + 1 : at + 9, :],
                sectioned_ref[item, column, at - 1 : at + 7, :],
                0.5 * vel_ref[level, rows, lanes],
                0.5 * vel_ref[LEVELS + level, rows, lanes],
                spread_of(scale_ref, field),
            )
            explicit_ref[item, rows, lanes] = 0.5 * (present_ref[item, rows, lanes] + (middle[column] + change))

    for item in range(ITEMS):
        for column, lanes in enumerate(columns()):
            wide_ref[item, column, 8:24, :] = present_ref[item, :, lanes]
    for turn in range(ITEMS + 1):
        for tile in range(ROWS // 8):
            if turn < ITEMS:
                section(ORDER[turn], tile)
            if turn > 0:
                average(ORDER[turn - 1], tile)


def strip_tiles(strip_ref, item, column, low):
    lines = [strip_ref[item, column, at : at + 8, :] for at in range(5)]
    return [jnp.where(low, lines[at], lines[at + 2]) for at in range(3)]


def explicit_kernel(parts, place_ref, scale_ref, factor_ref, inner_ref, present_ref, south_ref, north_ref, vel_ref,
                    vel_south_ref, vel_north_ref, face_ref, explicit_ref, send_ref, strip_ref, vel_strip_ref,
                    vel_tile_ref, sectioned_ref):
    last, begin = edge_lanes()
    low = lax.broadcasted_iota(jnp.int32, (8, LANES), 0) < 4
    for column, lanes in enumerate(columns()):
        for item in range(2 * LEVELS):
            row = slice(item % 2, item % 2 + 1)
            vel_strip_ref[item, column, 1:2, :] = 0.5 * vel_south_ref[ITEMS + item // 2, row, lanes]
            vel_strip_ref[item, column, 2:6, :] = 0.5 * vel_ref[item, 0:4, lanes]
            vel_strip_ref[item, column, 6:10, :] = 0.5 * vel_ref[item, ROWS - 4 : ROWS, lanes]
            vel_strip_ref[item, column, 10:11, :] = 0.5 * vel_north_ref[ITEMS + item // 2, row, lanes]
            _, near, far = strip_tiles(vel_strip_ref, item, column, low)
            vel_tile_ref[0, item, column] = near
            vel_tile_ref[1, item, column] = far
        for item in range(ITEMS):
            strip_ref[item, column, 0:2, :] = south_ref[item, :, lanes]
            strip_ref[item, column, 2:6, :] = present_ref[item, 0:4, lanes]
            strip_ref[item, column, 6:10, :] = present_ref[item, ROWS - 4 : ROWS, lanes]
            strip_ref[item, column, 10:12, :] = north_ref[item, :, lanes]

    def section(item):
        field, level = divmod(item, LEVELS)
        tiles = [strip_tiles(strip_ref, item, column, low) for column in range(COLUMNS)]
        middle = [tile[1] for tile in tiles]
        for column, (eastern, western) in enumerate(along_x(middle, last, begin)):
            sectioned_ref[item, column, 0:8, :] = middle[column] + tendency(
                middle[column],
                eastern,
                western,
                tiles[column][2],
                tiles[column][0],
                vel_tile_ref[0, level, column],
                vel_tile_ref[0, LEVELS + level, column],
                spread_of(scale_ref, field),
            )

    def average(item):
        field, level = divmod(item, LEVELS)
        middle = [sectioned_ref[item, column, 1:9, :] for column in range(COLUMNS)]
        for column, (eastern, western) in enumerate(along_x(middle, last, begin)):
            lanes = slice(column * LANES, column * LANES + LANES)
            change = tendency(
                middle[column],
                eastern,
                western,
                sectioned_ref[item, column, 2:10, :],
                sectioned_ref[item, column, 0:8, :],
                vel_tile_ref[1, level, column],
                vel_tile_ref[1, LEVELS + level, column],
                spread_of(scale_ref, field),
            )
            here = jnp.where(low, strip_ref[item, column, 2:10, :], strip_ref[item, column, 4:12, :])
            value = 0.5 * (here + (middle[column] + change))
            explicit_ref[item, 0:2, lanes] = value[0:2]
            explicit_ref[item, ROWS - 2 : ROWS, lanes] = value[4:6]

    for item in range(ITEMS):
        explicit_ref[item, 2 : ROWS - 2, :] = inner_ref[item, 2 : ROWS - 2, :]
    for turn in range(ITEMS + 1):
        if turn < ITEMS:
            section(ORDER[turn])
        if turn > 0:
            average(ORDER[turn - 1])
    for tile in range(ROWS // 8):
        rows = slice(tile * 8, tile * 8 + 8)
        target = turned_tile(place_ref, tile)
        for field in range(FIELDS):
            lines = zip(columns(), places(target, parts, field), places(target, parts, FIELDS + field), strict=True)
            for lanes, own, under in lines:
                factors = [factor_ref[item, field, rows, lanes] for item in range(FACTORS)]
                source = [explicit_ref[field * LEVELS + level, rows, lanes] for level in range(LEVELS)]
                first, _, third = solve_inner(source, factors)
                send_ref[own, :] = source[3] + factors[6] * third
                send_ref[under, :] = factors[5] * first
        if parts > COLUMNS:
            for level in range(LEVELS):
                for lanes, line in zip(columns(), places(target, parts, 8 + level), strict=True):
                    send_ref[line, :] = face_ref[level, rows, lanes]


def swap(value):
    return pltpu.roll(value, 4, 1)


def lower_half():
    return lax.broadcasted_iota(jnp.int32, TILE, 1) < 4


def pair_sources(got_ref, low):
    def side(block):
        return got_ref[block, 0:COLUMNS] + swap(got_ref[block + 1, 0:COLUMNS])

    return [jnp.where(low, side(step), swap(side(MEMBERS - 2 - step))) for step in range(PAIRS)]


def outer_source(got_ref, low):
    return jnp.where(low, swap(got_ref[0, 0:COLUMNS]), swap(got_ref[MEMBERS - 1, 0:COLUMNS]))


def eliminate(sources, gain_ref, center):
    value = sources[0]
    kept = [value]
    for step in range(1, PAIRS - 1):
        value = sources[step] + gain_ref[step - 1] * value
        kept.append(value)
    value = gain_ref[PAIRS - 2] * value
    return kept, (sources[PAIRS - 1] + value + swap(value)) * center


def face_rows(got_ref, block, level):
    rows = []
    for column in range(COLUMNS):
        tile, line = divmod(face_line(column, level), 8)
        rows.append(jnp.broadcast_to(got_ref[block, tile, line : line + 1, :], (8, LANES)))
    return jnp.stack(rows)


def reduce_kernel(first, got_ref, *refs):
    low = lower_half()
    if first:
        scale_ref, weight_ref, gain_ref, edge_ref, source_ref, send_ref = refs
        scale = jnp.concatenate([scale_ref[0:FIELDS, :]] * 2, 0)[None]
        couple, own, under = [], [], []
        for step in range(PAIRS):
            rates = [
                scale
                * jnp.where(
                    low,
                    face_rows(got_ref, step, level),
                    face_rows(got_ref, MEMBERS - 1 - step, level),
                )
                for level in range(LEVELS)
            ]
            part = inner_factors(rates)
            one = jnp.ones(TILE, jnp.float32)
            bottom, _, third = solve_inner([one, one, one], part)
            own.append(1.0 + rates[3] * third)
            under.append(rates[0] * bottom)
            couple.append(rates[0] * part[3] * part[4] * part[2] * rates[3])
        masses = [
            jnp.where(low, own[step] + under[step + 1], own[step + 1] + under[step]) for step in range(PAIRS - 1)
        ]
        last_own, last_under = own[PAIRS - 1], under[PAIRS - 1]
        masses.append(jnp.where(low, last_own + swap(last_under), swap(last_own) + last_under))
        hold = masses[0] + couple[0]
        through = couple[0]
        for step in range(PAIRS - 1):
            inward = couple[step + 1]
            weight = 1.0 / (hold + inward)
            gain = inward * weight
            weight_ref[step] = weight
            gain_ref[step] = gain
            through = through * gain
            hold = hold * gain + (masses[step + 1] if step + 2 < PAIRS else 0.0)
        center = 1.0 / (masses[PAIRS - 1] + hold + swap(hold))
        weight_ref[PAIRS - 1] = center
        edge_ref[...] = couple[0]
        kept, value = eliminate(masses, gain_ref, center)
        for step in reversed(range(PAIRS - 1)):
            value = weight_ref[step] * kept[step] + gain_ref[step] * value
        outer = jnp.where(low, under[0], own[0]) + couple[0] * value
        through = through * swap(through) * center
        for group in range(GROUPS):
            send_ref[group, COLUMNS : 2 * COLUMNS] = outer
            for item, pair in enumerate(pack_pairs(through, low)):
                send_ref[group, 2 * COLUMNS + item] = pair
    else:
        weight_ref, gain_ref, edge_ref, top_ref, source_ref, send_ref, port_ref = refs
    sources = pair_sources(got_ref, low)
    for step in range(PAIRS):
        source_ref[step] = sources[step]
    kept, value = eliminate(sources, gain_ref, weight_ref[PAIRS - 1])
    for step in reversed(range(PAIRS - 1)):
        value = weight_ref[step] * kept[step] + gain_ref[step] * value
    outer = outer_source(got_ref, low) + edge_ref[...] * value
    if first:
        for group in range(GROUPS):
            send_ref[group, 0:COLUMNS] = outer
    else:
        port_ref[...] = outer
        for group in range(GROUPS):
            part = outer * top_ref[group]
            for item, pair in enumerate(pack_pairs(part + swap(part), low)):
                send_ref[group, item] = pair


def pack_pairs(value, low):
    return [jnp.where(low[0], value[column], value[column + 1]) for column in range(0, COLUMNS, 2)]


def unpack_pairs(pairs, low):
    turned = swap(pairs)
    tiles = [jnp.where(low[0], one, other) for pair in zip(pairs, turned) for one, other in (pair, pair[::-1])]
    return jnp.stack(tiles)


def port_weights(parts, through, place, low):
    masses = []
    for group in range(GROUPS):
        mass = jnp.where(low, swap(parts[group]), parts[group])
        if group + 1 < GROUPS:
            mass = mass + jnp.where(low, parts[group + 1], swap(parts[group + 1]))
        masses.append(mass)
    under, gain = [masses[0] + through[0]], []
    for group in range(GROUPS - 1):
        gain.append(through[group + 1] / (under[group] + through[group + 1]))
        under.append(masses[group + 1] + under[group] * gain[group])
    over, rise = [masses[GROUPS - 1]], []
    for group in reversed(range(1, GROUPS)):
        rise.insert(0, through[group] / (over[0] + through[group]))
        over.insert(0, masses[group - 1] + over[0] * rise[0])
    rise.insert(0, None)
    one, zero = jnp.ones(TILE, jnp.float32), jnp.zeros(TILE, jnp.float32)
    weights = [zero] * GROUPS
    own = cross = zero
    for mine in range(GROUPS):
        here = place == mine
        for group in range(GROUPS):
            product = one
            for between in range(mine, group - 1):
                product = product * gain[between]
            for between in range(group + 1, mine):
                product = product * rise[between]
            if group > mine:
                tile = jnp.where(low, product * gain[mine - 1] if mine else zero, product)
            elif group < mine:
                tile = jnp.where(low, product, product * rise[mine])
            else:
                continue
            weights[group] = jnp.where(here, tile, weights[group])
        if mine:
            low_hold, high_hold, link = under[mine - 1], over[mine], through[mine]
            inverse = 1.0 / (low_hold * high_hold + link * (low_hold + high_hold))
            own = jnp.where(here, (jnp.where(low, high_hold, low_hold) + link) * inverse, own)
            cross = jnp.where(here, link * inverse, cross)
        else:
            own = jnp.where(here, jnp.where(low, zero, 1.0 / (over[0] + through[0])), own)
    return *weights, own, cross


def across(parts, low):
    ends = jnp.where(low, swap(parts[0]) + parts[1], parts[3])
    middle = jnp.where(low, swap(parts[1]) + parts[2], parts[2] + swap(parts[3]))
    return ends, middle


def return_kernel(first, place_ref, got_ref, source_ref, weight_ref, gain_ref, edge_ref, *refs):
    low = lower_half()
    place = place_ref[0]
    if first:
        top_ref, back_ref = refs
        parts = [got_ref[group, COLUMNS : 2 * COLUMNS] for group in range(GROUPS)]
        through = [
            unpack_pairs(got_ref[group, 2 * COLUMNS : 2 * COLUMNS + COLUMNS // 2], low) for group in range(GROUPS)
        ]
        for item, value in enumerate(port_weights(parts, through, place, low)):
            top_ref[item] = value
        ends, middle = across(parts, low)
        hold = ends + jnp.where(low, through[0], 0.0)
        inward = jnp.where(low, through[1], through[3])
        weight = 1.0 / (hold + inward)
        gain = inward * weight
        hold = middle + hold * gain
        other = swap(hold)
        inverse = 1.0 / (hold * other + through[2] * (hold + other))
        mine, cross = (other + through[2]) * inverse, through[2] * inverse
        ends, middle = across([got_ref[group, 0:COLUMNS] for group in range(GROUPS)], low)
        inner = middle + gain * ends
        inner = mine * inner + cross * swap(inner)
        ends = weight * ends + gain * inner
        turned = swap(ends)
        value = jnp.where(
            place == 0,
            jnp.where(low, 0.0, turned),
            jnp.where(
                place == 1,
                jnp.where(low, ends, swap(inner)),
                jnp.where(place == 2, inner, jnp.where(low, swap(inner), ends)),
            ),
        )
    else:
        port_ref, top_ref, back_ref = refs
        ports = port_ref[...]
        for group in range(GROUPS):
            below = jnp.where(place > group, 1.0, 0.0)
            above = jnp.where(place < group, 1.0, 0.0)
            ports = ports + jnp.where(low, below, above) * unpack_pairs(got_ref[group], low)
        value = top_ref[GROUPS] * ports + top_ref[GROUPS + 1] * swap(ports)
    sources = [source_ref[step] for step in range(PAIRS)]
    sources[0] = sources[0] + edge_ref[...] * value
    kept, center = eliminate(sources, gain_ref, weight_ref[PAIRS - 1])
    solved = [center]
    for step in reversed(range(PAIRS - 1)):
        solved.insert(0, weight_ref[step] * kept[step] + gain_ref[step] * solved[0])
    outer = value
    for step in range(PAIRS):
        turned = swap(solved[step])
        back_ref[step] = jnp.where(low, outer, turned)
        back_ref[MEMBERS - 1 - step] = jnp.where(low, turned, outer)
        outer = solved[step]


def finish_kernel(edges, place_ref, factor_ref, explicit_ref, back_ref, present_ref, *edge_refs):
    for tile in range(ROWS // 8):
        rows = slice(tile * 8, tile * 8 + 8)
        target = turned_tile(place_ref, tile)
        for field in range(FIELDS):
            lines = zip(columns(), places(target, COLUMNS, field), places(target, COLUMNS, FIELDS + field), strict=True)
            for lanes, below, top in lines:
                factors = [factor_ref[item, field, rows, lanes] for item in range(FACTORS)]
                source = [explicit_ref[field * LEVELS + level, rows, lanes] for level in range(LEVELS - 1)]
                top = back_ref[top, :]
                source[0] = source[0] + factors[5] * back_ref[below, :]
                source[2] = source[2] + factors[6] * top
                solved = solve_inner(source, factors) + (top,)
                for level in range(LEVELS):
                    item = field * LEVELS + level
                    present_ref[item, rows, lanes] = solved[level]
                    if edges and tile == 0:
                        edge_refs[0][item, :, lanes] = solved[level][0:2]
                    if edges and tile == 1:
                        edge_refs[1][item, :, lanes] = solved[level][6:8]


VMEM = pl.BlockSpec(memory_space=pltpu.VMEM)
SMEM = pl.BlockSpec(memory_space=pltpu.SMEM)
PARAMS = pltpu.CompilerParams(vmem_limit_bytes=8 << 20)


def struct(*shape):
    return jax.ShapeDtypeStruct(shape, jnp.float32)


def pack_part(present, vel):
    edge = struct(ITEMS + LEVELS, 2, WIDTH)
    return pl.pallas_call(
        pack_kernel,
        out_shape=(edge, edge),
        in_specs=[VMEM, VMEM],
        out_specs=(VMEM,) * 2,
        compiler_params=PARAMS,
        name="pack_part",
    )(present, vel)


def factor_part(scale, faces):
    return pl.pallas_call(
        factor_kernel,
        out_shape=struct(FACTORS, FIELDS, ROWS, WIDTH),
        in_specs=[VMEM, VMEM],
        out_specs=VMEM,
        compiler_params=PARAMS,
        name="factor_part",
    )(scale, faces)


def interior_part(scale, present, vel):
    return pl.pallas_call(
        interior_kernel,
        out_shape=struct(ITEMS, ROWS, WIDTH),
        in_specs=[VMEM] * 3,
        out_specs=VMEM,
        scratch_shapes=[pltpu.VMEM((ITEMS, COLUMNS, 32, LANES), jnp.float32)] * 2,
        compiler_params=PARAMS,
        cost_estimate=pl.CostEstimate(flops=8 << 20, bytes_accessed=3 << 20, transcendentals=0),
        name="interior_part",
    )(scale, present, vel)


def explicit_part(parts, *operands):
    return pl.pallas_call(
        functools.partial(explicit_kernel, parts),
        out_shape=(struct(ITEMS, ROWS, WIDTH), struct(MEMBERS * parts * 8, LANES)),
        in_specs=[SMEM] + [VMEM] * 10,
        out_specs=(VMEM, VMEM),
        scratch_shapes=[
            pltpu.VMEM((ITEMS, COLUMNS, 16, LANES), jnp.float32),
            pltpu.VMEM((2 * LEVELS, COLUMNS, 16, LANES), jnp.float32),
            pltpu.VMEM((2, 2 * LEVELS, COLUMNS, 8, LANES), jnp.float32),
            pltpu.VMEM((ITEMS, COLUMNS, 16, LANES), jnp.float32),
        ],
        compiler_params=PARAMS,
        name="explicit_part",
    )(*operands)


def reduce_part(got, factors=None, top=None, scale=None):
    first = not factors
    tiles = 2 * COLUMNS + COLUMNS // 2 if first else COLUMNS // 2
    outs = (struct(PAIRS, *TILE), struct(GROUPS, tiles, 8, LANES))
    if first:
        outs = (struct(PAIRS, *TILE), struct(PAIRS - 1, *TILE), struct(*TILE)) + outs
    else:
        outs += (struct(*TILE),)
    operands = (got, scale) if first else (got, *factors, top)
    return pl.pallas_call(
        functools.partial(reduce_kernel, first),
        out_shape=outs,
        in_specs=[VMEM] * len(operands),
        out_specs=(VMEM,) * len(outs),
        compiler_params=PARAMS,
        name="reduce_part",
    )(*operands)


def return_part(place, got, sources, factors, *more):
    first = not more
    outs = (struct(MEMBERS, *TILE),)
    if first:
        outs = (struct(GROUPS + 2, *TILE),) + outs
    operands = (got, sources, *factors, *more)
    return pl.pallas_call(
        functools.partial(return_kernel, first),
        out_shape=outs,
        in_specs=[SMEM] + [VMEM] * len(operands),
        out_specs=(VMEM,) * len(outs),
        compiler_params=PARAMS,
        name="return_part",
    )(place, *operands)


def finish_part(edges, *operands):
    shapes = [struct(ITEMS, ROWS, WIDTH)]
    if edges:
        shapes += [struct(ITEMS, 2, WIDTH)] * 2
    return pl.pallas_call(
        functools.partial(finish_kernel, edges),
        out_shape=tuple(shapes),
        in_specs=[SMEM] + [VMEM] * 3,
        out_specs=(VMEM,) * len(shapes),
        compiler_params=PARAMS,
        name="finish_part",
    )(*operands)


def on_device(fields, velocity, face_rate, xy_rate, z_scale):
    count = lax.axis_size("gy")
    up = [(i, (i + 1) % count) for i in range(count)]
    down = [(target, source) for source, target in up]
    scale = jnp.broadcast_to(jnp.concatenate([z_scale, xy_rate])[:, None], (2 * FIELDS, LANES))
    place = (lax.axis_index("gz") // MEMBERS).astype(jnp.int32).reshape(1)
    scale, place = lax.optimization_barrier((scale, place))

    present = fields.reshape(ITEMS, ROWS, WIDTH)
    vel = velocity.reshape(2 * LEVELS, ROWS, WIDTH)
    faces = face_rate
    lowest, highest = pack_part(present, vel)
    half_vel = vel
    south = vel_south = lax.ppermute(highest, "gy", up)
    north = vel_north = lax.ppermute(lowest, "gy", down)
    inner = factor_part(scale, faces)

    near_groups = [[group * MEMBERS + member for member in range(MEMBERS)] for group in range(GROUPS)]
    far_groups = [
        [group * MEMBERS + (row + group // 2 * 8) % MEMBERS for group in range(GROUPS)] for row in range(MEMBERS)
    ]

    def near(chunks):
        return lax.all_to_all(chunks, "gz", 0, 0, tiled=True, axis_index_groups=near_groups)

    def far(chunks):
        return lax.all_to_all(chunks, "gz", 0, 0, tiled=True, axis_index_groups=far_groups)

    factors = top = None
    for step in range(STEPS):
        if step > 0:
            south = lax.ppermute(highest, "gy", up)
            north = lax.ppermute(lowest, "gy", down)
        parts = COLUMNS if factors else COLUMNS + 2
        interior = interior_part(scale, present, half_vel)
        explicit, send = explicit_part(
            parts, place, scale, inner, interior, present, south, north, half_vel, vel_south, vel_north, faces
        )
        got = near(send.reshape(MEMBERS, parts, 8, LANES))
        if step == 0:
            *factors, sources, send = reduce_part(got, scale=scale)
            top, back = return_part(place, far(send), sources, factors)
        else:
            sources, send, ports = reduce_part(got, factors, top)
            (back,) = return_part(place, far(send), sources, factors, ports, top)
        present, *edges = finish_part(
            step + 1 < STEPS, place, inner, explicit, near(back).reshape(MEMBERS * COLUMNS * 8, LANES)
        )
        if edges:
            lowest, highest = edges
    return present.reshape(fields.shape)


def solution(mesh):
    in_specs = (P(None, "gz", "gy", None), P(None, "gz", "gy", None), P("gz", "gy", None), P(), P())
    out_specs = P(None, "gz", "gy", None)
    return jax.shard_map(
        on_device, mesh=mesh, in_specs=in_specs, out_specs=out_specs, check_vma=False
    )
```

```python
import functools

import jax
import jax.numpy as jnp
from jax import lax
from jax.experimental import pallas as pl
from jax.experimental.pallas import tpu as pltpu
from jax.sharding import PartitionSpec as P

STEPS = 2
FIELDS = 4
LEVELS = 4
ITEMS = FIELDS * LEVELS
ROWS = 16
WIDTH = 512
GROUPS = 4
MEMBERS = 16
PAIRS = MEMBERS // 2
FACTORS = 7
LANES = 128
COLUMNS = WIDTH // LANES
TILE = (COLUMNS, 8, LANES)


def columns():
    return [slice(column * LANES, column * LANES + LANES) for column in range(COLUMNS)]


def inner_pivots(rates):
    hold = 1.0 + rates[0]
    inverse = []
    for level in range(LEVELS - 1):
        once = 1.0 / (hold + rates[level + 1])
        inverse.append(once)
        hold = 1.0 + rates[level + 1] * hold * once
    return inverse


def inner_factors(rates):
    inverse = inner_pivots(rates)
    return [*inverse, rates[1] * inverse[0], rates[2] * inverse[1], rates[0], rates[3]]


def solve_inner(source, factors):
    second = source[1] + factors[3] * source[0]
    third = (source[2] + factors[4] * second) * factors[2]
    second = second * factors[1] + factors[4] * third
    return source[0] * factors[0] + factors[3] * second, second, third


def pack_kernel(present_ref, vel_ref, low_ref, high_ref):
    low_ref[0:ITEMS] = present_ref[:, 0:2, :]
    high_ref[0:ITEMS] = present_ref[:, ROWS - 2 : ROWS, :]
    for item in range(2 * LEVELS):
        low_ref[ITEMS + item // 2, item % 2 : item % 2 + 1, :] = vel_ref[item, 0:1, :]
        high_ref[ITEMS + item // 2, item % 2 : item % 2 + 1, :] = vel_ref[item, ROWS - 1 : ROWS, :]


def factor_kernel(scale_ref, face_ref, factor_ref):
    for tile in range(ROWS // 8):
        rows = slice(tile * 8, tile * 8 + 8)
        for lanes in columns():
            faces = [face_ref[level, rows, lanes] for level in range(LEVELS)]
            for field in range(FIELDS):
                scale = jnp.broadcast_to(scale_ref[field : field + 1, :], (8, LANES))
                for item, value in enumerate(inner_factors([scale * face for face in faces])):
                    factor_ref[item, field, rows, lanes] = value


def turned_tile(place_ref, tile):
    return jnp.where(place_ref[0] >= GROUPS // 2, 1 - tile, tile)


def places(tile, parts, line):
    for column in range(COLUMNS):
        start = column * 8 + line if line < 8 else face_line(column, line - 8)
        yield pl.ds(tile * (64 * parts) + start, 8, stride=8 * parts)


def face_line(column, level):
    return (COLUMNS + column // 2) * 8 + column % 2 * LEVELS + level


def along_x(middle, last, begin):
    ahead = [pltpu.roll(value, LANES - 1, 1) for value in middle]
    behind = [pltpu.roll(value, 1, 1) for value in middle]
    for column in range(COLUMNS):
        eastern = jnp.where(last, ahead[(column + 1) % COLUMNS], ahead[column])
        western = jnp.where(begin, behind[column - 1], behind[column])
        yield eastern, western


def tendency(middle, eastern, western, north, south, half_x, half_y, spread):
    return spread * (eastern + western + north + south - 4.0 * middle) - (
        half_x * (eastern - western) + half_y * (north - south)
    )


def edge_lanes():
    lane = lax.broadcasted_iota(jnp.int32, (8, LANES), 1)
    return lane == LANES - 1, lane == 0


def spread_of(scale_ref, field):
    return jnp.broadcast_to(scale_ref[FIELDS + field : FIELDS + field + 1, :], (8, LANES))


ORDER = [field * LEVELS + level for level in range(LEVELS) for field in range(FIELDS)]


def interior_kernel(scale_ref, present_ref, vel_ref, explicit_ref, wide_ref, sectioned_ref):
    last, begin = edge_lanes()

    def section(item, tile):
        field, level = divmod(item, LEVELS)
        rows, at = slice(tile * 8, tile * 8 + 8), tile * 8 + 8
        middle = [present_ref[item, rows, lanes] for lanes in columns()]
        for column, (eastern, western) in enumerate(along_x(middle, last, begin)):
            lanes = slice(column * LANES, column * LANES + LANES)
            sectioned_ref[item, column, at : at + 8, :] = middle[column] + tendency(
                middle[column],
                eastern,
                western,
                wide_ref[item, column, at + 1 : at + 9, :],
                wide_ref[item, column, at - 1 : at + 7, :],
                0.5 * vel_ref[level, rows, lanes],
                0.5 * vel_ref[LEVELS + level, rows, lanes],
                spread_of(scale_ref, field),
            )

    def average(item, tile):
        field, level = divmod(item, LEVELS)
        rows, at = slice(tile * 8, tile * 8 + 8), tile * 8 + 8
        middle = [sectioned_ref[item, column, at : at + 8, :] for column in range(COLUMNS)]
        for column, (eastern, western) in enumerate(along_x(middle, last, begin)):
            lanes = slice(column * LANES, column * LANES + LANES)
            change = tendency(
                middle[column],
                eastern,
                western,
                sectioned_ref[item, column, at + 1 : at + 9, :],
                sectioned_ref[item, column, at - 1 : at + 7, :],
                0.5 * vel_ref[level, rows, lanes],
                0.5 * vel_ref[LEVELS + level, rows, lanes],
                spread_of(scale_ref, field),
            )
            explicit_ref[item, rows, lanes] = 0.5 * (present_ref[item, rows, lanes] + (middle[column] + change))

    for item in range(ITEMS):
        for column, lanes in enumerate(columns()):
            wide_ref[item, column, 8:24, :] = present_ref[item, :, lanes]
    for turn in range(ITEMS + 1):
        for tile in range(ROWS // 8):
            if turn < ITEMS:
                section(ORDER[turn], tile)
            if turn > 0:
                average(ORDER[turn - 1], tile)


def strip_tiles(strip_ref, item, column, low):
    lines = [strip_ref[item, column, at : at + 8, :] for at in range(5)]
    return [jnp.where(low, lines[at], lines[at + 2]) for at in range(3)]


def explicit_kernel(parts, place_ref, scale_ref, factor_ref, inner_ref, present_ref, south_ref, north_ref, vel_ref,
                    vel_south_ref, vel_north_ref, face_ref, explicit_ref, send_ref, strip_ref, vel_strip_ref,
                    vel_tile_ref, sectioned_ref):
    last, begin = edge_lanes()
    low = lax.broadcasted_iota(jnp.int32, (8, LANES), 0) < 4
    for column, lanes in enumerate(columns()):
        for item in range(2 * LEVELS):
            row = slice(item % 2, item % 2 + 1)
            vel_strip_ref[item, column, 1:2, :] = 0.5 * vel_south_ref[ITEMS + item // 2, row, lanes]
            vel_strip_ref[item, column, 2:6, :] = 0.5 * vel_ref[item, 0:4, lanes]
            vel_strip_ref[item, column, 6:10, :] = 0.5 * vel_ref[item, ROWS - 4 : ROWS, lanes]
            vel_strip_ref[item, column, 10:11, :] = 0.5 * vel_north_ref[ITEMS + item // 2, row, lanes]
            _, near, far = strip_tiles(vel_strip_ref, item, column, low)
            vel_tile_ref[0, item, column] = near
            vel_tile_ref[1, item, column] = far
        for item in range(ITEMS):
            strip_ref[item, column, 0:2, :] = south_ref[item, :, lanes]
            strip_ref[item, column, 2:6, :] = present_ref[item, 0:4, lanes]
            strip_ref[item, column, 6:10, :] = present_ref[item, ROWS - 4 : ROWS, lanes]
            strip_ref[item, column, 10:12, :] = north_ref[item, :, lanes]

    def section(item):
        field, level = divmod(item, LEVELS)
        tiles = [strip_tiles(strip_ref, item, column, low) for column in range(COLUMNS)]
        middle = [tile[1] for tile in tiles]
        for column, (eastern, western) in enumerate(along_x(middle, last, begin)):
            sectioned_ref[item, column, 0:8, :] = middle[column] + tendency(
                middle[column],
                eastern,
                western,
                tiles[column][2],
                tiles[column][0],
                vel_tile_ref[0, level, column],
                vel_tile_ref[0, LEVELS + level, column],
                spread_of(scale_ref, field),
            )

    def average(item):
        field, level = divmod(item, LEVELS)
        middle = [sectioned_ref[item, column, 1:9, :] for column in range(COLUMNS)]
        for column, (eastern, western) in enumerate(along_x(middle, last, begin)):
            lanes = slice(column * LANES, column * LANES + LANES)
            change = tendency(
                middle[column],
                eastern,
                western,
                sectioned_ref[item, column, 2:10, :],
                sectioned_ref[item, column, 0:8, :],
                vel_tile_ref[1, level, column],
                vel_tile_ref[1, LEVELS + level, column],
                spread_of(scale_ref, field),
            )
            here = jnp.where(low, strip_ref[item, column, 2:10, :], strip_ref[item, column, 4:12, :])
            value = 0.5 * (here + (middle[column] + change))
            explicit_ref[item, 0:2, lanes] = value[0:2]
            explicit_ref[item, ROWS - 2 : ROWS, lanes] = value[4:6]

    for item in range(ITEMS):
        explicit_ref[item, 2 : ROWS - 2, :] = inner_ref[item, 2 : ROWS - 2, :]
    for turn in range(ITEMS + 1):
        if turn < ITEMS:
            section(ORDER[turn])
        if turn > 0:
            average(ORDER[turn - 1])
    for tile in range(ROWS // 8):
        rows = slice(tile * 8, tile * 8 + 8)
        target = turned_tile(place_ref, tile)
        for field in range(FIELDS):
            lines = zip(columns(), places(target, parts, field), places(target, parts, FIELDS + field), strict=True)
            for lanes, own, under in lines:
                factors = [factor_ref[item, field, rows, lanes] for item in range(FACTORS)]
                source = [explicit_ref[field * LEVELS + level, rows, lanes] for level in range(LEVELS)]
                first, _, third = solve_inner(source, factors)
                send_ref[own, :] = source[3] + factors[6] * third
                send_ref[under, :] = factors[5] * first
        if parts > COLUMNS:
            for level in range(LEVELS):
                for lanes, line in zip(columns(), places(target, parts, 8 + level), strict=True):
                    send_ref[line, :] = face_ref[level, rows, lanes]


def swap(value):
    return pltpu.roll(value, 4, 1)


def lower_half():
    return lax.broadcasted_iota(jnp.int32, TILE, 1) < 4


def pair_sources(got_ref, low):
    def side(block):
        return got_ref[block, 0:COLUMNS] + swap(got_ref[block + 1, 0:COLUMNS])

    return [jnp.where(low, side(step), swap(side(MEMBERS - 2 - step))) for step in range(PAIRS)]


def outer_source(got_ref, low):
    return jnp.where(low, swap(got_ref[0, 0:COLUMNS]), swap(got_ref[MEMBERS - 1, 0:COLUMNS]))


def eliminate(sources, gain_ref, center):
    value = sources[0]
    kept = [value]
    for step in range(1, PAIRS - 1):
        value = sources[step] + gain_ref[step - 1] * value
        kept.append(value)
    value = gain_ref[PAIRS - 2] * value
    return kept, (sources[PAIRS - 1] + value + swap(value)) * center


def face_rows(got_ref, block, level):
    rows = []
    for column in range(COLUMNS):
        tile, line = divmod(face_line(column, level), 8)
        rows.append(jnp.broadcast_to(got_ref[block, tile, line : line + 1, :], (8, LANES)))
    return jnp.stack(rows)


def reduce_kernel(first, got_ref, *refs):
    low = lower_half()
    if first:
        scale_ref, weight_ref, gain_ref, edge_ref, source_ref, send_ref = refs
        scale = jnp.concatenate([scale_ref[0:FIELDS, :]] * 2, 0)[None]
        couple, own, under = [], [], []
        for step in range(PAIRS):
            rates = [
                scale
                * jnp.where(
                    low,
                    face_rows(got_ref, step, level),
                    face_rows(got_ref, MEMBERS - 1 - step, level),
                )
                for level in range(LEVELS)
            ]
            part = inner_factors(rates)
            one = jnp.ones(TILE, jnp.float32)
            bottom, _, third = solve_inner([one, one, one], part)
            own.append(1.0 + rates[3] * third)
            under.append(rates[0] * bottom)
            couple.append(rates[0] * part[3] * part[4] * part[2] * rates[3])
        masses = [
            jnp.where(low, own[step] + under[step + 1], own[step + 1] + under[step]) for step in range(PAIRS - 1)
        ]
        last_own, last_under = own[PAIRS - 1], under[PAIRS - 1]
        masses.append(jnp.where(low, last_own + swap(last_under), swap(last_own) + last_under))
        hold = masses[0] + couple[0]
        through = couple[0]
        for step in range(PAIRS - 1):
            inward = couple[step + 1]
            weight = 1.0 / (hold + inward)
            gain = inward * weight
            weight_ref[step] = weight
            gain_ref[step] = gain
            through = through * gain
            hold = hold * gain + (masses[step + 1] if step + 2 < PAIRS else 0.0)
        center = 1.0 / (masses[PAIRS - 1] + hold + swap(hold))
        weight_ref[PAIRS - 1] = center
        edge_ref[...] = couple[0]
        kept, value = eliminate(masses, gain_ref, center)
        for step in reversed(range(PAIRS - 1)):
            value = weight_ref[step] * kept[step] + gain_ref[step] * value
        outer = jnp.where(low, under[0], own[0]) + couple[0] * value
        through = through * swap(through) * center
        for group in range(GROUPS):
            send_ref[group, COLUMNS : 2 * COLUMNS] = outer
            for item, pair in enumerate(pack_pairs(through, low)):
                send_ref[group, 2 * COLUMNS + item] = pair
    else:
        weight_ref, gain_ref, edge_ref, top_ref, source_ref, send_ref, port_ref = refs
    sources = pair_sources(got_ref, low)
    for step in range(PAIRS):
        source_ref[step] = sources[step]
    kept, value = eliminate(sources, gain_ref, weight_ref[PAIRS - 1])
    for step in reversed(range(PAIRS - 1)):
        value = weight_ref[step] * kept[step] + gain_ref[step] * value
    outer = outer_source(got_ref, low) + edge_ref[...] * value
    if first:
        for group in range(GROUPS):
            send_ref[group, 0:COLUMNS] = outer
    else:
        port_ref[...] = outer
        for group in range(GROUPS):
            part = outer * top_ref[group]
            for item, pair in enumerate(pack_pairs(part + swap(part), low)):
                send_ref[group, item] = pair


def pack_pairs(value, low):
    return [jnp.where(low[0], value[column], value[column + 1]) for column in range(0, COLUMNS, 2)]


def unpack_pairs(pairs, low):
    turned = swap(pairs)
    tiles = [jnp.where(low[0], one, other) for pair in zip(pairs, turned) for one, other in (pair, pair[::-1])]
    return jnp.stack(tiles)


def port_weights(parts, through, place, low):
    masses = []
    for group in range(GROUPS):
        mass = jnp.where(low, swap(parts[group]), parts[group])
        if group + 1 < GROUPS:
            mass = mass + jnp.where(low, parts[group + 1], swap(parts[group + 1]))
        masses.append(mass)
    under, gain = [masses[0] + through[0]], []
    for group in range(GROUPS - 1):
        gain.append(through[group + 1] / (under[group] + through[group + 1]))
        under.append(masses[group + 1] + under[group] * gain[group])
    over, rise = [masses[GROUPS - 1]], []
    for group in reversed(range(1, GROUPS)):
        rise.insert(0, through[group] / (over[0] + through[group]))
        over.insert(0, masses[group - 1] + over[0] * rise[0])
    rise.insert(0, None)
    one, zero = jnp.ones(TILE, jnp.float32), jnp.zeros(TILE, jnp.float32)
    weights = [zero] * GROUPS
    own = cross = zero
    for mine in range(GROUPS):
        here = place == mine
        for group in range(GROUPS):
            product = one
            for between in range(mine, group - 1):
                product = product * gain[between]
            for between in range(group + 1, mine):
                product = product * rise[between]
            if group > mine:
                tile = jnp.where(low, product * gain[mine - 1] if mine else zero, product)
            elif group < mine:
                tile = jnp.where(low, product, product * rise[mine])
            else:
                continue
            weights[group] = jnp.where(here, tile, weights[group])
        if mine:
            low_hold, high_hold, link = under[mine - 1], over[mine], through[mine]
            inverse = 1.0 / (low_hold * high_hold + link * (low_hold + high_hold))
            own = jnp.where(here, (jnp.where(low, high_hold, low_hold) + link) * inverse, own)
            cross = jnp.where(here, link * inverse, cross)
        else:
            own = jnp.where(here, jnp.where(low, zero, 1.0 / (over[0] + through[0])), own)
    return *weights, own, cross


def across(parts, low):
    ends = jnp.where(low, swap(parts[0]) + parts[1], parts[3])
    middle = jnp.where(low, swap(parts[1]) + parts[2], parts[2] + swap(parts[3]))
    return ends, middle


def return_kernel(first, place_ref, got_ref, source_ref, weight_ref, gain_ref, edge_ref, *refs):
    low = lower_half()
    place = place_ref[0]
    if first:
        top_ref, back_ref = refs
        parts = [got_ref[group, COLUMNS : 2 * COLUMNS] for group in range(GROUPS)]
        through = [
            unpack_pairs(got_ref[group, 2 * COLUMNS : 2 * COLUMNS + COLUMNS // 2], low) for group in range(GROUPS)
        ]
        for item, value in enumerate(port_weights(parts, through, place, low)):
            top_ref[item] = value
        ends, middle = across(parts, low)
        hold = ends + jnp.where(low, through[0], 0.0)
        inward = jnp.where(low, through[1], through[3])
        weight = 1.0 / (hold + inward)
        gain = inward * weight
        hold = middle + hold * gain
        other = swap(hold)
        inverse = 1.0 / (hold * other + through[2] * (hold + other))
        mine, cross = (other + through[2]) * inverse, through[2] * inverse
        ends, middle = across([got_ref[group, 0:COLUMNS] for group in range(GROUPS)], low)
        inner = middle + gain * ends
        inner = mine * inner + cross * swap(inner)
        ends = weight * ends + gain * inner
        turned = swap(ends)
        value = jnp.where(
            place == 0,
            jnp.where(low, 0.0, turned),
            jnp.where(
                place == 1,
                jnp.where(low, ends, swap(inner)),
                jnp.where(place == 2, inner, jnp.where(low, swap(inner), ends)),
            ),
        )
    else:
        port_ref, top_ref, back_ref = refs
        ports = port_ref[...]
        for group in range(GROUPS):
            below = jnp.where(place > group, 1.0, 0.0)
            above = jnp.where(place < group, 1.0, 0.0)
            ports = ports + jnp.where(low, below, above) * unpack_pairs(got_ref[group], low)
        value = top_ref[GROUPS] * ports + top_ref[GROUPS + 1] * swap(ports)
    sources = [source_ref[step] for step in range(PAIRS)]
    sources[0] = sources[0] + edge_ref[...] * value
    kept, center = eliminate(sources, gain_ref, weight_ref[PAIRS - 1])
    solved = [center]
    for step in reversed(range(PAIRS - 1)):
        solved.insert(0, weight_ref[step] * kept[step] + gain_ref[step] * solved[0])
    outer = value
    for step in range(PAIRS):
        turned = swap(solved[step])
        back_ref[step] = jnp.where(low, outer, turned)
        back_ref[MEMBERS - 1 - step] = jnp.where(low, turned, outer)
        outer = solved[step]


def finish_field(field, place_ref, factor_ref, explicit_ref, back_ref, present_ref, edge_refs=None):
    for tile in range(ROWS // 8):
        rows = slice(tile * 8, tile * 8 + 8)
        target = turned_tile(place_ref, tile)
        lines = zip(columns(), places(target, COLUMNS, field), places(target, COLUMNS, FIELDS + field), strict=True)
        for lanes, below, top in lines:
            factors = [factor_ref[item, field, rows, lanes] for item in range(FACTORS)]
            source = [explicit_ref[field * LEVELS + level, rows, lanes] for level in range(LEVELS - 1)]
            top = back_ref[top, :]
            source[0] = source[0] + factors[5] * back_ref[below, :]
            source[2] = source[2] + factors[6] * top
            solved = solve_inner(source, factors) + (top,)
            for level in range(LEVELS):
                item = field * LEVELS + level
                present_ref[item, rows, lanes] = solved[level]
                if edge_refs and tile == 0:
                    edge_refs[0][item, :, lanes] = solved[level][0:2]
                if edge_refs and tile == 1:
                    edge_refs[1][item, :, lanes] = solved[level][6:8]


def finish_kernel(place_ref, factor_ref, explicit_ref, back_ref, present_ref, *edge_refs):
    for field in range(FIELDS):
        finish_field(field, place_ref, factor_ref, explicit_ref, back_ref, present_ref, edge_refs)


def output_kernel(place_ref, factor_ref, explicit_ref, back_ref, out_ref, present_ref, sems):
    copies = []
    for field in range(FIELDS):
        finish_field(field, place_ref, factor_ref, explicit_ref, back_ref, present_ref)
        items = pl.ds(field * LEVELS, LEVELS)
        copies.append(pltpu.make_async_copy(present_ref.at[items], out_ref.at[items], sems.at[field]))
        copies[-1].start()
    for copy in copies:
        copy.wait()


VMEM = pl.BlockSpec(memory_space=pltpu.VMEM)
SMEM = pl.BlockSpec(memory_space=pltpu.SMEM)
PARAMS = pltpu.CompilerParams(vmem_limit_bytes=8 << 20)


def struct(*shape):
    return jax.ShapeDtypeStruct(shape, jnp.float32)


def pack_part(present, vel):
    edge = struct(ITEMS + LEVELS, 2, WIDTH)
    return pl.pallas_call(
        pack_kernel,
        out_shape=(edge, edge),
        in_specs=[VMEM, VMEM],
        out_specs=(VMEM,) * 2,
        compiler_params=PARAMS,
        name="pack_part",
    )(present, vel)


def factor_part(scale, faces):
    return pl.pallas_call(
        factor_kernel,
        out_shape=struct(FACTORS, FIELDS, ROWS, WIDTH),
        in_specs=[VMEM, VMEM],
        out_specs=VMEM,
        compiler_params=PARAMS,
        name="factor_part",
    )(scale, faces)


def interior_part(scale, present, vel):
    return pl.pallas_call(
        interior_kernel,
        out_shape=struct(ITEMS, ROWS, WIDTH),
        in_specs=[VMEM] * 3,
        out_specs=VMEM,
        scratch_shapes=[pltpu.VMEM((ITEMS, COLUMNS, 32, LANES), jnp.float32)] * 2,
        compiler_params=PARAMS,
        cost_estimate=pl.CostEstimate(flops=8 << 20, bytes_accessed=3 << 20, transcendentals=0),
        name="interior_part",
    )(scale, present, vel)


def explicit_part(parts, *operands):
    return pl.pallas_call(
        functools.partial(explicit_kernel, parts),
        out_shape=(struct(ITEMS, ROWS, WIDTH), struct(MEMBERS * parts * 8, LANES)),
        in_specs=[SMEM] + [VMEM] * 10,
        out_specs=(VMEM, VMEM),
        scratch_shapes=[
            pltpu.VMEM((ITEMS, COLUMNS, 16, LANES), jnp.float32),
            pltpu.VMEM((2 * LEVELS, COLUMNS, 16, LANES), jnp.float32),
            pltpu.VMEM((2, 2 * LEVELS, COLUMNS, 8, LANES), jnp.float32),
            pltpu.VMEM((ITEMS, COLUMNS, 16, LANES), jnp.float32),
        ],
        compiler_params=PARAMS,
        name="explicit_part",
    )(*operands)


def reduce_part(got, factors=None, top=None, scale=None):
    first = not factors
    tiles = 2 * COLUMNS + COLUMNS // 2 if first else COLUMNS // 2
    outs = (struct(PAIRS, *TILE), struct(GROUPS, tiles, 8, LANES))
    if first:
        outs = (struct(PAIRS, *TILE), struct(PAIRS - 1, *TILE), struct(*TILE)) + outs
    else:
        outs += (struct(*TILE),)
    operands = (got, scale) if first else (got, *factors, top)
    return pl.pallas_call(
        functools.partial(reduce_kernel, first),
        out_shape=outs,
        in_specs=[VMEM] * len(operands),
        out_specs=(VMEM,) * len(outs),
        compiler_params=PARAMS,
        name="reduce_part",
    )(*operands)


def return_part(place, got, sources, factors, *more):
    first = not more
    outs = (struct(MEMBERS, *TILE),)
    if first:
        outs = (struct(GROUPS + 2, *TILE),) + outs
    operands = (got, sources, *factors, *more)
    return pl.pallas_call(
        functools.partial(return_kernel, first),
        out_shape=outs,
        in_specs=[SMEM] + [VMEM] * len(operands),
        out_specs=(VMEM,) * len(outs),
        compiler_params=PARAMS,
        name="return_part",
    )(place, *operands)


def finish_part(*operands):
    edge = struct(ITEMS, 2, WIDTH)
    return pl.pallas_call(
        finish_kernel,
        out_shape=(struct(ITEMS, ROWS, WIDTH), edge, edge),
        in_specs=[SMEM] + [VMEM] * 3,
        out_specs=(VMEM,) * 3,
        compiler_params=PARAMS,
        name="finish_part",
    )(*operands)


def output_part(*operands):
    return pl.pallas_call(
        output_kernel,
        out_shape=struct(ITEMS, ROWS, WIDTH),
        in_specs=[SMEM] + [VMEM] * 3,
        out_specs=pl.BlockSpec(memory_space=pl.ANY),
        scratch_shapes=[
            pltpu.VMEM((ITEMS, ROWS, WIDTH), jnp.float32),
            pltpu.SemaphoreType.DMA((FIELDS,)),
        ],
        compiler_params=PARAMS,
        name="output_part",
    )(*operands)


def on_device(fields, velocity, face_rate, xy_rate, z_scale):
    count = lax.axis_size("gy")
    up = [(i, (i + 1) % count) for i in range(count)]
    down = [(target, source) for source, target in up]
    scale = jnp.broadcast_to(jnp.concatenate([z_scale, xy_rate])[:, None], (2 * FIELDS, LANES))
    place = (lax.axis_index("gz") // MEMBERS).astype(jnp.int32).reshape(1)
    scale, place = lax.optimization_barrier((scale, place))

    present = fields.reshape(ITEMS, ROWS, WIDTH)
    vel = velocity.reshape(2 * LEVELS, ROWS, WIDTH)
    faces = face_rate
    lowest, highest = pack_part(present, vel)
    half_vel = vel
    south = vel_south = lax.ppermute(highest, "gy", up)
    north = vel_north = lax.ppermute(lowest, "gy", down)
    inner = factor_part(scale, faces)

    near_groups = [[group * MEMBERS + member for member in range(MEMBERS)] for group in range(GROUPS)]
    far_groups = [
        [group * MEMBERS + (row + group // 2 * 8) % MEMBERS for group in range(GROUPS)] for row in range(MEMBERS)
    ]

    def near(chunks):
        return lax.all_to_all(chunks, "gz", 0, 0, tiled=True, axis_index_groups=near_groups)

    def far(chunks):
        return lax.all_to_all(chunks, "gz", 0, 0, tiled=True, axis_index_groups=far_groups)

    factors = top = None
    for step in range(STEPS):
        if step > 0:
            south = lax.ppermute(highest, "gy", up)
            north = lax.ppermute(lowest, "gy", down)
        parts = COLUMNS if factors else COLUMNS + 2
        interior = interior_part(scale, present, half_vel)
        explicit, send = explicit_part(
            parts, place, scale, inner, interior, present, south, north, half_vel, vel_south, vel_north, faces
        )
        got = near(send.reshape(MEMBERS, parts, 8, LANES))
        if step == 0:
            *factors, sources, send = reduce_part(got, scale=scale)
            top, back = return_part(place, far(send), sources, factors)
        else:
            sources, send, ports = reduce_part(got, factors, top)
            (back,) = return_part(place, far(send), sources, factors, ports, top)
        operands = place, inner, explicit, near(back).reshape(MEMBERS * COLUMNS * 8, LANES)
        if step + 1 < STEPS:
            present, lowest, highest = finish_part(*operands)
        else:
            present = output_part(*operands)
    return present.reshape(fields.shape)


def solution(mesh):
    in_specs = (P(None, "gz", "gy", None), P(None, "gz", "gy", None), P("gz", "gy", None), P(), P())
    out_specs = P(None, "gz", "gy", None)
    return jax.shard_map(
        on_device, mesh=mesh, in_specs=in_specs, out_specs=out_specs, check_vma=False
    )
```

```python
import functools

import jax
import jax.numpy as jnp
from jax import lax
from jax.experimental import pallas as pl
from jax.experimental.pallas import tpu as pltpu
from jax.sharding import PartitionSpec as P

STEPS = 2
FIELDS = 4
LEVELS = 4
ITEMS = FIELDS * LEVELS
ROWS = 16
WIDTH = 512
GROUPS = 4
MEMBERS = 16
PAIRS = MEMBERS // 2
FACTORS = 7
LANES = 128
COLUMNS = WIDTH // LANES
TILE = (COLUMNS, 8, LANES)


def columns():
    return [slice(column * LANES, column * LANES + LANES) for column in range(COLUMNS)]


def inner_pivots(rates):
    hold = 1.0 + rates[0]
    inverse = []
    for level in range(LEVELS - 1):
        once = 1.0 / (hold + rates[level + 1])
        inverse.append(once)
        hold = 1.0 + rates[level + 1] * hold * once
    return inverse


def inner_factors(rates):
    inverse = inner_pivots(rates)
    return [*inverse, rates[1] * inverse[0], rates[2] * inverse[1], rates[0], rates[3]]


def solve_inner(source, factors):
    second = source[1] + factors[3] * source[0]
    third = (source[2] + factors[4] * second) * factors[2]
    second = second * factors[1] + factors[4] * third
    return source[0] * factors[0] + factors[3] * second, second, third


def pack_kernel(present_ref, vel_ref, low_ref, high_ref):
    low_ref[0:ITEMS] = present_ref[:, 0:2, :]
    high_ref[0:ITEMS] = present_ref[:, ROWS - 2 : ROWS, :]
    for item in range(2 * LEVELS):
        low_ref[ITEMS + item // 2, item % 2 : item % 2 + 1, :] = vel_ref[item, 0:1, :]
        high_ref[ITEMS + item // 2, item % 2 : item % 2 + 1, :] = vel_ref[item, ROWS - 1 : ROWS, :]


def factor_kernel(scale_ref, face_ref, factor_ref):
    for tile in range(ROWS // 8):
        rows = slice(tile * 8, tile * 8 + 8)
        for lanes in columns():
            faces = [face_ref[level, rows, lanes] for level in range(LEVELS)]
            for field in range(FIELDS):
                scale = jnp.broadcast_to(scale_ref[field : field + 1, :], (8, LANES))
                for item, value in enumerate(inner_factors([scale * face for face in faces])):
                    factor_ref[item, field, rows, lanes] = value


def turned_tile(place_ref, tile):
    return jnp.where(place_ref[0] >= GROUPS // 2, 1 - tile, tile)


def places(tile, parts, line):
    for column in range(COLUMNS):
        start = column * 8 + line if line < 8 else face_line(column, line - 8)
        yield pl.ds(tile * (64 * parts) + start, 8, stride=8 * parts)


def face_line(column, level):
    return (COLUMNS + column // 2) * 8 + column % 2 * LEVELS + level


def along_x(middle, last, begin):
    ahead = [pltpu.roll(value, LANES - 1, 1) for value in middle]
    behind = [pltpu.roll(value, 1, 1) for value in middle]
    for column in range(COLUMNS):
        eastern = jnp.where(last, ahead[(column + 1) % COLUMNS], ahead[column])
        western = jnp.where(begin, behind[column - 1], behind[column])
        yield eastern, western


def tendency(middle, eastern, western, north, south, half_x, half_y, spread):
    return spread * (eastern + western + north + south - 4.0 * middle) - (
        half_x * (eastern - western) + half_y * (north - south)
    )


def edge_lanes():
    lane = lax.broadcasted_iota(jnp.int32, (8, LANES), 1)
    return lane == LANES - 1, lane == 0


def spread_of(scale_ref, field):
    return jnp.broadcast_to(scale_ref[FIELDS + field : FIELDS + field + 1, :], (8, LANES))


ORDER = [field * LEVELS + level for level in range(LEVELS) for field in range(FIELDS)]


def interior_kernel(scale_ref, present_ref, vel_ref, explicit_ref, wide_ref, sectioned_ref):
    last, begin = edge_lanes()

    def section(item, tile):
        field, level = divmod(item, LEVELS)
        rows, at = slice(tile * 8, tile * 8 + 8), tile * 8 + 8
        middle = [present_ref[item, rows, lanes] for lanes in columns()]
        for column, (eastern, western) in enumerate(along_x(middle, last, begin)):
            lanes = slice(column * LANES, column * LANES + LANES)
            sectioned_ref[item, column, at : at + 8, :] = middle[column] + tendency(
                middle[column],
                eastern,
                western,
                wide_ref[item, column, at + 1 : at + 9, :],
                wide_ref[item, column, at - 1 : at + 7, :],
                0.5 * vel_ref[level, rows, lanes],
                0.5 * vel_ref[LEVELS + level, rows, lanes],
                spread_of(scale_ref, field),
            )

    def average(item, tile):
        field, level = divmod(item, LEVELS)
        rows, at = slice(tile * 8, tile * 8 + 8), tile * 8 + 8
        middle = [sectioned_ref[item, column, at : at + 8, :] for column in range(COLUMNS)]
        for column, (eastern, western) in enumerate(along_x(middle, last, begin)):
            lanes = slice(column * LANES, column * LANES + LANES)
            change = tendency(
                middle[column],
                eastern,
                western,
                sectioned_ref[item, column, at + 1 : at + 9, :],
                sectioned_ref[item, column, at - 1 : at + 7, :],
                0.5 * vel_ref[level, rows, lanes],
                0.5 * vel_ref[LEVELS + level, rows, lanes],
                spread_of(scale_ref, field),
            )
            explicit_ref[item, rows, lanes] = 0.5 * (present_ref[item, rows, lanes] + (middle[column] + change))

    for item in range(ITEMS):
        for column, lanes in enumerate(columns()):
            wide_ref[item, column, 8:24, :] = present_ref[item, :, lanes]
    for turn in range(ITEMS + 1):
        for tile in range(ROWS // 8):
            if turn < ITEMS:
                section(ORDER[turn], tile)
            if turn > 0:
                average(ORDER[turn - 1], tile)


def strip_tiles(strip_ref, item, column, low):
    lines = [strip_ref[item, column, at : at + 8, :] for at in range(5)]
    return [jnp.where(low, lines[at], lines[at + 2]) for at in range(3)]


def explicit_kernel(parts, place_ref, scale_ref, factor_ref, inner_ref, present_ref, south_ref, north_ref, vel_ref,
                    vel_south_ref, vel_north_ref, face_ref, explicit_ref, send_ref, strip_ref, vel_strip_ref,
                    vel_tile_ref, sectioned_ref):
    last, begin = edge_lanes()
    low = lax.broadcasted_iota(jnp.int32, (8, LANES), 0) < 4
    for column, lanes in enumerate(columns()):
        for item in range(2 * LEVELS):
            row = slice(item % 2, item % 2 + 1)
            vel_strip_ref[item, column, 1:2, :] = 0.5 * vel_south_ref[ITEMS + item // 2, row, lanes]
            vel_strip_ref[item, column, 2:6, :] = 0.5 * vel_ref[item, 0:4, lanes]
            vel_strip_ref[item, column, 6:10, :] = 0.5 * vel_ref[item, ROWS - 4 : ROWS, lanes]
            vel_strip_ref[item, column, 10:11, :] = 0.5 * vel_north_ref[ITEMS + item // 2, row, lanes]
            _, near, far = strip_tiles(vel_strip_ref, item, column, low)
            vel_tile_ref[0, item, column] = near
            vel_tile_ref[1, item, column] = far
        for item in range(ITEMS):
            strip_ref[item, column, 0:2, :] = south_ref[item, :, lanes]
            strip_ref[item, column, 2:6, :] = present_ref[item, 0:4, lanes]
            strip_ref[item, column, 6:10, :] = present_ref[item, ROWS - 4 : ROWS, lanes]
            strip_ref[item, column, 10:12, :] = north_ref[item, :, lanes]

    def section(item):
        field, level = divmod(item, LEVELS)
        tiles = [strip_tiles(strip_ref, item, column, low) for column in range(COLUMNS)]
        middle = [tile[1] for tile in tiles]
        for column, (eastern, western) in enumerate(along_x(middle, last, begin)):
            sectioned_ref[item, column, 0:8, :] = middle[column] + tendency(
                middle[column],
                eastern,
                western,
                tiles[column][2],
                tiles[column][0],
                vel_tile_ref[0, level, column],
                vel_tile_ref[0, LEVELS + level, column],
                spread_of(scale_ref, field),
            )

    def average(item):
        field, level = divmod(item, LEVELS)
        explicit_ref[item] = inner_ref[item]
        middle = [sectioned_ref[item, column, 1:9, :] for column in range(COLUMNS)]
        for column, (eastern, western) in enumerate(along_x(middle, last, begin)):
            lanes = slice(column * LANES, column * LANES + LANES)
            change = tendency(
                middle[column],
                eastern,
                western,
                sectioned_ref[item, column, 2:10, :],
                sectioned_ref[item, column, 0:8, :],
                vel_tile_ref[1, level, column],
                vel_tile_ref[1, LEVELS + level, column],
                spread_of(scale_ref, field),
            )
            here = jnp.where(low, strip_ref[item, column, 2:10, :], strip_ref[item, column, 4:12, :])
            value = 0.5 * (here + (middle[column] + change))
            explicit_ref[item, 0:2, lanes] = value[0:2]
            explicit_ref[item, ROWS - 2 : ROWS, lanes] = value[4:6]

    for turn in range(ITEMS + 1):
        if turn < ITEMS:
            section(ORDER[turn])
        if turn > 0:
            average(ORDER[turn - 1])
    for tile in range(ROWS // 8):
        rows = slice(tile * 8, tile * 8 + 8)
        target = turned_tile(place_ref, tile)
        for field in range(FIELDS):
            lines = zip(columns(), places(target, parts, field), places(target, parts, FIELDS + field), strict=True)
            for lanes, own, under in lines:
                factors = [factor_ref[item, field, rows, lanes] for item in range(FACTORS)]
                source = [explicit_ref[field * LEVELS + level, rows, lanes] for level in range(LEVELS)]
                first, _, third = solve_inner(source, factors)
                send_ref[own, :] = source[3] + factors[6] * third
                send_ref[under, :] = factors[5] * first
        if parts > COLUMNS:
            for level in range(LEVELS):
                for lanes, line in zip(columns(), places(target, parts, 8 + level), strict=True):
                    send_ref[line, :] = face_ref[level, rows, lanes]


def swap(value):
    return pltpu.roll(value, 4, 1)


def lower_half():
    return lax.broadcasted_iota(jnp.int32, TILE, 1) < 4


def pair_sources(got_ref, low):
    def side(block):
        return got_ref[block, 0:COLUMNS] + swap(got_ref[block + 1, 0:COLUMNS])

    return [jnp.where(low, side(step), swap(side(MEMBERS - 2 - step))) for step in range(PAIRS)]


def outer_source(got_ref, low):
    return jnp.where(low, swap(got_ref[0, 0:COLUMNS]), swap(got_ref[MEMBERS - 1, 0:COLUMNS]))


def eliminate(sources, gain_ref, center):
    value = sources[0]
    kept = [value]
    for step in range(1, PAIRS - 1):
        value = sources[step] + gain_ref[step - 1] * value
        kept.append(value)
    value = gain_ref[PAIRS - 2] * value
    return kept, (sources[PAIRS - 1] + value + swap(value)) * center


def face_rows(got_ref, block, level):
    rows = []
    for column in range(COLUMNS):
        tile, line = divmod(face_line(column, level), 8)
        rows.append(jnp.broadcast_to(got_ref[block, tile, line : line + 1, :], (8, LANES)))
    return jnp.stack(rows)


def reduce_kernel(first, got_ref, *refs):
    low = lower_half()
    if first:
        scale_ref, weight_ref, gain_ref, edge_ref, source_ref, send_ref = refs
        scale = jnp.concatenate([scale_ref[0:FIELDS, :]] * 2, 0)[None]
        couple, own, under = [], [], []
        for step in range(PAIRS):
            rates = [
                scale
                * jnp.where(
                    low,
                    face_rows(got_ref, step, level),
                    face_rows(got_ref, MEMBERS - 1 - step, level),
                )
                for level in range(LEVELS)
            ]
            part = inner_factors(rates)
            one = jnp.ones(TILE, jnp.float32)
            bottom, _, third = solve_inner([one, one, one], part)
            own.append(1.0 + rates[3] * third)
            under.append(rates[0] * bottom)
            couple.append(rates[0] * part[3] * part[4] * part[2] * rates[3])
        masses = [
            jnp.where(low, own[step] + under[step + 1], own[step + 1] + under[step]) for step in range(PAIRS - 1)
        ]
        last_own, last_under = own[PAIRS - 1], under[PAIRS - 1]
        masses.append(jnp.where(low, last_own + swap(last_under), swap(last_own) + last_under))
        hold = masses[0] + couple[0]
        through = couple[0]
        for step in range(PAIRS - 1):
            inward = couple[step + 1]
            weight = 1.0 / (hold + inward)
            gain = inward * weight
            weight_ref[step] = weight
            gain_ref[step] = gain
            through = through * gain
            hold = hold * gain + (masses[step + 1] if step + 2 < PAIRS else 0.0)
        center = 1.0 / (masses[PAIRS - 1] + hold + swap(hold))
        weight_ref[PAIRS - 1] = center
        edge_ref[...] = couple[0]
        kept, value = eliminate(masses, gain_ref, center)
        for step in reversed(range(PAIRS - 1)):
            value = weight_ref[step] * kept[step] + gain_ref[step] * value
        outer = jnp.where(low, under[0], own[0]) + couple[0] * value
        through = through * swap(through) * center
        for group in range(GROUPS):
            send_ref[group, COLUMNS : 2 * COLUMNS] = outer
            for item, pair in enumerate(pack_pairs(through, low)):
                send_ref[group, 2 * COLUMNS + item] = pair
    else:
        weight_ref, gain_ref, edge_ref, top_ref, source_ref, send_ref, port_ref = refs
    sources = pair_sources(got_ref, low)
    for step in range(PAIRS):
        source_ref[step] = sources[step]
    kept, value = eliminate(sources, gain_ref, weight_ref[PAIRS - 1])
    for step in reversed(range(PAIRS - 1)):
        value = weight_ref[step] * kept[step] + gain_ref[step] * value
    outer = outer_source(got_ref, low) + edge_ref[...] * value
    if first:
        for group in range(GROUPS):
            send_ref[group, 0:COLUMNS] = outer
    else:
        port_ref[...] = outer
        for group in range(GROUPS):
            part = outer * top_ref[group]
            for item, pair in enumerate(pack_pairs(part + swap(part), low)):
                send_ref[group, item] = pair


def pack_pairs(value, low):
    return [jnp.where(low[0], value[column], value[column + 1]) for column in range(0, COLUMNS, 2)]


def unpack_pairs(pairs, low):
    turned = swap(pairs)
    tiles = [jnp.where(low[0], one, other) for pair in zip(pairs, turned) for one, other in (pair, pair[::-1])]
    return jnp.stack(tiles)


def port_weights(parts, through, place, low):
    masses = []
    for group in range(GROUPS):
        mass = jnp.where(low, swap(parts[group]), parts[group])
        if group + 1 < GROUPS:
            mass = mass + jnp.where(low, parts[group + 1], swap(parts[group + 1]))
        masses.append(mass)
    under, gain = [masses[0] + through[0]], []
    for group in range(GROUPS - 1):
        gain.append(through[group + 1] / (under[group] + through[group + 1]))
        under.append(masses[group + 1] + under[group] * gain[group])
    over, rise = [masses[GROUPS - 1]], []
    for group in reversed(range(1, GROUPS)):
        rise.insert(0, through[group] / (over[0] + through[group]))
        over.insert(0, masses[group - 1] + over[0] * rise[0])
    rise.insert(0, None)
    one, zero = jnp.ones(TILE, jnp.float32), jnp.zeros(TILE, jnp.float32)
    weights = [zero] * GROUPS
    own = cross = zero
    for mine in range(GROUPS):
        here = place == mine
        for group in range(GROUPS):
            product = one
            for between in range(mine, group - 1):
                product = product * gain[between]
            for between in range(group + 1, mine):
                product = product * rise[between]
            if group > mine:
                tile = jnp.where(low, product * gain[mine - 1] if mine else zero, product)
            elif group < mine:
                tile = jnp.where(low, product, product * rise[mine])
            else:
                continue
            weights[group] = jnp.where(here, tile, weights[group])
        if mine:
            low_hold, high_hold, link = under[mine - 1], over[mine], through[mine]
            inverse = 1.0 / (low_hold * high_hold + link * (low_hold + high_hold))
            own = jnp.where(here, (jnp.where(low, high_hold, low_hold) + link) * inverse, own)
            cross = jnp.where(here, link * inverse, cross)
        else:
            own = jnp.where(here, jnp.where(low, zero, 1.0 / (over[0] + through[0])), own)
    return *weights, own, cross


def across(parts, low):
    ends = jnp.where(low, swap(parts[0]) + parts[1], parts[3])
    middle = jnp.where(low, swap(parts[1]) + parts[2], parts[2] + swap(parts[3]))
    return ends, middle


def return_kernel(first, place_ref, got_ref, source_ref, weight_ref, gain_ref, edge_ref, *refs):
    low = lower_half()
    place = place_ref[0]
    if first:
        top_ref, back_ref = refs
        parts = [got_ref[group, COLUMNS : 2 * COLUMNS] for group in range(GROUPS)]
        through = [
            unpack_pairs(got_ref[group, 2 * COLUMNS : 2 * COLUMNS + COLUMNS // 2], low) for group in range(GROUPS)
        ]
        for item, value in enumerate(port_weights(parts, through, place, low)):
            top_ref[item] = value
        ends, middle = across(parts, low)
        hold = ends + jnp.where(low, through[0], 0.0)
        inward = jnp.where(low, through[1], through[3])
        weight = 1.0 / (hold + inward)
        gain = inward * weight
        hold = middle + hold * gain
        other = swap(hold)
        inverse = 1.0 / (hold * other + through[2] * (hold + other))
        mine, cross = (other + through[2]) * inverse, through[2] * inverse
        ends, middle = across([got_ref[group, 0:COLUMNS] for group in range(GROUPS)], low)
        inner = middle + gain * ends
        inner = mine * inner + cross * swap(inner)
        ends = weight * ends + gain * inner
        turned = swap(ends)
        value = jnp.where(
            place == 0,
            jnp.where(low, 0.0, turned),
            jnp.where(
                place == 1,
                jnp.where(low, ends, swap(inner)),
                jnp.where(place == 2, inner, jnp.where(low, swap(inner), ends)),
            ),
        )
    else:
        port_ref, top_ref, back_ref = refs
        ports = port_ref[...]
        for group in range(GROUPS):
            below = jnp.where(place > group, 1.0, 0.0)
            above = jnp.where(place < group, 1.0, 0.0)
            ports = ports + jnp.where(low, below, above) * unpack_pairs(got_ref[group], low)
        value = top_ref[GROUPS] * ports + top_ref[GROUPS + 1] * swap(ports)
    sources = [source_ref[step] for step in range(PAIRS)]
    sources[0] = sources[0] + edge_ref[...] * value
    kept, center = eliminate(sources, gain_ref, weight_ref[PAIRS - 1])
    solved = [center]
    for step in reversed(range(PAIRS - 1)):
        solved.insert(0, weight_ref[step] * kept[step] + gain_ref[step] * solved[0])
    outer = value
    for step in range(PAIRS):
        turned = swap(solved[step])
        back_ref[step] = jnp.where(low, outer, turned)
        back_ref[MEMBERS - 1 - step] = jnp.where(low, turned, outer)
        outer = solved[step]


def finish_field(field, place_ref, factor_ref, explicit_ref, back_ref, present_ref, edge_refs=None):
    for tile in range(ROWS // 8):
        rows = slice(tile * 8, tile * 8 + 8)
        target = turned_tile(place_ref, tile)
        lines = zip(columns(), places(target, COLUMNS, field), places(target, COLUMNS, FIELDS + field), strict=True)
        for lanes, below, top in lines:
            factors = [factor_ref[item, field, rows, lanes] for item in range(FACTORS)]
            source = [explicit_ref[field * LEVELS + level, rows, lanes] for level in range(LEVELS - 1)]
            top = back_ref[top, :]
            source[0] = source[0] + factors[5] * back_ref[below, :]
            source[2] = source[2] + factors[6] * top
            solved = solve_inner(source, factors) + (top,)
            for level in range(LEVELS):
                item = field * LEVELS + level
                present_ref[item, rows, lanes] = solved[level]
                if edge_refs and tile == 0:
                    edge_refs[0][item, :, lanes] = solved[level][0:2]
                if edge_refs and tile == 1:
                    edge_refs[1][item, :, lanes] = solved[level][6:8]


def finish_kernel(place_ref, factor_ref, explicit_ref, back_ref, present_ref, *edge_refs):
    for field in range(FIELDS):
        finish_field(field, place_ref, factor_ref, explicit_ref, back_ref, present_ref, edge_refs)


def output_kernel(place_ref, factor_ref, explicit_ref, back_ref, out_ref, present_ref, sems):
    copies = []
    for field in range(FIELDS):
        finish_field(field, place_ref, factor_ref, explicit_ref, back_ref, present_ref)
        items = pl.ds(field * LEVELS, LEVELS)
        copies.append(pltpu.make_async_copy(present_ref.at[items], out_ref.at[items], sems.at[field]))
        copies[-1].start()
    for copy in copies:
        copy.wait()


VMEM = pl.BlockSpec(memory_space=pltpu.VMEM)
SMEM = pl.BlockSpec(memory_space=pltpu.SMEM)
PARAMS = pltpu.CompilerParams(vmem_limit_bytes=8 << 20)


def struct(*shape):
    return jax.ShapeDtypeStruct(shape, jnp.float32)


def pack_part(present, vel):
    edge = struct(ITEMS + LEVELS, 2, WIDTH)
    return pl.pallas_call(
        pack_kernel,
        out_shape=(edge, edge),
        in_specs=[VMEM, VMEM],
        out_specs=(VMEM,) * 2,
        compiler_params=PARAMS,
        name="pack_part",
    )(present, vel)


def factor_part(scale, faces):
    return pl.pallas_call(
        factor_kernel,
        out_shape=struct(FACTORS, FIELDS, ROWS, WIDTH),
        in_specs=[VMEM, VMEM],
        out_specs=VMEM,
        compiler_params=PARAMS,
        name="factor_part",
    )(scale, faces)


def interior_part(scale, present, vel):
    return pl.pallas_call(
        interior_kernel,
        out_shape=struct(ITEMS, ROWS, WIDTH),
        in_specs=[VMEM] * 3,
        out_specs=VMEM,
        scratch_shapes=[pltpu.VMEM((ITEMS, COLUMNS, 32, LANES), jnp.float32)] * 2,
        compiler_params=PARAMS,
        cost_estimate=pl.CostEstimate(flops=8 << 20, bytes_accessed=3 << 20, transcendentals=0),
        name="interior_part",
    )(scale, present, vel)


def explicit_part(parts, *operands):
    return pl.pallas_call(
        functools.partial(explicit_kernel, parts),
        out_shape=(struct(ITEMS, ROWS, WIDTH), struct(MEMBERS * parts * 8, LANES)),
        in_specs=[SMEM] + [VMEM] * 10,
        out_specs=(VMEM, VMEM),
        scratch_shapes=[
            pltpu.VMEM((ITEMS, COLUMNS, 16, LANES), jnp.float32),
            pltpu.VMEM((2 * LEVELS, COLUMNS, 16, LANES), jnp.float32),
            pltpu.VMEM((2, 2 * LEVELS, COLUMNS, 8, LANES), jnp.float32),
            pltpu.VMEM((ITEMS, COLUMNS, 16, LANES), jnp.float32),
        ],
        compiler_params=PARAMS,
        name="explicit_part",
    )(*operands)


def reduce_part(got, factors=None, top=None, scale=None):
    first = not factors
    tiles = 2 * COLUMNS + COLUMNS // 2 if first else COLUMNS // 2
    outs = (struct(PAIRS, *TILE), struct(GROUPS, tiles, 8, LANES))
    if first:
        outs = (struct(PAIRS, *TILE), struct(PAIRS - 1, *TILE), struct(*TILE)) + outs
    else:
        outs += (struct(*TILE),)
    operands = (got, scale) if first else (got, *factors, top)
    return pl.pallas_call(
        functools.partial(reduce_kernel, first),
        out_shape=outs,
        in_specs=[VMEM] * len(operands),
        out_specs=(VMEM,) * len(outs),
        compiler_params=PARAMS,
        name="reduce_part",
    )(*operands)


def return_part(place, got, sources, factors, *more):
    first = not more
    outs = (struct(MEMBERS, *TILE),)
    if first:
        outs = (struct(GROUPS + 2, *TILE),) + outs
    operands = (got, sources, *factors, *more)
    return pl.pallas_call(
        functools.partial(return_kernel, first),
        out_shape=outs,
        in_specs=[SMEM] + [VMEM] * len(operands),
        out_specs=(VMEM,) * len(outs),
        compiler_params=PARAMS,
        name="return_part",
    )(place, *operands)


def finish_part(*operands):
    edge = struct(ITEMS, 2, WIDTH)
    return pl.pallas_call(
        finish_kernel,
        out_shape=(struct(ITEMS, ROWS, WIDTH), edge, edge),
        in_specs=[SMEM] + [VMEM] * 3,
        out_specs=(VMEM,) * 3,
        compiler_params=PARAMS,
        name="finish_part",
    )(*operands)


def output_part(*operands):
    return pl.pallas_call(
        output_kernel,
        out_shape=struct(ITEMS, ROWS, WIDTH),
        in_specs=[SMEM] + [VMEM] * 3,
        out_specs=pl.BlockSpec(memory_space=pl.ANY),
        scratch_shapes=[
            pltpu.VMEM((ITEMS, ROWS, WIDTH), jnp.float32),
            pltpu.SemaphoreType.DMA((FIELDS,)),
        ],
        compiler_params=PARAMS,
        name="output_part",
    )(*operands)


def on_device(fields, velocity, face_rate, xy_rate, z_scale):
    count = lax.axis_size("gy")
    up = [(i, (i + 1) % count) for i in range(count)]
    down = [(target, source) for source, target in up]
    scale = jnp.broadcast_to(jnp.concatenate([z_scale, xy_rate])[:, None], (2 * FIELDS, LANES))
    place = lax.shift_right_logical(lax.axis_index("gz"), MEMBERS.bit_length() - 1).astype(jnp.int32).reshape(1)
    scale, place = lax.optimization_barrier((scale, place))

    present = fields.reshape(ITEMS, ROWS, WIDTH)
    vel = velocity.reshape(2 * LEVELS, ROWS, WIDTH)
    faces = face_rate
    lowest, highest = pack_part(present, vel)
    half_vel = vel
    south = vel_south = lax.ppermute(highest, "gy", up)
    north = vel_north = lax.ppermute(lowest, "gy", down)
    inner = factor_part(scale, faces)

    near_groups = [[group * MEMBERS + member for member in range(MEMBERS)] for group in range(GROUPS)]
    far_groups = [
        [group * MEMBERS + (row + group // 2 * 8) % MEMBERS for group in range(GROUPS)] for row in range(MEMBERS)
    ]

    def near(chunks):
        return lax.all_to_all(chunks, "gz", 0, 0, tiled=True, axis_index_groups=near_groups)

    def far(chunks):
        return lax.all_to_all(chunks, "gz", 0, 0, tiled=True, axis_index_groups=far_groups)

    factors = top = None
    for step in range(STEPS):
        if step > 0:
            south = lax.ppermute(highest, "gy", up)
            north = lax.ppermute(lowest, "gy", down)
        parts = COLUMNS if factors else COLUMNS + 2
        interior = interior_part(scale, present, half_vel)
        explicit, send = explicit_part(
            parts, place, scale, inner, interior, present, south, north, half_vel, vel_south, vel_north, faces
        )
        got = near(send.reshape(MEMBERS, parts, 8, LANES))
        if step == 0:
            *factors, sources, send = reduce_part(got, scale=scale)
            top, back = return_part(place, far(send), sources, factors)
        else:
            sources, send, ports = reduce_part(got, factors, top)
            (back,) = return_part(place, far(send), sources, factors, ports, top)
        operands = place, inner, explicit, near(back).reshape(MEMBERS * COLUMNS * 8, LANES)
        if step + 1 < STEPS:
            present, lowest, highest = finish_part(*operands)
        else:
            present = output_part(*operands)
    return present.reshape(fields.shape)


def solution(mesh):
    in_specs = (P(None, "gz", "gy", None), P(None, "gz", "gy", None), P("gz", "gy", None), P(), P())
    out_specs = P(None, "gz", "gy", None)
    return jax.shard_map(
        on_device, mesh=mesh, in_specs=in_specs, out_specs=out_specs, check_vma=False
    )
```
